32 devices in a mesh: days: 2 (over x), sta: 16 (over z, y, core).
Axes of the slice: x: 2, y: 2, z: 4, core: 2. Of those that a mesh axis runs over, the one named last changes fastest.
Arguments:
- records: bfloat16 [384, 256, 256], P(('days', 'sta')), parts along dimension 0, may hold values from -330 to 330
- counts: int32 [128, 4], P(('days', 'sta')), parts along dimension 0, may hold values from 0 to 64
- gap_mask: int32 [128, 256], P(('days', 'sta')), parts along dimension 0, may hold values 0 or 1
Outputs:
- cross_spectra: bfloat16 [7, 2, 384, 12, 128], P(None, None, ('days', 'sta')), parts along dimension 2
The draws below stay inside these ranges and needn't reach their ends.
There are 2 independent parts, one for each index of `days`. The reference program is written for one: setup_inputs(seed, part) draws one part's arguments, and reference() takes and returns one part's arrays. A program takes and returns all parts, laid end to end along the dimension named above; each array names one. Nothing has to cross between parts.
All inputs are finite; a program needn't handle non-finite values. No bound on the sum of `gap_mask` on one device may be relied on, other than what follows from the above.
Results may differ from the reference program's by a relative error of at most 0.0062.
Values may be sent and summed in bfloat16 or wider, within the bound.
No kernel may reach another device: no remote copies, remote signals or barrier semaphores. Data moves between devices by JAX's collectives and lax.ppermute only.
A program may use at most 64 MiB of HBM per device.

```python
import math
import jax
import jax.numpy as jnp
from jax import lax

F = 128
SEG_LEN = 256
ST_DEV = 4
CH_DEV = 12
STATIONS = 64
CHANS = 192
HOURS = 4
SEG_H = 64
SEGS = 256
ROUNDS = 3
N_STA = 16


def draw_records(key, part):
    key_noise, key_tilt, key_scale = jax.random.split(key, 3)
    noise = jnp.clip(jax.random.normal(key_noise, (CHANS, SEGS, SEG_LEN), jnp.float32), -6.0, 6.0)
    tilt = jax.random.uniform(key_tilt, (CHANS, 1, 1), jnp.float32, -0.9, 0.9)
    earlier = jnp.concatenate([noise[:, :, -1:], noise[:, :, :-1]], axis=2)
    colored = noise + tilt * earlier
    station_scale = jnp.exp(jax.random.uniform(key_scale, (STATIONS, SEGS, 1), jnp.float32, 0.0, math.log(10.0)))
    station_scale = jnp.repeat(station_scale, 3, axis=0)
    return (colored * station_scale).astype(jnp.bfloat16)


def plant(drawn, rng, smallest, largest):
    extent = drawn.shape
    spot = [jax.random.randint(jax.random.fold_in(rng, axis), (), 0, extent[axis]) for axis in range(len(extent))]
    drawn = drawn.at[tuple(spot)].set(smallest)
    longest = extent.index(max(extent))
    spot[longest] = (spot[longest] + 1) % extent[longest]
    return drawn.at[tuple(spot)].set(largest)


def setup_inputs(seed: int = 0, part: int = 0) -> dict:
    key_of = jax.random.split(jax.random.key(seed), 4)
    part_splits = jax.random.split(jax.random.fold_in(key_of[3], part), 4)
    return {
        "records": draw_records(jax.random.fold_in(jax.random.fold_in(key_of[3], part), 71), part),
        "counts": plant(jax.random.randint(part_splits[1], (STATIONS, HOURS), 0, SEG_H + 1), jax.random.fold_in(part_splits[1], 1), 0, SEG_H).astype(jnp.int32),
        "gap_mask": plant((jax.random.randint(part_splits[2], (STATIONS, SEGS), 0, 8) < 7).astype(jnp.int32), jax.random.fold_in(part_splits[2], 1), 0, 1),
    }


epsilon = 1e-06

def fourier_matrix(samples):
    freq_bins = samples // 2
    times_axis = jnp.arange(samples, dtype=jnp.int32)
    bins_axis = jnp.arange(freq_bins, dtype=jnp.int32)
    phase_idx = times_axis[:, None] * bins_axis[None, :] % samples
    angle = 2.0 * math.pi / samples * phase_idx.astype(jnp.float32)
    taper = 0.5 - 0.5 * jnp.cos(2.0 * math.pi / samples * (times_axis.astype(jnp.float32) + 0.5))
    table_full = jnp.concatenate([taper[:, None] * jnp.cos(angle), -taper[:, None] * jnp.sin(angle)], axis=1)
    return table_full.astype(jnp.bfloat16)

def whiten(records, counts, gap_mask, fourier):
    channels, segments, samples = records.shape
    stations, hour_count = counts.shape
    seg_hour = segments // hour_count
    spectrum = jnp.dot(records.reshape(channels * segments, samples), fourier, preferred_element_type=jnp.float32).reshape(channels, segments, samples)
    band_power = lax.optimization_barrier(jnp.mean(spectrum * spectrum, axis=2, keepdims=True))
    position = jnp.arange(seg_hour, dtype=jnp.int32)
    station_valid = (position[None, None, :] < counts[:, :, None]).astype(jnp.float32)
    station_valid = station_valid * gap_mask.reshape(stations, hour_count, seg_hour).astype(jnp.float32)
    validity = jnp.repeat(station_valid.reshape(stations, segments), 3, axis=0)
    whitened = (spectrum * lax.rsqrt(band_power + epsilon) * validity[:, :, None]).astype(jnp.bfloat16)
    return (whitened.reshape(channels, hour_count, seg_hour, 2, samples // 2), validity.astype(jnp.bfloat16).reshape(channels, hour_count, seg_hour))

def pair_spectra(own_block, partner, own_valid, partner_valid):
    hour_count = own_block.shape[1]
    first = own_block.astype(jnp.float32)
    second = partner.astype(jnp.float32)
    real_part = jnp.einsum('ahspk,bhspk->hkab', first, second)
    imag_part = jnp.einsum('ahsk,bhsk->hkab', first[:, :, :, 1], second[:, :, :, 0]) - jnp.einsum('ahsk,bhsk->hkab', first[:, :, :, 0], second[:, :, :, 1])
    joint = jnp.einsum('ahs,bhs->hab', own_valid.astype(jnp.float32), partner_valid.astype(jnp.float32))
    weighting = 1.0 / (hour_count * jnp.maximum(joint, 1.0))
    real_sum = lax.optimization_barrier(jnp.sum(real_part * weighting[:, None], axis=0))
    imag_sum = lax.optimization_barrier(jnp.sum(imag_part * weighting[:, None], axis=0))
    return jnp.stack([jnp.transpose(real_sum, (1, 2, 0)), jnp.transpose(imag_sum, (1, 2, 0))]).astype(jnp.bfloat16)

def reference(records, counts, gap_mask):
    fourier = fourier_matrix(SEG_LEN)
    blocks_raw = records.reshape(N_STA, CH_DEV, SEGS, SEG_LEN)
    counts_blocks = counts.reshape(N_STA, ST_DEV, HOURS)
    gaps_blocks = gap_mask.reshape(N_STA, ST_DEV, SEGS)

    def prepare(pieces):
        return whiten(pieces[0], pieces[1], pieces[2], fourier)
    whitened, validity = lax.map(prepare, (blocks_raw, counts_blocks, gaps_blocks))

    def one_block(block_index):
        own_block = whitened[block_index]
        own_valid = validity[block_index]
        results = []
        for slot_index in range(2 * ROUNDS + 1):
            partner_idx = (block_index + slot_index - ROUNDS) % N_STA
            results.append(pair_spectra(own_block, whitened[partner_idx], own_valid, validity[partner_idx]))
        return jnp.stack(results)
    stacked = lax.map(one_block, jnp.arange(N_STA, dtype=jnp.int32))
    return jnp.transpose(stacked, (1, 2, 0, 3, 4, 5)).reshape(2 * ROUNDS + 1, 2, N_STA * CH_DEV, CH_DEV, F)
```

```python
import math

import jax
import jax.numpy as jnp
from jax import lax
from jax.experimental import pallas as pl
from jax.experimental.pallas import tpu as pltpu
from jax.sharding import PartitionSpec as P

ROUNDS = 3
COMPONENTS = 3
LANES = 128
PITCH = 16

epsilon = 1e-06

NT = (((1,), (1,)), ((), ()))


def fourier_matrix(samples):
    freq_bins = samples // 2
    times_axis = jnp.arange(samples, dtype=jnp.int32)
    bins_axis = jnp.arange(freq_bins, dtype=jnp.int32)
    phase_idx = times_axis[:, None] * bins_axis[None, :] % samples
    angle = 2.0 * math.pi / samples * phase_idx.astype(jnp.float32)
    taper = 0.5 - 0.5 * jnp.cos(2.0 * math.pi / samples * (times_axis.astype(jnp.float32) + 0.5))
    table_re = taper[:, None] * jnp.cos(angle)
    table_im = -taper[:, None] * jnp.sin(angle)
    return jnp.concatenate([table_re.T, table_im.T], axis=1).astype(jnp.bfloat16)


def lane_iota(rows):
    return lax.broadcasted_iota(jnp.int32, (rows, LANES), 1)


def whiten_hour_kernel(hour, counts_ref, records_ref, gap_ref, table_ref, out_ref):
    channels, seg_hour, samples = records_ref.shape
    bins = samples // 2
    stations = gap_ref.shape[0]
    per_tile = LANES // seg_hour
    tile = gap_ref[:, pl.ds(hour // per_tile * LANES, LANES)].astype(jnp.float32)
    turned = pltpu.roll(tile, seg_hour, 1)
    lane = lane_iota(stations)
    low = lane < seg_hour
    doubled = jnp.where(low, tile, turned) if hour % per_tile == 0 else jnp.where(low, turned, tile)
    position = jnp.where(low, lane, lane - seg_hour)
    row = lax.broadcasted_iota(jnp.int32, (bins, LANES), 0)
    side = lane_iota(bins)
    slot = jnp.logical_and(row == 0, side >= seg_hour)
    table = table_ref[...]
    zeros = jnp.zeros((seg_hour, samples), jnp.bfloat16)
    for station in range(stations):
        valid = jnp.where(
            position[station : station + 1] < counts_ref[station, hour],
            doubled[station : station + 1],
            0.0,
        )
        for component in range(channels // stations):
            channel = station * (channels // stations) + component
            record = records_ref[channel]
            upper = jnp.concatenate([record, zeros], axis=0)
            lower = jnp.concatenate([zeros, record], axis=0)
            spectrum = lax.dot_general(
                table[:, :samples], upper, NT, preferred_element_type=jnp.float32
            ) + lax.dot_general(table[:, samples:], lower, NT, preferred_element_type=jnp.float32)
            power = jnp.sum(spectrum * spectrum, axis=0, keepdims=True)
            power = (power + pltpu.roll(power, seg_hour, 1)) * (1.0 / samples)
            scale = lax.rsqrt(power + epsilon) * valid
            out_ref[channel] = jnp.where(slot, valid, spectrum * scale).astype(jnp.bfloat16)


def whiten_hour(records, counts, gap_mask, table, hour):
    channels, segments, samples = records.shape
    seg_hour = segments // counts.shape[1]
    bins = samples // 2
    return pl.pallas_call(
        lambda *refs: whiten_hour_kernel(hour, *refs),
        grid=(1,),
        out_shape=jax.ShapeDtypeStruct((channels, bins, LANES), jnp.bfloat16),
        in_specs=[
            pl.BlockSpec(memory_space=pltpu.SMEM),
            pl.BlockSpec((channels, seg_hour, samples), lambda i: (0, hour, 0)),
            pl.BlockSpec(gap_mask.shape, lambda i: (0, 0)),
            pl.BlockSpec(table.shape, lambda i: (0, 0)),
        ],
        out_specs=pl.BlockSpec((channels, bins, LANES), lambda i: (0, 0, 0)),
        name="whiten_hour",
    )(counts, records, gap_mask, table)


def pair_hour_kernel(hours, first, last, *refs):
    refs = list(refs)
    distance_ref = refs.pop(0) if last else None
    blocks = [refs.pop(0) for _ in range(ROUNDS + 1)]
    before_ref = None if first else refs.pop(0)
    channels, bins, _ = blocks[0].shape
    half = LANES // 2
    if last:
        kept_ref, back_ref, wide_ref, acc_ref, kept_f32, back_f32 = refs
    else:
        acc_ref, wide_ref = refs
    pitch = wide_ref.shape[0] // (len(blocks) * channels + PITCH - channels)
    for q, block in enumerate(blocks):
        for channel in range(channels):
            start = (q * channels + channel) * pitch
            wide_ref[start : start + bins, :] = block[channel].astype(jnp.float32)
    for pad in range(PITCH - channels):
        start = (len(blocks) * channels + pad) * pitch
        wide_ref[start : start + bins, :] = jnp.zeros((bins, LANES), jnp.float32)

    def tile_at(q, k):
        return wide_ref[pl.ds(q * channels * pitch + k, PITCH, stride=pitch), :]

    low = lane_iota(PITCH) < half
    zeroth = [tile_at(q, 0) for q in range(len(blocks))]
    valid = [jnp.where(low, pltpu.roll(t, half, 1), t).astype(jnp.bfloat16) for t in zeroth]
    for q, t in enumerate(zeroth):
        wide_ref[pl.ds(q * channels * pitch, PITCH, stride=pitch), :] = jnp.where(low, t, 0.0)
    joint = 0.5 * lax.dot_general(
        valid[0], jnp.concatenate(valid + valid, axis=0), NT, preferred_element_type=jnp.float32
    )
    weight = 1.0 / (hours * jnp.maximum(joint, 1.0))
    sign = jnp.where(low, -1.0, 1.0)

    def step(k, carry):
        tiles = [tile_at(q, k) for q in range(len(blocks))]
        straight = [t.astype(jnp.bfloat16) for t in tiles]
        turned = [(pltpu.roll(t, half, 1) * sign).astype(jnp.bfloat16) for t in tiles]
        product = weight * lax.dot_general(
            straight[0],
            jnp.concatenate(straight + turned, axis=0),
            NT,
            preferred_element_type=jnp.float32,
        )
        if not first:
            product = product + before_ref[k]
        acc_ref[k] = product
        return carry

    lax.fori_loop(0, bins, step, 0, unroll=8)
    if not last:
        return
    for a in range(channels):
        by_bin = acc_ref[:, a, :].T
        for q in range(len(blocks)):
            for part in range(2):
                start = part * half + q * PITCH
                rows = by_bin[start : start + channels]
                kept_f32[q, pl.ds(a * 2 * channels + part, channels, stride=2), :] = rows
                if q:
                    back_f32[q - 1, pl.ds(2 * a + part, channels, stride=2 * channels), :] = (
                        -rows if part else rows
                    )
    kept_ref[ROUNDS] = kept_f32[0].astype(jnp.bfloat16)
    for q in range(ROUNDS):
        away = distance_ref[q]
        kept_ref[ROUNDS - away] = kept_f32[q + 1].astype(jnp.bfloat16)
        back_ref[away - 1] = back_f32[q].astype(jnp.bfloat16)


def pair_hour(blocks, before, distances, hours, last):
    channels, bins, lanes = blocks[0].shape
    first = before is None
    acc = (bins, PITCH, lanes)
    rows = 2 * channels * channels
    pitch = bins + 8
    wide = pltpu.VMEM(((len(blocks) * channels + PITCH - channels) * pitch, lanes), jnp.float32)
    vmem = pl.BlockSpec(memory_space=pltpu.VMEM)
    args, specs = [], []
    if last:
        args.append(distances)
        specs.append(pl.BlockSpec(memory_space=pltpu.SMEM))
    args += blocks
    specs += [vmem] * len(blocks)
    if not first:
        args.append(before)
        specs.append(vmem)
    if last:
        out_shape = [
            jax.ShapeDtypeStruct((ROUNDS + 1, rows, lanes), jnp.bfloat16),
            jax.ShapeDtypeStruct((ROUNDS, rows, lanes), jnp.bfloat16),
        ]
        out_specs = [vmem, vmem]
        scratch = [
            wide,
            pltpu.VMEM(acc, jnp.float32),
            pltpu.VMEM((ROUNDS + 1, rows, lanes), jnp.float32),
            pltpu.VMEM((ROUNDS, rows, lanes), jnp.float32),
        ]
    else:
        out_shape = jax.ShapeDtypeStruct(acc, jnp.float32)
        out_specs = vmem
        scratch = [wide]
    return pl.pallas_call(
        lambda *refs: pair_hour_kernel(hours, first, last, *refs),
        out_shape=out_shape,
        in_specs=specs,
        out_specs=out_specs,
        scratch_shapes=scratch,
        name="pair_hour_last" if last else "pair_hour",
    )(*args)


def from_behind(value, count, steps):
    pairs = [(source, (source + steps) % count) for source in range(count)]
    return lax.ppermute(value, "sta", pairs)


LEVEL = 4
DISTANCES = ((3, 1, 2), (1, 3, 2), (3, 2, 1), (1, 2, 3))


def moves(count, *hops):
    levels = count // LEVEL
    return [
        (LEVEL * level + source, LEVEL * ((level + up) % levels) + target)
        for source, target, up in hops
        for level in range(levels)
    ]


def fetch_partners(block, count, role):
    if count % LEVEL:
        return [from_behind(block, count, steps) for steps in range(1, ROUNDS + 1)]
    shifted = lax.ppermute(
        block, "sta", moves(count, (0, 1, 0), (2, 3, 0), (1, 0, 1), (3, 2, 1))
    )
    crossed = lax.ppermute(block, "sta", moves(count, (0, 2, 0), (1, 3, 0), (2, 1, 1)))
    relayed = lax.ppermute(shifted, "sta", moves(count, (2, 0, 0)))
    second = jnp.where(role == 0, relayed, crossed)
    third = lax.ppermute(second, "sta", moves(count, (0, 1, 0), (1, 0, 0), (2, 3, 0), (3, 2, 0)))
    return [shifted, second, third]


def per_device(records, counts, gap_mask):
    channels, segments, samples = records.shape
    hours = counts.shape[1]
    bins = samples // 2
    count = lax.axis_size("sta")
    role = lax.axis_index("sta") % LEVEL
    if count % LEVEL:
        distances = jnp.arange(1, ROUNDS + 1, dtype=jnp.int32)
    else:
        distances = jnp.array(DISTANCES, jnp.int32)[role]
    table = fourier_matrix(samples)
    whitened = [whiten_hour(records, counts, gap_mask, table, hour) for hour in range(hours)]
    partners = [fetch_partners(block, count, role) for block in whitened]
    acc = None
    for hour in range(hours):
        acc = pair_hour(
            [whitened[hour], *partners[hour]], acc, distances, hours, hour == hours - 1
        )
    kept, back = acc
    returned = [from_behind(back[d - 1], count, -d)[None] for d in range(1, ROUNDS + 1)]
    stacked = jnp.concatenate([kept, *returned], axis=0)
    stacked = stacked.reshape(2 * ROUNDS + 1, channels, channels, 2, bins)
    return jnp.transpose(stacked, (0, 3, 1, 2, 4))


def solution(mesh):
    in_specs = (P(("days", "sta"), None, None), P(("days", "sta"), None), P(("days", "sta"), None))
    out_specs = P(None, None, ("days", "sta"), None, None)
    return jax.shard_map(
        per_device, mesh=mesh, in_specs=in_specs, out_specs=out_specs, check_vma=False
    )
```

```python
import math

import jax
import jax.numpy as jnp
from jax import lax
from jax.experimental import pallas as pl
from jax.experimental.pallas import tpu as pltpu
from jax.sharding import PartitionSpec as P

ROUNDS = 3
COMPONENTS = 3
LANES = 128
PITCH = 16
SKEW = 8
UNROLL = 16
PAIR_COST = pl.CostEstimate(flops=3_000_000_000, transcendentals=0, bytes_accessed=12_000_000)
WHITEN_COST = pl.CostEstimate(flops=2_000_000_000, transcendentals=0, bytes_accessed=8_000_000)

epsilon = 1e-06

NT = (((1,), (1,)), ((), ()))


def fourier_matrix(samples):
    freq_bins = samples // 2
    times_axis = jnp.arange(samples, dtype=jnp.int32)
    bins_axis = jnp.arange(freq_bins, dtype=jnp.int32)
    phase_idx = times_axis[:, None] * bins_axis[None, :] % samples
    angle = 2.0 * math.pi / samples * phase_idx.astype(jnp.float32)
    taper = 0.5 - 0.5 * jnp.cos(2.0 * math.pi / samples * (times_axis.astype(jnp.float32) + 0.5))
    table_re = taper[:, None] * jnp.cos(angle)
    table_im = -taper[:, None] * jnp.sin(angle)
    return jnp.concatenate([table_re.T, table_im.T], axis=1).astype(jnp.bfloat16)


def lane_iota(rows):
    return lax.broadcasted_iota(jnp.int32, (rows, LANES), 1)


def whiten_hour_kernel(hour, counts_ref, records_ref, gap_ref, table_ref, out_ref):
    channels, seg_hour, samples = records_ref.shape
    bins = samples // 2
    stations = gap_ref.shape[0]
    per_tile = LANES // seg_hour
    tile = gap_ref[:, pl.ds(hour // per_tile * LANES, LANES)].astype(jnp.float32)
    turned = pltpu.roll(tile, seg_hour, 1)
    lane = lane_iota(stations)
    low = lane < seg_hour
    doubled = jnp.where(low, tile, turned) if hour % per_tile == 0 else jnp.where(low, turned, tile)
    position = jnp.where(low, lane, lane - seg_hour)
    row = lax.broadcasted_iota(jnp.int32, (bins, LANES), 0)
    side = lane_iota(bins)
    slot = jnp.logical_and(row == 0, side >= seg_hour)
    table = table_ref[...]
    zeros = jnp.zeros((seg_hour, samples), jnp.bfloat16)
    for station in range(stations):
        valid = jnp.where(
            position[station : station + 1] < counts_ref[station, hour],
            doubled[station : station + 1],
            0.0,
        )
        for component in range(channels // stations):
            channel = station * (channels // stations) + component
            record = records_ref[channel]
            upper = jnp.concatenate([record, zeros], axis=0)
            lower = jnp.concatenate([zeros, record], axis=0)
            spectrum = lax.dot_general(
                table[:, :samples], upper, NT, preferred_element_type=jnp.float32
            ) + lax.dot_general(table[:, samples:], lower, NT, preferred_element_type=jnp.float32)
            power = jnp.sum(spectrum * spectrum, axis=0, keepdims=True)
            power = (power + pltpu.roll(power, seg_hour, 1)) * (1.0 / samples)
            scale = lax.rsqrt(power + epsilon) * valid
            out_ref[channel] = jnp.where(slot, valid, spectrum * scale).astype(jnp.bfloat16)


def whiten_hour(records, counts, gap_mask, table, hour):
    channels, segments, samples = records.shape
    seg_hour = segments // counts.shape[1]
    bins = samples // 2
    return pl.pallas_call(
        lambda *refs: whiten_hour_kernel(hour, *refs),
        grid=(1,),
        out_shape=jax.ShapeDtypeStruct((channels, bins, LANES), jnp.bfloat16),
        in_specs=[
            pl.BlockSpec(memory_space=pltpu.SMEM),
            pl.BlockSpec((channels, seg_hour, samples), lambda i: (0, hour, 0)),
            pl.BlockSpec(gap_mask.shape, lambda i: (0, 0)),
            pl.BlockSpec(table.shape, lambda i: (0, 0)),
        ],
        out_specs=pl.BlockSpec((channels, bins, LANES), lambda i: (0, 0, 0)),
        cost_estimate=WHITEN_COST,
        name="whiten_hour",
    )(counts, records, gap_mask, table)


def pair_hour_kernel(hours, first, last, *refs):
    refs = list(refs)
    distance_ref = refs.pop(0) if last else None
    blocks = [refs.pop(0) for _ in range(ROUNDS + 1)]
    before_ref = None if first else refs.pop(0)
    channels, bins, _ = blocks[0].shape
    half = LANES // 2
    if last:
        kept_ref, back_ref, wide_ref, acc_ref, back_f32 = refs
    else:
        acc_ref, wide_ref = refs
    pitch = bins + SKEW
    for q, block in enumerate(blocks):
        for channel in range(channels):
            start = (q * channels + channel) * pitch
            wide_ref[start : start + bins, :] = block[channel].astype(jnp.float32)
    for pad in range(PITCH - channels):
        start = (len(blocks) * channels + pad) * pitch
        wide_ref[start : start + bins, :] = jnp.zeros((bins, LANES), jnp.float32)

    def tile_at(q, k):
        return wide_ref[pl.ds(q * channels * pitch + k, PITCH, stride=pitch), :]

    low = lane_iota(PITCH) < half
    zeroth = [tile_at(q, 0) for q in range(len(blocks))]
    valid = [jnp.where(low, pltpu.roll(t, half, 1), t).astype(jnp.bfloat16) for t in zeroth]
    for q, t in enumerate(zeroth):
        wide_ref[pl.ds(q * channels * pitch, PITCH, stride=pitch), :] = jnp.where(low, t, 0.0)
    joint = 0.5 * lax.dot_general(
        valid[0], jnp.concatenate(valid, axis=0), NT, preferred_element_type=jnp.float32
    )
    weight = 1.0 / (hours * jnp.maximum(joint, 1.0))
    weight = jnp.concatenate([weight, weight], axis=0)
    sign = jnp.where(low, 1.0, -1.0)

    def step(k, carry):
        tiles = [tile_at(q, k) for q in range(len(blocks))]
        turned = (pltpu.roll(tiles[0], half, 1) * sign).astype(jnp.bfloat16)
        tiles = [t.astype(jnp.bfloat16) for t in tiles]
        product = weight * lax.dot_general(
            jnp.concatenate([tiles[0], turned], axis=0),
            jnp.concatenate(tiles, axis=0),
            NT,
            preferred_element_type=jnp.float32,
        )
        if not first:
            product = product + before_ref[k]
        acc_ref[k] = product
        return carry

    lax.fori_loop(0, bins, step, 0, unroll=UNROLL)
    if not last:
        return
    for a in range(channels):
        for part in range(2):
            by_bin = acc_ref[:, part * PITCH + a, :].T
            for q in range(len(blocks)):
                rows = by_bin[q * PITCH : q * PITCH + channels]
                place = pl.ds(a * 2 * channels + part, channels, stride=2)
                if q:
                    kept_ref[distance_ref[q - 1], place, :] = rows
                    back_f32[q - 1, pl.ds(2 * a + part, channels, stride=2 * channels), :] = (
                        -rows if part else rows
                    )
                else:
                    kept_ref[0, place, :] = rows
    for q in range(ROUNDS):
        back_ref[distance_ref[q] - 1] = back_f32[q].astype(jnp.bfloat16)


def pair_hour(blocks, before, distances, hours, last):
    channels, bins, lanes = blocks[0].shape
    first = before is None
    acc = (bins, 2 * PITCH, len(blocks) * PITCH)
    rows = 2 * channels * channels
    wide = pltpu.VMEM(
        ((len(blocks) * channels + PITCH - channels) * (bins + SKEW), lanes), jnp.float32
    )
    vmem = pl.BlockSpec(memory_space=pltpu.VMEM)
    args, specs = [], []
    if last:
        args.append(distances)
        specs.append(pl.BlockSpec(memory_space=pltpu.SMEM))
    args += blocks
    specs += [vmem] * len(blocks)
    if not first:
        args.append(before)
        specs.append(vmem)
    if last:
        out_shape = [
            jax.ShapeDtypeStruct((ROUNDS + 1, rows, lanes), jnp.float32),
            jax.ShapeDtypeStruct((ROUNDS, rows, lanes), jnp.bfloat16),
        ]
        out_specs = [vmem, vmem]
        scratch = [
            wide,
            pltpu.VMEM(acc, jnp.float32),
            pltpu.VMEM((ROUNDS, rows, lanes), jnp.float32),
        ]
    else:
        out_shape = jax.ShapeDtypeStruct(acc, jnp.float32)
        out_specs = vmem
        scratch = [wide]
    return pl.pallas_call(
        lambda *refs: pair_hour_kernel(hours, first, last, *refs),
        out_shape=out_shape,
        in_specs=specs,
        out_specs=out_specs,
        scratch_shapes=scratch,
        cost_estimate=PAIR_COST,
        name="pair_hour_last" if last else "pair_hour",
    )(*args)


def join_kernel(behind_ref, ahead_ref, *refs):
    from_ahead, from_rear, out_ref = refs[:ROUNDS], refs[ROUNDS : 2 * ROUNDS], refs[-1]
    pairs = out_ref.shape[1]

    def put(slot, value):
        out_ref[slot] = value.reshape(pairs, 2, LANES).astype(jnp.bfloat16)

    put(ROUNDS, behind_ref[0] + ahead_ref[0])
    for d in range(1, ROUNDS + 1):
        put(ROUNDS - d, behind_ref[d] + from_rear[d - 1][...].astype(jnp.float32))
        put(ROUNDS + d, ahead_ref[d] + from_ahead[d - 1][...].astype(jnp.float32))


def join(behind, ahead, from_ahead, from_rear):
    _, rows, lanes = behind.shape
    vmem = pl.BlockSpec(memory_space=pltpu.VMEM)
    return pl.pallas_call(
        join_kernel,
        out_shape=jax.ShapeDtypeStruct((2 * ROUNDS + 1, rows // 2, 2, lanes), jnp.bfloat16),
        in_specs=[vmem] * (2 * ROUNDS + 2),
        out_specs=vmem,
        name="join",
    )(behind, ahead, *from_ahead, *from_rear)


LEVEL = 4
DISTANCES = ((3, 1, 2), (1, 3, 2), (3, 2, 1), (1, 2, 3))


def send(value, count, mirrored, *hops):
    levels = count // LEVEL
    pairs = [
        (LEVEL * level + source, LEVEL * ((level + up) % levels) + target)
        for source, target, up in hops
        for level in range(levels)
    ]
    if mirrored:
        pairs = [(count - 1 - source, count - 1 - target) for source, target in pairs]
    return lax.ppermute(value, "sta", pairs)


def shift(value, count, steps):
    pairs = [(source, (source + steps) % count) for source in range(count)]
    return lax.ppermute(value, "sta", pairs)


def fetch_partners(block, count, mirrored):
    if count % LEVEL:
        way = -1 if mirrored else 1
        return [shift(block, count, way * steps) for steps in range(1, ROUNDS + 1)]
    near = send(block, count, mirrored, (0, 1, 0), (2, 3, 0), (1, 0, 1), (3, 2, 1))
    far = send(block, count, mirrored, (0, 2, 0), (1, 3, 0), (2, 1, 1), (3, 0, 1))
    other = send(far, count, mirrored, (0, 1, 0), (1, 0, 0), (2, 3, 0), (3, 2, 0))
    return [near, far, other]


def distances_of(count, position, mirrored):
    if count % LEVEL:
        return jnp.arange(1, ROUNDS + 1, dtype=jnp.int32)
    role = position % LEVEL
    return jnp.array(DISTANCES, jnp.int32)[LEVEL - 1 - role if mirrored else role]


def per_device(records, counts, gap_mask):
    channels, segments, samples = records.shape
    hours = counts.shape[1]
    bins = samples // 2
    count = lax.axis_size("sta")
    position = lax.axis_index("sta")
    table = fourier_matrix(samples)
    whitened = [whiten_hour(records, counts, gap_mask, table, hour) for hour in range(hours)]
    partners = [fetch_partners(whitened[hour], count, hour % 2 == 1) for hour in range(hours)]
    sums = [None, None]
    for hour in range(hours):
        mirrored = hour % 2
        sums[mirrored] = pair_hour(
            [whitened[hour], *partners[hour]],
            sums[mirrored],
            distances_of(count, position, mirrored == 1),
            hours,
            hour + 2 >= hours,
        )
    (behind, back), (ahead, forth) = sums
    from_ahead = [shift(back[d - 1], count, -d) for d in range(1, ROUNDS + 1)]
    from_rear = [shift(forth[d - 1], count, d) for d in range(1, ROUNDS + 1)]
    stacked = join(behind, ahead, from_ahead, from_rear)
    stacked = stacked.reshape(2 * ROUNDS + 1, channels, channels, 2, bins)
    return jnp.transpose(stacked, (0, 3, 1, 2, 4))


def solution(mesh):
    in_specs = (P(("days", "sta"), None, None), P(("days", "sta"), None), P(("days", "sta"), None))
    out_specs = P(None, None, ("days", "sta"), None, None)
    return jax.shard_map(
        per_device, mesh=mesh, in_specs=in_specs, out_specs=out_specs, check_vma=False
    )
```

```python
import math

import jax
import jax.numpy as jnp
from jax import lax
from jax.experimental import pallas as pl
from jax.experimental.pallas import tpu as pltpu
from jax.sharding import PartitionSpec as P

ROUNDS = 3
COMPONENTS = 3
LANES = 128
PITCH = 16
SKEW = 8
UNROLL = 16
MIB = 1 << 20
PAIR_COST = pl.CostEstimate(flops=3_000_000_000, transcendentals=0, bytes_accessed=12_000_000)
WHITEN_COST = pl.CostEstimate(flops=2_000_000_000, transcendentals=0, bytes_accessed=8_000_000)

epsilon = 1e-06

NT = (((1,), (1,)), ((), ()))


def fourier_matrix(samples):
    freq_bins = samples // 2
    times_axis = jnp.arange(samples, dtype=jnp.int32)
    bins_axis = jnp.arange(freq_bins, dtype=jnp.int32)
    phase_idx = times_axis[:, None] * bins_axis[None, :] % samples
    angle = 2.0 * math.pi / samples * phase_idx.astype(jnp.float32)
    taper = 0.5 - 0.5 * jnp.cos(2.0 * math.pi / samples * (times_axis.astype(jnp.float32) + 0.5))
    table_re = taper[:, None] * jnp.cos(angle)
    table_im = -taper[:, None] * jnp.sin(angle)
    return jnp.concatenate([table_re.T, table_im.T], axis=0).astype(jnp.bfloat16)


def lane_iota(rows):
    return lax.broadcasted_iota(jnp.int32, (rows, LANES), 1)


def whiten_hour_kernel(hour, counts_ref, records_ref, gap_ref, table_ref, out_ref):
    channels, seg_hour, samples = records_ref.shape
    bins = samples // 2
    stations = gap_ref.shape[0]
    per_tile = LANES // seg_hour
    tile = gap_ref[:, pl.ds(hour // per_tile * LANES, LANES)].astype(jnp.float32)
    turned = pltpu.roll(tile, seg_hour, 1)
    lane = lane_iota(stations)
    low = lane < seg_hour
    doubled = jnp.where(low, tile, turned) if hour % per_tile == 0 else jnp.where(low, turned, tile)
    position = jnp.where(low, lane, lane - seg_hour)
    row = lax.broadcasted_iota(jnp.int32, (bins, LANES), 0)
    low_side = lane_iota(bins) < seg_hour
    slot = jnp.logical_and(row == 0, jnp.logical_not(low_side))
    table = table_ref[...]
    per_station = channels // stations
    valid = [
        jnp.where(
            position[station : station + 1] < counts_ref[station, hour],
            doubled[station : station + 1],
            0.0,
        )
        for station in range(stations)
    ]
    first_half = lane_iota(1) < seg_hour
    for channel in range(0, channels, 2):
        both = jnp.concatenate([records_ref[channel], records_ref[channel + 1]], axis=0)
        spectrum = lax.dot_general(table, both, NT, preferred_element_type=jnp.float32)
        power = jnp.sum(spectrum * spectrum, axis=0, keepdims=True) * (1.0 / samples)
        pair_valid = jnp.where(
            first_half, valid[channel // per_station], valid[(channel + 1) // per_station]
        )
        scaled = spectrum * (lax.rsqrt(power + epsilon) * pair_valid)
        real, imag = scaled[:bins], scaled[bins:]
        one = jnp.where(low_side, real, pltpu.roll(imag, seg_hour, 1))
        two = jnp.where(low_side, pltpu.roll(real, seg_hour, 1), imag)
        for value, at in ((one, channel), (two, channel + 1)):
            value = jnp.where(slot, valid[at // per_station], value)
            out_ref[at] = value.astype(jnp.bfloat16)


def whiten_hour(records, counts, gap_mask, table, hour):
    channels, segments, samples = records.shape
    seg_hour = segments // counts.shape[1]
    bins = samples // 2
    return pl.pallas_call(
        lambda *refs: whiten_hour_kernel(hour, *refs),
        grid=(1,),
        out_shape=jax.ShapeDtypeStruct((channels, bins, LANES), jnp.bfloat16),
        in_specs=[
            pl.BlockSpec(memory_space=pltpu.SMEM),
            pl.BlockSpec((channels, seg_hour, samples), lambda i: (0, hour, 0)),
            pl.BlockSpec(gap_mask.shape, lambda i: (0, 0)),
            pl.BlockSpec(table.shape, lambda i: (0, 0)),
        ],
        out_specs=pl.BlockSpec((channels, bins, LANES), lambda i: (0, 0, 0)),
        cost_estimate=WHITEN_COST,
        compiler_params=pltpu.CompilerParams(vmem_limit_bytes=8 * MIB),
        name="whiten_hour",
    )(counts, records, gap_mask, table)


def pair_hour_kernel(hours, first, last, *refs):
    refs = list(refs)
    distance_ref = refs.pop(0) if last else None
    blocks = [refs.pop(0) for _ in range(ROUNDS + 1)]
    before_ref = None if first else refs.pop(0)
    channels, bins, _ = blocks[0].shape
    half = LANES // 2
    if last:
        kept_ref, *back_refs, wide_ref, acc_ref, back_f32 = refs
    else:
        acc_ref, wide_ref = refs
    pitch = bins + SKEW
    for q, block in enumerate(blocks):
        for channel in range(channels):
            start = (q * channels + channel) * pitch
            wide_ref[start : start + bins, :] = block[channel].astype(jnp.float32)
    for pad in range(PITCH - channels):
        start = (len(blocks) * channels + pad) * pitch
        wide_ref[start : start + bins, :] = jnp.zeros((bins, LANES), jnp.float32)

    def tile_at(q, k):
        return wide_ref[pl.ds(q * channels * pitch + k, PITCH, stride=pitch), :]

    low = lane_iota(PITCH) < half
    zeroth = [tile_at(q, 0) for q in range(len(blocks))]
    valid = [jnp.where(low, pltpu.roll(t, half, 1), t).astype(jnp.bfloat16) for t in zeroth]
    for q, t in enumerate(zeroth):
        wide_ref[pl.ds(q * channels * pitch, PITCH, stride=pitch), :] = jnp.where(low, t, 0.0)
    joint = 0.5 * lax.dot_general(
        valid[0], jnp.concatenate(valid, axis=0), NT, preferred_element_type=jnp.float32
    )
    weight = 1.0 / (hours * jnp.maximum(joint, 1.0))
    weight = jnp.concatenate([weight, weight], axis=0)
    sign = jnp.where(low, 1.0, -1.0)

    def step(k, carry):
        tiles = [tile_at(q, k) for q in range(len(blocks))]
        turned = (pltpu.roll(tiles[0], half, 1) * sign).astype(jnp.bfloat16)
        tiles = [t.astype(jnp.bfloat16) for t in tiles]
        product = weight * lax.dot_general(
            jnp.concatenate([tiles[0], turned], axis=0),
            jnp.concatenate(tiles, axis=0),
            NT,
            preferred_element_type=jnp.float32,
        )
        if not first:
            product = product + before_ref[k]
        acc_ref[k] = product
        return carry

    lax.fori_loop(0, bins, step, 0, unroll=UNROLL)
    if not last:
        return
    for a in range(channels):
        for part in range(2):
            by_bin = acc_ref[:, part * PITCH + a, :].T
            for q in range(len(blocks)):
                rows = by_bin[q * PITCH : q * PITCH + channels]
                place = pl.ds(a * 2 * channels + part, channels, stride=2)
                if q:
                    kept_ref[distance_ref[q - 1], place, :] = rows
                    back_f32[q - 1, pl.ds(2 * a + part, channels, stride=2 * channels), :] = (
                        -rows if part else rows
                    )
                else:
                    kept_ref[0, place, :] = rows
    for q in range(ROUNDS):
        for d in range(ROUNDS):

            @pl.when(distance_ref[q] == d + 1)
            def _():
                back_refs[d][...] = back_f32[q].astype(jnp.bfloat16)


def pair_hour(blocks, before, distances, hours, last):
    channels, bins, lanes = blocks[0].shape
    first = before is None
    acc = (bins, 2 * PITCH, len(blocks) * PITCH)
    rows = 2 * channels * channels
    wide = pltpu.VMEM(
        ((len(blocks) * channels + PITCH - channels) * (bins + SKEW), lanes), jnp.float32
    )
    vmem = pl.BlockSpec(memory_space=pltpu.VMEM)
    args, specs = [], []
    if last:
        args.append(distances)
        specs.append(pl.BlockSpec(memory_space=pltpu.SMEM))
    args += blocks
    specs += [vmem] * len(blocks)
    if not first:
        args.append(before)
        specs.append(vmem)
    if last:
        out_shape = [
            jax.ShapeDtypeStruct((ROUNDS + 1, rows, lanes), jnp.float32),
            *[jax.ShapeDtypeStruct((rows, lanes), jnp.bfloat16)] * ROUNDS,
        ]
        out_specs = [vmem] * (ROUNDS + 1)
        scratch = [
            wide,
            pltpu.VMEM(acc, jnp.float32),
            pltpu.VMEM((ROUNDS, rows, lanes), jnp.float32),
        ]
    else:
        out_shape = jax.ShapeDtypeStruct(acc, jnp.float32)
        out_specs = vmem
        scratch = [wide]
    return pl.pallas_call(
        lambda *refs: pair_hour_kernel(hours, first, last, *refs),
        out_shape=out_shape,
        in_specs=specs,
        out_specs=out_specs,
        scratch_shapes=scratch,
        cost_estimate=PAIR_COST,
        compiler_params=pltpu.CompilerParams(vmem_limit_bytes=16 * MIB),
        name="pair_hour_last" if last else "pair_hour",
    )(*args)


def join_kernel(behind_ref, ahead_ref, *refs):
    from_ahead, from_rear, out_ref = refs[:ROUNDS], refs[ROUNDS : 2 * ROUNDS], refs[-1]
    pairs = out_ref.shape[1]

    def put(slot, value):
        out_ref[slot] = value.reshape(pairs, 2, LANES).astype(jnp.bfloat16)

    put(ROUNDS, behind_ref[0] + ahead_ref[0])
    for d in range(1, ROUNDS + 1):
        put(ROUNDS - d, behind_ref[d] + from_rear[d - 1][...].astype(jnp.float32))
        put(ROUNDS + d, ahead_ref[d] + from_ahead[d - 1][...].astype(jnp.float32))


def join(behind, ahead, from_ahead, from_rear):
    _, rows, lanes = behind.shape
    vmem = pl.BlockSpec(memory_space=pltpu.VMEM)
    return pl.pallas_call(
        join_kernel,
        out_shape=jax.ShapeDtypeStruct((2 * ROUNDS + 1, rows // 2, 2, lanes), jnp.bfloat16),
        in_specs=[vmem] * (2 * ROUNDS + 2),
        out_specs=vmem,
        compiler_params=pltpu.CompilerParams(vmem_limit_bytes=8 * MIB),
        name="join",
    )(behind, ahead, *from_ahead, *from_rear)


LEVEL = 4
DISTANCES = ((3, 1, 2), (1, 3, 2), (3, 2, 1), (1, 2, 3))


def send(value, count, mirrored, *hops):
    levels = count // LEVEL
    pairs = [
        (LEVEL * level + source, LEVEL * ((level + up) % levels) + target)
        for source, target, up in hops
        for level in range(levels)
    ]
    if mirrored:
        pairs = [(count - 1 - source, count - 1 - target) for source, target in pairs]
    return lax.ppermute(value, "sta", pairs)


def shift(value, count, steps):
    pairs = [(source, (source + steps) % count) for source in range(count)]
    return lax.ppermute(value, "sta", pairs)


def fetch_partners(block, count, mirrored):
    if count % LEVEL:
        way = -1 if mirrored else 1
        return [shift(block, count, way * steps) for steps in range(1, ROUNDS + 1)]
    near = send(block, count, mirrored, (0, 1, 0), (2, 3, 0), (1, 0, 1), (3, 2, 1))
    far = send(block, count, mirrored, (0, 2, 0), (1, 3, 0), (2, 1, 1), (3, 0, 1))
    other = send(far, count, mirrored, (0, 1, 0), (1, 0, 0), (2, 3, 0), (3, 2, 0))
    return [near, far, other]


def distances_of(count, position, mirrored):
    if count % LEVEL:
        return jnp.arange(1, ROUNDS + 1, dtype=jnp.int32)
    role = position % LEVEL
    return jnp.array(DISTANCES, jnp.int32)[LEVEL - 1 - role if mirrored else role]


def per_device(records, counts, gap_mask):
    channels, segments, samples = records.shape
    hours = counts.shape[1]
    bins = samples // 2
    count = lax.axis_size("sta")
    position = lax.axis_index("sta")
    table = fourier_matrix(samples)
    whitened = [whiten_hour(records, counts, gap_mask, table, hour) for hour in range(hours)]
    partners = [fetch_partners(whitened[hour], count, hour % 2 == 1) for hour in range(hours)]
    sums = [None, None]
    for hour in range(hours):
        mirrored = hour % 2
        sums[mirrored] = pair_hour(
            [whitened[hour], *partners[hour]],
            sums[mirrored],
            distances_of(count, position, mirrored == 1),
            hours,
            hour + 2 >= hours,
        )
    (behind, *back), (ahead, *forth) = sums
    from_ahead = [shift(back[d - 1], count, -d) for d in range(1, ROUNDS + 1)]
    from_rear = [shift(forth[d - 1], count, d) for d in range(1, ROUNDS + 1)]
    stacked = join(behind, ahead, from_ahead, from_rear)
    stacked = stacked.reshape(2 * ROUNDS + 1, channels, channels, 2, bins)
    return jnp.transpose(stacked, (0, 3, 1, 2, 4))


def solution(mesh):
    in_specs = (P(("days", "sta"), None, None), P(("days", "sta"), None), P(("days", "sta"), None))
    out_specs = P(None, None, ("days", "sta"), None, None)
    return jax.shard_map(
        per_device, mesh=mesh, in_specs=in_specs, out_specs=out_specs, check_vma=False
    )
```

```python
import math

import jax
import jax.numpy as jnp
from jax import lax
from jax.experimental import pallas as pl
from jax.experimental.pallas import tpu as pltpu
from jax.sharding import PartitionSpec as P


ROUNDS = 3
LANES = 128
PITCH = 16
SKEW = 8
UNROLL = 16
MIB = 1 << 20
PAIR_COST = pl.CostEstimate(flops=3_000_000_000, transcendentals=0, bytes_accessed=12_000_000)
WHITEN_COST = pl.CostEstimate(flops=2_000_000_000, transcendentals=0, bytes_accessed=8_000_000)

epsilon = 1e-06

NT = (((1,), (1,)), ((), ()))


def fourier_matrix(samples):
    freq_bins = samples // 2
    times_axis = jnp.arange(samples, dtype=jnp.int32)
    bins_axis = jnp.arange(freq_bins, dtype=jnp.int32)
    phase_idx = times_axis[:, None] * bins_axis[None, :] % samples
    angle = 2.0 * math.pi / samples * phase_idx.astype(jnp.float32)
    taper = 0.5 - 0.5 * jnp.cos(2.0 * math.pi / samples * (times_axis.astype(jnp.float32) + 0.5))
    table_re = taper[:, None] * jnp.cos(angle)
    table_im = -taper[:, None] * jnp.sin(angle)
    return jnp.concatenate([table_re.T, table_im.T], axis=0).astype(jnp.bfloat16)


def lane_iota(rows):
    return lax.broadcasted_iota(jnp.int32, (rows, LANES), 1)


def whiten_hour_kernel(hour, counts_ref, records_ref, gap_ref, table_ref, out_ref):
    channels, seg_hour, samples = records_ref.shape
    bins = samples // 2
    stations = gap_ref.shape[0]
    per_tile = LANES // seg_hour
    tile = gap_ref[:, pl.ds(hour // per_tile * LANES, LANES)].astype(jnp.float32)
    turned = pltpu.roll(tile, seg_hour, 1)
    lane = lane_iota(stations)
    low = lane < seg_hour
    doubled = jnp.where(low, tile, turned) if hour % per_tile == 0 else jnp.where(low, turned, tile)
    position = jnp.where(low, lane, lane - seg_hour)
    row = lax.broadcasted_iota(jnp.int32, (bins, LANES), 0)
    low_side = lane_iota(bins) < seg_hour
    slot = jnp.logical_and(row == 0, jnp.logical_not(low_side))
    table = table_ref[...]
    per_station = channels // stations
    valid = [
        jnp.where(
            position[station : station + 1] < counts_ref[station, hour],
            doubled[station : station + 1],
            0.0,
        )
        for station in range(stations)
    ]
    first_half = lane_iota(1) < seg_hour
    for channel in range(0, channels, 2):
        both = jnp.concatenate([records_ref[channel], records_ref[channel + 1]], axis=0)
        spectrum = lax.dot_general(table, both, NT, preferred_element_type=jnp.float32)
        power = jnp.sum(spectrum * spectrum, axis=0, keepdims=True) * (1.0 / samples)
        pair_valid = jnp.where(
            first_half, valid[channel // per_station], valid[(channel + 1) // per_station]
        )
        scaled = spectrum * (lax.rsqrt(power + epsilon) * pair_valid)
        real, imag = scaled[:bins], scaled[bins:]
        one = jnp.where(low_side, real, pltpu.roll(imag, seg_hour, 1))
        two = jnp.where(low_side, pltpu.roll(real, seg_hour, 1), imag)
        for value, at in ((one, channel), (two, channel + 1)):
            value = jnp.where(slot, valid[at // per_station], value)
            out_ref[at] = value.astype(jnp.bfloat16)


def whiten_hour(records, counts, gap_mask, table, hour):
    channels, segments, samples = records.shape
    seg_hour = segments // counts.shape[1]
    bins = samples // 2
    return pl.pallas_call(
        lambda *refs: whiten_hour_kernel(hour, *refs),
        grid=(1,),
        out_shape=jax.ShapeDtypeStruct((channels, bins, LANES), jnp.bfloat16),
        in_specs=[
            pl.BlockSpec(memory_space=pltpu.SMEM),
            pl.BlockSpec((channels, seg_hour, samples), lambda i: (0, hour, 0)),
            pl.BlockSpec(gap_mask.shape, lambda i: (0, 0)),
            pl.BlockSpec(table.shape, lambda i: (0, 0)),
        ],
        out_specs=pl.BlockSpec((channels, bins, LANES), lambda i: (0, 0, 0)),
        cost_estimate=WHITEN_COST,
        compiler_params=pltpu.CompilerParams(vmem_limit_bytes=8 * MIB),
        name="whiten_hour",
    )(counts, records, gap_mask, table)


def pair_hour_kernel(hours, first, last, *refs):
    refs = list(refs)
    distance_ref = refs.pop(0) if last else None
    blocks = [refs.pop(0) for _ in range(ROUNDS + 1)]
    before_ref = None if first else refs.pop(0)
    channels, bins, _ = blocks[0].shape
    half = LANES // 2
    if last:
        kept_ref, *back_refs, wide_ref, acc_ref, back_f32 = refs
    else:
        acc_ref, wide_ref = refs
    pitch = bins + SKEW
    for q, block in enumerate(blocks):
        for channel in range(channels):
            start = (q * channels + channel) * pitch
            wide_ref[start : start + bins, :] = block[channel].astype(jnp.float32)
    for pad in range(PITCH - channels):
        start = (len(blocks) * channels + pad) * pitch
        wide_ref[start : start + bins, :] = jnp.zeros((bins, LANES), jnp.float32)

    def tile_at(q, k):
        return wide_ref[pl.ds(q * channels * pitch + k, PITCH, stride=pitch), :]

    low = lane_iota(PITCH) < half
    zeroth = [tile_at(q, 0) for q in range(len(blocks))]
    valid = [jnp.where(low, pltpu.roll(t, half, 1), t).astype(jnp.bfloat16) for t in zeroth]
    for q, t in enumerate(zeroth):
        wide_ref[pl.ds(q * channels * pitch, PITCH, stride=pitch), :] = jnp.where(low, t, 0.0)
    joint = 0.5 * lax.dot_general(
        valid[0], jnp.concatenate(valid, axis=0), NT, preferred_element_type=jnp.float32
    )
    weight = 1.0 / (hours * jnp.maximum(joint, 1.0))
    weight = jnp.concatenate([weight, weight], axis=0)
    sign = jnp.where(low, 1.0, -1.0)

    def step(k, carry):
        tiles = [tile_at(q, k) for q in range(len(blocks))]
        turned = (pltpu.roll(tiles[0], half, 1) * sign).astype(jnp.bfloat16)
        tiles = [t.astype(jnp.bfloat16) for t in tiles]
        product = weight * lax.dot_general(
            jnp.concatenate([tiles[0], turned], axis=0),
            jnp.concatenate(tiles, axis=0),
            NT,
            preferred_element_type=jnp.float32,
        )
        if not first:
            product = product + before_ref[k]
        acc_ref[k] = product
        return carry

    lax.fori_loop(0, bins, step, 0, unroll=UNROLL)
    if not last:
        return
    for a in range(channels):
        for part in range(2):
            by_bin = acc_ref[:, part * PITCH + a, :].T
            for q in range(len(blocks)):
                rows = by_bin[q * PITCH : q * PITCH + channels]
                place = pl.ds(a * 2 * channels + part, channels, stride=2)
                if q:
                    kept_ref[distance_ref[q - 1], place, :] = rows
                    back_f32[q - 1, pl.ds(2 * a + part, channels, stride=2 * channels), :] = (
                        -rows if part else rows
                    )
                else:
                    kept_ref[0, place, :] = rows
    for q in range(ROUNDS):
        for d in range(ROUNDS):

            @pl.when(distance_ref[q] == d + 1)
            def _():
                back_refs[d][...] = back_f32[q].astype(jnp.bfloat16)


def pair_hour(blocks, before, distances, hours, last):
    channels, bins, lanes = blocks[0].shape
    first = before is None
    acc = (bins, 2 * PITCH, len(blocks) * PITCH)
    rows = 2 * channels * channels
    wide = pltpu.VMEM(
        ((len(blocks) * channels + PITCH - channels) * (bins + SKEW), lanes), jnp.float32
    )
    vmem = pl.BlockSpec(memory_space=pltpu.VMEM)
    args, specs = [], []
    if last:
        args.append(distances)
        specs.append(pl.BlockSpec(memory_space=pltpu.SMEM))
    args += blocks
    specs += [vmem] * len(blocks)
    if not first:
        args.append(before)
        specs.append(vmem)
    if last:
        out_shape = [
            jax.ShapeDtypeStruct((ROUNDS + 1, rows, lanes), jnp.float32),
            *[jax.ShapeDtypeStruct((rows, lanes), jnp.bfloat16)] * ROUNDS,
        ]
        out_specs = [vmem] * (ROUNDS + 1)
        scratch = [
            wide,
            pltpu.VMEM(acc, jnp.float32),
            pltpu.VMEM((ROUNDS, rows, lanes), jnp.float32),
        ]
    else:
        out_shape = jax.ShapeDtypeStruct(acc, jnp.float32)
        out_specs = vmem
        scratch = [wide]
    return pl.pallas_call(
        lambda *refs: pair_hour_kernel(hours, first, last, *refs),
        out_shape=out_shape,
        in_specs=specs,
        out_specs=out_specs,
        scratch_shapes=scratch,
        cost_estimate=PAIR_COST,
        compiler_params=pltpu.CompilerParams(vmem_limit_bytes=16 * MIB),
        name="pair_hour_last" if last else "pair_hour",
    )(*args)


def join_kernel(behind_ref, ahead_ref, *refs):
    from_ahead, from_rear, out_ref = refs[:ROUNDS], refs[ROUNDS : 2 * ROUNDS], refs[-1]
    pairs = out_ref.shape[1]

    def put(slot, value):
        out_ref[slot] = value.reshape(pairs, 2, LANES).astype(jnp.bfloat16)

    put(ROUNDS, behind_ref[0] + ahead_ref[0])
    for d in range(1, ROUNDS + 1):
        put(ROUNDS - d, behind_ref[d] + from_rear[d - 1][...].astype(jnp.float32))
        put(ROUNDS + d, ahead_ref[d] + from_ahead[d - 1][...].astype(jnp.float32))


def join(behind, ahead, from_ahead, from_rear):
    _, rows, lanes = behind.shape
    vmem = pl.BlockSpec(memory_space=pltpu.VMEM)
    return pl.pallas_call(
        join_kernel,
        out_shape=jax.ShapeDtypeStruct((2 * ROUNDS + 1, rows // 2, 2, lanes), jnp.bfloat16),
        in_specs=[vmem] * (2 * ROUNDS + 2),
        out_specs=vmem,
        compiler_params=pltpu.CompilerParams(vmem_limit_bytes=8 * MIB),
        name="join",
    )(behind, ahead, *from_ahead, *from_rear)


LEVEL = 4
DISTANCES = ((3, 1, 2), (1, 3, 2), (3, 2, 1), (1, 2, 3))


def send(value, count, mirrored, *hops):
    levels = count // LEVEL
    pairs = [
        (LEVEL * level + source, LEVEL * ((level + up) % levels) + target)
        for source, target, up in hops
        for level in range(levels)
    ]
    if mirrored:
        pairs = [(count - 1 - source, count - 1 - target) for source, target in pairs]
    return lax.ppermute(value, "sta", pairs)


def shift(value, count, steps):
    pairs = [(source, (source + steps) % count) for source in range(count)]
    return lax.ppermute(value, "sta", pairs)


def fetch_partners(block, count, hour):
    mirrored = hour % 2 == 1
    if count % LEVEL:
        way = -1 if mirrored else 1
        return [shift(block, count, way * steps) for steps in range(1, ROUNDS + 1)]
    far = send(block, count, mirrored, (0, 2, 0), (1, 3, 0), (2, 1, 1), (3, 0, 1))
    near = send(block, count, mirrored, (0, 1, 0), (2, 3, 0), (1, 0, 1), (3, 2, 1))
    other = send(far, count, mirrored, (0, 1, 0), (1, 0, 0), (2, 3, 0), (3, 2, 0))
    return [near, far, other]


def distances_of(count, position, mirrored):
    if count % LEVEL:
        return jnp.arange(1, ROUNDS + 1, dtype=jnp.int32)
    role = position % LEVEL
    return jnp.array(DISTANCES, jnp.int32)[LEVEL - 1 - role if mirrored else role]


def spectra(records, counts, gap_mask):
    channels, _, samples = records.shape
    hours = counts.shape[1]
    bins = samples // 2
    count = lax.axis_size("sta")
    position = lax.axis_index("sta")
    table = fourier_matrix(samples)
    whitened = [whiten_hour(records, counts, gap_mask, table, hour) for hour in range(hours)]
    partners = [fetch_partners(whitened[hour], count, hour) for hour in range(hours)]
    sums = [None, None]
    for hour in range(hours):
        mirrored = hour % 2
        sums[mirrored] = pair_hour(
            [whitened[hour], *partners[hour]],
            sums[mirrored],
            distances_of(count, position, mirrored == 1),
            hours,
            hour + 2 >= hours,
        )
    (behind, *back), (ahead, *forth) = sums
    from_ahead = [shift(back[d - 1], count, -d) for d in range(1, ROUNDS + 1)]
    from_rear = [shift(forth[d - 1], count, d) for d in range(1, ROUNDS + 1)]
    stacked = join(behind, ahead, from_ahead, from_rear)
    stacked = stacked.reshape(2 * ROUNDS + 1, channels, channels, 2, bins)
    return jnp.transpose(stacked, (0, 3, 1, 2, 4))


def solution(mesh):
    in_specs = (P(("days", "sta"), None, None), P(("days", "sta"), None), P(("days", "sta"), None))
    out_specs = P(None, None, ("days", "sta"), None, None)
    return jax.shard_map(
        spectra, mesh=mesh, in_specs=in_specs, out_specs=out_specs, check_vma=False
    )
```

```python
import math

import jax
import jax.numpy as jnp
from jax import lax
from jax.experimental import pallas as pl
from jax.experimental.pallas import tpu as pltpu
from jax.sharding import PartitionSpec as P


ROUNDS = 3
LANES = 128
PITCH = 16
SKEW = 8
UNROLL = 8
MIB = 1 << 20
PAIR_COST = pl.CostEstimate(flops=3_000_000_000, transcendentals=0, bytes_accessed=12_000_000)
WHITEN_COST = pl.CostEstimate(flops=2_000_000_000, transcendentals=0, bytes_accessed=8_000_000)

epsilon = 1e-06

NT = (((1,), (1,)), ((), ()))


def fourier_matrix(samples):
    freq_bins = samples // 2
    times_axis = jnp.arange(samples, dtype=jnp.int32)
    bins_axis = jnp.arange(freq_bins, dtype=jnp.int32)
    phase_idx = times_axis[:, None] * bins_axis[None, :] % samples
    angle = 2.0 * math.pi / samples * phase_idx.astype(jnp.float32)
    taper = 0.5 - 0.5 * jnp.cos(2.0 * math.pi / samples * (times_axis.astype(jnp.float32) + 0.5))
    table_re = taper[:, None] * jnp.cos(angle)
    table_im = -taper[:, None] * jnp.sin(angle)
    return jnp.concatenate([table_re.T, table_im.T], axis=0).astype(jnp.bfloat16)


def lane_iota(rows):
    return lax.broadcasted_iota(jnp.int32, (rows, LANES), 1)


def validity_rows(hour, seg_hour, counts_ref, gap_ref):
    stations = gap_ref.shape[0]
    per_tile = LANES // seg_hour
    tile = gap_ref[:, pl.ds(hour // per_tile * LANES, LANES)].astype(jnp.float32)
    turned = pltpu.roll(tile, seg_hour, 1)
    lane = lane_iota(stations)
    low = lane < seg_hour
    doubled = jnp.where(low, tile, turned) if hour % per_tile == 0 else jnp.where(low, turned, tile)
    position = jnp.where(low, lane, lane - seg_hour)
    return [
        jnp.where(
            position[station : station + 1] < counts_ref[station, hour],
            doubled[station : station + 1],
            0.0,
        )
        for station in range(stations)
    ]


def whiten_block(records_ref, valid, table_ref, out_ref):
    channels, seg_hour, samples = records_ref.shape
    bins = samples // 2
    row = lax.broadcasted_iota(jnp.int32, (bins, LANES), 0)
    low_side = lane_iota(bins) < seg_hour
    slot = jnp.logical_and(row == 0, jnp.logical_not(low_side))
    table = table_ref[...]
    per_station = channels // len(valid)
    first_half = lane_iota(1) < seg_hour
    for channel in range(0, channels, 2):
        both = jnp.concatenate([records_ref[channel], records_ref[channel + 1]], axis=0)
        spectrum = lax.dot_general(table, both, NT, preferred_element_type=jnp.float32)
        power = jnp.sum(spectrum * spectrum, axis=0, keepdims=True) * (1.0 / samples)
        pair_valid = jnp.where(
            first_half, valid[channel // per_station], valid[(channel + 1) // per_station]
        )
        scaled = spectrum * (lax.rsqrt(power + epsilon) * pair_valid)
        real, imag = scaled[:bins], scaled[bins:]
        one = jnp.where(low_side, real, pltpu.roll(imag, seg_hour, 1))
        two = jnp.where(low_side, pltpu.roll(real, seg_hour, 1), imag)
        for value, at in ((one, channel), (two, channel + 1)):
            value = jnp.where(slot, valid[at // per_station], value)
            out_ref[at] = value.astype(jnp.bfloat16)


def whiten_first_kernel(counts_hbm, records_hbm, gap_hbm, table_ref, *refs):
    out_ref, rest_ref, valid_ref, counts_ref, records_ref, gap_ref, sems = refs
    seg_hour = records_ref.shape[1]
    hours = valid_ref.shape[0]

    def hour_of(hour):
        return records_hbm.at[:, pl.ds(hour * seg_hour, seg_hour), :]

    moves = [(counts_hbm, counts_ref), (gap_hbm, gap_ref), (hour_of(0), records_ref)]
    moves += [(hour_of(hour), rest_ref.at[hour - 1]) for hour in range(1, hours)]
    copies = [
        pltpu.make_async_copy(source, target, sems.at[i])
        for i, (source, target) in enumerate(moves)
    ]
    for copy in copies:
        copy.start()
    for copy in copies[:3]:
        copy.wait()
    valid = [validity_rows(hour, seg_hour, counts_ref, gap_ref) for hour in range(hours)]
    for hour in range(1, hours):
        for station, row in enumerate(valid[hour]):
            valid_ref[hour, station : station + 1, :] = row
    whiten_block(records_ref, valid[0], table_ref, out_ref)
    for copy in copies[3:]:
        copy.wait()


def whiten_first(records, counts, gap_mask, table):
    channels, segments, samples = records.shape
    stations, hours = counts.shape
    seg_hour = segments // hours
    hbm = pl.BlockSpec(memory_space=pltpu.HBM)
    vmem = pl.BlockSpec(memory_space=pltpu.VMEM)
    block = (channels, seg_hour, samples)
    return pl.pallas_call(
        whiten_first_kernel,
        out_shape=[
            jax.ShapeDtypeStruct((channels, samples // 2, LANES), jnp.bfloat16),
            jax.ShapeDtypeStruct((hours - 1, *block), records.dtype),
            jax.ShapeDtypeStruct((hours, stations, LANES), jnp.float32),
        ],
        in_specs=[hbm, hbm, hbm, vmem],
        out_specs=[vmem] * 3,
        scratch_shapes=[
            pltpu.SMEM(counts.shape, counts.dtype),
            pltpu.VMEM(block, records.dtype),
            pltpu.VMEM(gap_mask.shape, gap_mask.dtype),
            pltpu.SemaphoreType.DMA((hours + 2,)),
        ],
        cost_estimate=WHITEN_COST,
        compiler_params=pltpu.CompilerParams(vmem_limit_bytes=8 * MIB),
        name="whiten_first",
    )(
        *(pltpu.with_memory_space_constraint(x, pltpu.HBM) for x in (counts, records, gap_mask)),
        table,
    )


def whiten_hour_kernel(hour, rest_ref, valid_ref, table_ref, out_ref):
    valid = [valid_ref[hour, station : station + 1, :] for station in range(valid_ref.shape[1])]
    whiten_block(rest_ref.at[hour - 1], valid, table_ref, out_ref)


def whiten_hour(rest, valid, table, hour):
    _, channels, _, samples = rest.shape
    vmem = pl.BlockSpec(memory_space=pltpu.VMEM)
    return pl.pallas_call(
        lambda *refs: whiten_hour_kernel(hour, *refs),
        out_shape=jax.ShapeDtypeStruct((channels, samples // 2, LANES), jnp.bfloat16),
        in_specs=[vmem] * 3,
        out_specs=vmem,
        cost_estimate=WHITEN_COST,
        compiler_params=pltpu.CompilerParams(vmem_limit_bytes=8 * MIB),
        name="whiten_hour",
    )(rest, valid, table)


def pair_hour_kernel(hours, first, last, *refs):
    refs = list(refs)
    distance_ref = refs.pop(0) if last else None
    blocks = [refs.pop(0) for _ in range(ROUNDS + 1)]
    before_ref = None if first else refs.pop(0)
    channels, bins, _ = blocks[0].shape
    half = LANES // 2
    if last:
        kept_ref, *back_refs, wide_ref, acc_ref, back_f32 = refs
    else:
        acc_ref, wide_ref = refs
    pitch = bins + SKEW
    for q, block in enumerate(blocks):
        for channel in range(channels):
            start = (q * channels + channel) * pitch
            wide_ref[start : start + bins, :] = block[channel].astype(jnp.float32)
    for pad in range(PITCH - channels):
        start = (len(blocks) * channels + pad) * pitch
        wide_ref[start : start + bins, :] = jnp.zeros((bins, LANES), jnp.float32)

    def tile_at(q, k):
        return wide_ref[pl.ds(q * channels * pitch + k, PITCH, stride=pitch), :]

    low = lane_iota(PITCH) < half
    zeroth = [tile_at(q, 0) for q in range(len(blocks))]
    valid = [jnp.where(low, pltpu.roll(t, half, 1), t).astype(jnp.bfloat16) for t in zeroth]
    for q, t in enumerate(zeroth):
        wide_ref[pl.ds(q * channels * pitch, PITCH, stride=pitch), :] = jnp.where(low, t, 0.0)
    joint = 0.5 * lax.dot_general(
        valid[0], jnp.concatenate(valid + valid, axis=0), NT, preferred_element_type=jnp.float32
    )
    weight = 1.0 / (hours * jnp.maximum(joint, 1.0))
    weight = jnp.concatenate([weight, weight], axis=0)
    sign = jnp.where(low, 1.0, -1.0)
    low_product = lane_iota(2 * PITCH) < half
    half_bins = bins // 2

    def step(k, carry):
        left, right = [], []
        for part in range(2):
            tiles = [tile_at(q, k + part * half_bins) for q in range(len(blocks))]
            turned = pltpu.roll(tiles[0], half, 1) * sign
            tiles = [t.astype(jnp.bfloat16) for t in tiles]
            left += [tiles[0], turned.astype(jnp.bfloat16)]
            right += tiles
        product = lax.dot_general(
            jnp.concatenate(left, axis=0),
            jnp.concatenate(right, axis=0),
            NT,
            preferred_element_type=jnp.float32,
        )
        product = weight * jnp.where(low_product, product[: 2 * PITCH], product[2 * PITCH :])
        place = pl.ds(pl.multiple_of(k * 2 * PITCH, 2 * PITCH), 2 * PITCH)
        if not first:
            product = product + before_ref[place, :]
        acc_ref[place, :] = product
        return carry

    lax.fori_loop(0, half_bins, step, 0, unroll=UNROLL)
    if not last:
        return
    row = lax.broadcasted_iota(jnp.int32, (LANES, LANES), 0)
    unit = (row == lane_iota(LANES)).astype(jnp.bfloat16)
    low_half = lane_iota(half) < half

    def finish(a, carry):
        both = jnp.concatenate(
            [
                acc_ref[pl.ds(part * PITCH + a, half_bins, stride=2 * PITCH), :]
                for part in range(2)
            ],
            axis=0,
        )
        high = both.astype(jnp.bfloat16)
        rest = (both - high.astype(jnp.float32)).astype(jnp.bfloat16)
        by_bin = lax.dot_general(
            unit, high, NT, preferred_element_type=jnp.float32
        ) + lax.dot_general(unit, rest, NT, preferred_element_type=jnp.float32)
        upper, lower = by_bin[:half], by_bin[half:]
        real = jnp.where(low_half, upper, pltpu.roll(lower, half, 1))
        imag = jnp.where(low_half, pltpu.roll(upper, half, 1), lower)
        for part, value in enumerate((real, imag)):
            for q in range(len(blocks)):
                rows = value[q * PITCH : q * PITCH + channels]
                place = pl.ds(a * 2 * channels + part, channels, stride=2)
                if q:
                    kept_ref[distance_ref[q - 1], place, :] = rows
                    back_f32[q - 1, pl.ds(2 * a + part, channels, stride=2 * channels), :] = (
                        -rows if part else rows
                    )
                else:
                    kept_ref[0, place, :] = rows
        return carry

    lax.fori_loop(0, channels, finish, 0, unroll=12)
    for q in range(ROUNDS):
        for d in range(ROUNDS):

            @pl.when(distance_ref[q] == d + 1)
            def _():
                back_refs[d][...] = back_f32[q].astype(jnp.bfloat16)


def pair_hour(blocks, before, distances, hours, last):
    channels, bins, lanes = blocks[0].shape
    first = before is None
    acc = (bins // 2 * 2 * PITCH, lanes)
    rows = 2 * channels * channels
    wide = pltpu.VMEM(
        ((len(blocks) * channels + PITCH - channels) * (bins + SKEW), lanes), jnp.float32
    )
    vmem = pl.BlockSpec(memory_space=pltpu.VMEM)
    args, specs = [], []
    if last:
        args.append(distances)
        specs.append(pl.BlockSpec(memory_space=pltpu.SMEM))
    args += blocks
    specs += [vmem] * len(blocks)
    if not first:
        args.append(before)
        specs.append(vmem)
    if last:
        out_shape = [
            jax.ShapeDtypeStruct((ROUNDS + 1, rows, lanes), jnp.float32),
            *[jax.ShapeDtypeStruct((rows, lanes), jnp.bfloat16)] * ROUNDS,
        ]
        out_specs = [vmem] * (ROUNDS + 1)
        scratch = [
            wide,
            pltpu.VMEM(acc, jnp.float32),
            pltpu.VMEM((ROUNDS, rows, lanes), jnp.float32),
        ]
    else:
        out_shape = jax.ShapeDtypeStruct(acc, jnp.float32)
        out_specs = vmem
        scratch = [wide]
    return pl.pallas_call(
        lambda *refs: pair_hour_kernel(hours, first, last, *refs),
        out_shape=out_shape,
        in_specs=specs,
        out_specs=out_specs,
        scratch_shapes=scratch,
        cost_estimate=PAIR_COST,
        compiler_params=pltpu.CompilerParams(vmem_limit_bytes=16 * MIB),
        name="pair_hour_last" if last else "pair_hour",
    )(*args)


def join_kernel(behind_ref, ahead_ref, *refs):
    from_ahead, from_rear, out_ref = refs[:ROUNDS], refs[ROUNDS : 2 * ROUNDS], refs[-1]
    pairs = out_ref.shape[1]

    def put(slot, value):
        out_ref[slot] = value.reshape(pairs, 2, LANES).astype(jnp.bfloat16)

    put(ROUNDS, behind_ref[0] + ahead_ref[0])
    for d in range(1, ROUNDS + 1):
        put(ROUNDS - d, behind_ref[d] + from_rear[d - 1][...].astype(jnp.float32))
        put(ROUNDS + d, ahead_ref[d] + from_ahead[d - 1][...].astype(jnp.float32))


def join(behind, ahead, from_ahead, from_rear):
    _, rows, lanes = behind.shape
    vmem = pl.BlockSpec(memory_space=pltpu.VMEM)
    return pl.pallas_call(
        join_kernel,
        out_shape=jax.ShapeDtypeStruct((2 * ROUNDS + 1, rows // 2, 2, lanes), jnp.bfloat16),
        in_specs=[vmem] * (2 * ROUNDS + 2),
        out_specs=vmem,
        compiler_params=pltpu.CompilerParams(vmem_limit_bytes=8 * MIB),
        name="join",
    )(behind, ahead, *from_ahead, *from_rear)


LEVEL = 4
DISTANCES = ((3, 1, 2), (1, 3, 2), (3, 2, 1), (1, 2, 3))


def send(value, count, mirrored, *hops):
    levels = count // LEVEL
    pairs = [
        (LEVEL * level + source, LEVEL * ((level + up) % levels) + target)
        for source, target, up in hops
        for level in range(levels)
    ]
    if mirrored:
        pairs = [(count - 1 - source, count - 1 - target) for source, target in pairs]
    return lax.ppermute(value, "sta", pairs)


def shift(value, count, steps):
    pairs = [(source, (source + steps) % count) for source in range(count)]
    return lax.ppermute(value, "sta", pairs)


def fetch_partners(block, count, hour):
    mirrored = hour % 2 == 1
    if count % LEVEL:
        way = -1 if mirrored else 1
        return [shift(block, count, way * steps) for steps in range(1, ROUNDS + 1)]
    far = send(block, count, mirrored, (0, 2, 0), (1, 3, 0), (2, 1, 1), (3, 0, 1))
    near = send(block, count, mirrored, (0, 1, 0), (2, 3, 0), (1, 0, 1), (3, 2, 1))
    other = send(far, count, mirrored, (0, 1, 0), (1, 0, 0), (2, 3, 0), (3, 2, 0))
    return [near, far, other]


def distances_of(count, position, mirrored):
    if count % LEVEL:
        return jnp.arange(1, ROUNDS + 1, dtype=jnp.int32)
    role = position % LEVEL
    return jnp.array(DISTANCES, jnp.int32)[LEVEL - 1 - role if mirrored else role]


def spectra(records, counts, gap_mask):
    channels, _, samples = records.shape
    hours = counts.shape[1]
    bins = samples // 2
    count = lax.axis_size("sta")
    position = lax.axis_index("sta")
    table = fourier_matrix(samples)
    first, rest, valid = whiten_first(records, counts, gap_mask, table)
    whitened = [first] + [whiten_hour(rest, valid, table, hour) for hour in range(1, hours)]
    partners = [fetch_partners(whitened[hour], count, hour) for hour in range(hours)]
    sums = [None, None]
    for hour in range(hours):
        mirrored = hour % 2
        sums[mirrored] = pair_hour(
            [whitened[hour], *partners[hour]],
            sums[mirrored],
            distances_of(count, position, mirrored == 1),
            hours,
            hour + 2 >= hours,
        )
    (behind, *back), (ahead, *forth) = sums
    from_ahead, from_rear = [], []
    for d in range(1, ROUNDS + 1):
        from_ahead.append(shift(back[d - 1], count, -d))
        from_rear.append(shift(forth[d - 1], count, d))
    stacked = join(behind, ahead, from_ahead, from_rear)
    stacked = stacked.reshape(2 * ROUNDS + 1, channels, channels, 2, bins)
    return jnp.transpose(stacked, (0, 3, 1, 2, 4))


def solution(mesh):
    in_specs = (P(("days", "sta"), None, None), P(("days", "sta"), None), P(("days", "sta"), None))
    out_specs = P(None, None, ("days", "sta"), None, None)
    return jax.shard_map(
        spectra, mesh=mesh, in_specs=in_specs, out_specs=out_specs, check_vma=False
    )
```

```python
import math

import jax
import jax.numpy as jnp
from jax import lax
from jax.experimental import pallas as pl
from jax.experimental.pallas import tpu as pltpu
from jax.sharding import PartitionSpec as P


ROUNDS = 3
LANES = 128
PITCH = 16
SKEW = 8
MIB = 1 << 20
PAIR_LIMIT = 10 * MIB
PAIR_COST = pl.CostEstimate(flops=3_000_000_000, transcendentals=0, bytes_accessed=12_000_000)
WHITEN_COST = pl.CostEstimate(flops=2_000_000_000, transcendentals=0, bytes_accessed=8_000_000)

epsilon = 1e-06

NT = (((1,), (1,)), ((), ()))


def fourier_matrix(samples):
    freq_bins = samples // 2
    times_axis = jnp.arange(samples, dtype=jnp.int32)
    bins_axis = jnp.arange(freq_bins, dtype=jnp.int32)
    phase_idx = times_axis[:, None] * bins_axis[None, :] % samples
    angle = 2.0 * math.pi / samples * phase_idx.astype(jnp.float32)
    taper = 0.5 - 0.5 * jnp.cos(2.0 * math.pi / samples * (times_axis.astype(jnp.float32) + 0.5))
    table_re = taper[:, None] * jnp.cos(angle)
    table_im = -taper[:, None] * jnp.sin(angle)
    return jnp.concatenate([table_re.T, table_im.T], axis=0).astype(jnp.bfloat16)


def lane_iota(rows):
    return lax.broadcasted_iota(jnp.int32, (rows, LANES), 1)


def validity_rows(hour, seg_hour, counts_ref, gap_ref):
    stations = gap_ref.shape[0]
    per_tile = LANES // seg_hour
    tile = gap_ref[:, pl.ds(hour // per_tile * LANES, LANES)].astype(jnp.float32)
    turned = pltpu.roll(tile, seg_hour, 1)
    lane = lane_iota(stations)
    low = lane < seg_hour
    doubled = jnp.where(low, tile, turned) if hour % per_tile == 0 else jnp.where(low, turned, tile)
    position = jnp.where(low, lane, lane - seg_hour)
    return [
        jnp.where(
            position[station : station + 1] < counts_ref[station, hour],
            doubled[station : station + 1],
            0.0,
        )
        for station in range(stations)
    ]


def whiten_block(records_ref, valid, table_ref, out_ref):
    channels, seg_hour, samples = records_ref.shape
    bins = samples // 2
    row = lax.broadcasted_iota(jnp.int32, (bins, LANES), 0)
    low_side = lane_iota(bins) < seg_hour
    slot = jnp.logical_and(row == 0, jnp.logical_not(low_side))
    table = table_ref[...]
    per_station = channels // len(valid)
    first_half = lane_iota(1) < seg_hour
    for channel in range(0, channels, 2):
        both = jnp.concatenate([records_ref[channel], records_ref[channel + 1]], axis=0)
        spectrum = lax.dot_general(table, both, NT, preferred_element_type=jnp.float32)
        power = jnp.sum(spectrum * spectrum, axis=0, keepdims=True) * (1.0 / samples)
        pair_valid = jnp.where(
            first_half, valid[channel // per_station], valid[(channel + 1) // per_station]
        )
        scaled = spectrum * (lax.rsqrt(power + epsilon) * pair_valid)
        real, imag = scaled[:bins], scaled[bins:]
        one = jnp.where(low_side, real, pltpu.roll(imag, seg_hour, 1))
        two = jnp.where(low_side, pltpu.roll(real, seg_hour, 1), imag)
        for value, at in ((one, channel), (two, channel + 1)):
            value = jnp.where(slot, valid[at // per_station], value)
            out_ref[at] = value.astype(jnp.bfloat16)


def whiten_first_kernel(counts_hbm, records_hbm, gap_hbm, table_ref, *refs):
    out_ref, rest_ref, valid_ref, counts_ref, records_ref, gap_ref, sems = refs
    seg_hour = records_ref.shape[1]
    hours = valid_ref.shape[0]

    def hour_of(hour):
        return records_hbm.at[:, pl.ds(hour * seg_hour, seg_hour), :]

    moves = [(counts_hbm, counts_ref), (gap_hbm, gap_ref), (hour_of(0), records_ref)]
    moves += [(hour_of(hour), rest_ref.at[hour - 1]) for hour in range(1, hours)]
    copies = [
        pltpu.make_async_copy(source, target, sems.at[i])
        for i, (source, target) in enumerate(moves)
    ]
    for copy in copies:
        copy.start()
    for copy in copies[:3]:
        copy.wait()
    valid = [validity_rows(hour, seg_hour, counts_ref, gap_ref) for hour in range(hours)]
    for hour in range(1, hours):
        for station, row in enumerate(valid[hour]):
            valid_ref[hour, station : station + 1, :] = row
    whiten_block(records_ref, valid[0], table_ref, out_ref)
    for copy in copies[3:]:
        copy.wait()


def whiten_first(records, counts, gap_mask, table):
    channels, segments, samples = records.shape
    stations, hours = counts.shape
    seg_hour = segments // hours
    hbm = pl.BlockSpec(memory_space=pltpu.HBM)
    vmem = pl.BlockSpec(memory_space=pltpu.VMEM)
    block = (channels, seg_hour, samples)
    return pl.pallas_call(
        whiten_first_kernel,
        out_shape=[
            jax.ShapeDtypeStruct((channels, samples // 2, LANES), jnp.bfloat16),
            jax.ShapeDtypeStruct((hours - 1, *block), records.dtype),
            jax.ShapeDtypeStruct((hours, stations, LANES), jnp.float32),
        ],
        in_specs=[hbm, hbm, hbm, vmem],
        out_specs=[vmem] * 3,
        scratch_shapes=[
            pltpu.SMEM(counts.shape, counts.dtype),
            pltpu.VMEM(block, records.dtype),
            pltpu.VMEM(gap_mask.shape, gap_mask.dtype),
            pltpu.SemaphoreType.DMA((hours + 2,)),
        ],
        cost_estimate=WHITEN_COST,
        compiler_params=pltpu.CompilerParams(vmem_limit_bytes=4 * MIB),
        name="whiten_first",
    )(
        *(pltpu.with_memory_space_constraint(x, pltpu.HBM) for x in (counts, records, gap_mask)),
        table,
    )


def whiten_hour_kernel(hour, rest_ref, valid_ref, table_ref, out_ref):
    valid = [valid_ref[hour, station : station + 1, :] for station in range(valid_ref.shape[1])]
    whiten_block(rest_ref.at[hour - 1], valid, table_ref, out_ref)


def whiten_hour(rest, valid, table, hour):
    _, channels, _, samples = rest.shape
    vmem = pl.BlockSpec(memory_space=pltpu.VMEM)
    return pl.pallas_call(
        lambda *refs: whiten_hour_kernel(hour, *refs),
        out_shape=jax.ShapeDtypeStruct((channels, samples // 2, LANES), jnp.bfloat16),
        in_specs=[vmem] * 3,
        out_specs=vmem,
        cost_estimate=WHITEN_COST,
        compiler_params=pltpu.CompilerParams(vmem_limit_bytes=4 * MIB),
        name="whiten_hour",
    )(rest, valid, table)


def pair_hour_kernel(hours, first, last, mirrored, *refs):
    refs = list(refs)
    blocks = [refs.pop(0) for _ in range(ROUNDS + 1)]
    before_ref = None if first else refs.pop(0)
    channels, bins, _ = blocks[0].shape
    half = LANES // 2
    if last:
        kept_ref, *back_refs, wide_ref, acc_ref, back_f32 = refs
    else:
        acc_ref, wide_ref = refs
    pitch = bins + SKEW
    for q, block in enumerate(blocks):
        for channel in range(channels):
            start = (q * channels + channel) * pitch
            wide_ref[start : start + bins, :] = block[channel].astype(jnp.float32)
    for pad in range(PITCH - channels):
        start = (len(blocks) * channels + pad) * pitch
        wide_ref[start : start + bins, :] = jnp.zeros((bins, LANES), jnp.float32)

    def tile_at(q, k):
        return wide_ref[pl.ds(q * channels * pitch + k, PITCH, stride=pitch), :]

    low = lane_iota(PITCH) < half
    zeroth = [tile_at(q, 0) for q in range(len(blocks))]
    valid = [jnp.where(low, pltpu.roll(t, half, 1), t).astype(jnp.bfloat16) for t in zeroth]
    for q, t in enumerate(zeroth):
        wide_ref[pl.ds(q * channels * pitch, PITCH, stride=pitch), :] = jnp.where(low, t, 0.0)
    joint = 0.5 * lax.dot_general(
        valid[0], jnp.concatenate(valid + valid, axis=0), NT, preferred_element_type=jnp.float32
    )
    weight = 1.0 / (hours * jnp.maximum(joint, 1.0))
    weight = jnp.concatenate([weight, weight], axis=0)
    sign = jnp.where(low, 1.0, -1.0)
    low_product = lane_iota(2 * PITCH) < half
    half_bins = bins // 2

    def step(k, carry):
        left, right = [], []
        for part in range(2):
            tiles = [tile_at(q, k + part * half_bins) for q in range(len(blocks))]
            turned = pltpu.roll(tiles[0], half, 1) * sign
            tiles = [t.astype(jnp.bfloat16) for t in tiles]
            left += [tiles[0], turned.astype(jnp.bfloat16)]
            right += tiles
        product = lax.dot_general(
            jnp.concatenate(left, axis=0),
            jnp.concatenate(right, axis=0),
            NT,
            preferred_element_type=jnp.float32,
        )
        product = weight * jnp.where(low_product, product[: 2 * PITCH], product[2 * PITCH :])
        place = pl.ds(pl.multiple_of(k * 2 * PITCH, 2 * PITCH), 2 * PITCH)
        if not first:
            product = product + before_ref[place, :]
        acc_ref[place, :] = product
        return carry

    lax.fori_loop(0, half_bins, step, 0, unroll=half_bins)
    if not last:
        return
    low_half = lane_iota(half) < half
    distances = distances_of(mirrored)

    def finish(a, carry):
        both = jnp.concatenate(
            [
                acc_ref[pl.ds(part * PITCH + a, half_bins, stride=2 * PITCH), :]
                for part in range(2)
            ],
            axis=0,
        )
        by_bin = both.T
        upper, lower = by_bin[:half], by_bin[half:]
        real = jnp.where(low_half, upper, pltpu.roll(lower, half, 1))
        imag = jnp.where(low_half, pltpu.roll(upper, half, 1), lower)
        for part, value in enumerate((real, imag)):
            for q in range(len(blocks)):
                rows = value[q * PITCH : q * PITCH + channels]
                place = pl.ds(a * 2 * channels + part, channels, stride=2)
                if q:
                    kept_ref[distances[q - 1], place, :] = rows
                    back_f32[q - 1, pl.ds(2 * a + part, channels, stride=2 * channels), :] = (
                        -rows if part else rows
                    )
                else:
                    kept_ref[0, place, :] = rows
        return carry

    lax.fori_loop(0, channels, finish, 0, unroll=12)
    for q in range(ROUNDS):
        for d in range(ROUNDS):

            @pl.when(distances[q] == d + 1)
            def _():
                back_refs[d][...] = back_f32[q].astype(jnp.bfloat16)


def pair_hour(blocks, before, hours, last, mirrored):
    channels, bins, lanes = blocks[0].shape
    first = before is None
    acc = (bins // 2 * 2 * PITCH, lanes)
    rows = 2 * channels * channels
    wide = pltpu.VMEM(
        ((len(blocks) * channels + PITCH - channels) * (bins + SKEW), lanes), jnp.float32
    )
    vmem = pl.BlockSpec(memory_space=pltpu.VMEM)
    args, specs = [], []
    args += blocks
    specs += [vmem] * len(blocks)
    if not first:
        args.append(before)
        specs.append(vmem)
    if last:
        out_shape = [
            jax.ShapeDtypeStruct((ROUNDS + 1, rows, lanes), jnp.float32),
            *[jax.ShapeDtypeStruct((rows, lanes), jnp.bfloat16)] * ROUNDS,
        ]
        out_specs = [vmem] * (ROUNDS + 1)
        scratch = [
            wide,
            pltpu.VMEM(acc, jnp.float32),
            pltpu.VMEM((ROUNDS, rows, lanes), jnp.float32),
        ]
    else:
        out_shape = jax.ShapeDtypeStruct(acc, jnp.float32)
        out_specs = vmem
        scratch = [wide]
    return pl.pallas_call(
        lambda *refs: pair_hour_kernel(hours, first, last, mirrored, *refs),
        out_shape=out_shape,
        in_specs=specs,
        out_specs=out_specs,
        scratch_shapes=scratch,
        cost_estimate=PAIR_COST,
        compiler_params=pltpu.CompilerParams(vmem_limit_bytes=PAIR_LIMIT),
        name="pair_hour_last" if last else "pair_hour",
    )(*args)


def join_kernel(behind_ref, ahead_ref, *refs):
    from_ahead, from_rear, out_ref = refs[:ROUNDS], refs[ROUNDS : 2 * ROUNDS], refs[-1]
    pairs = out_ref.shape[1]

    def put(slot, value):
        out_ref[slot] = value.reshape(pairs, 2, LANES).astype(jnp.bfloat16)

    put(ROUNDS, behind_ref[0] + ahead_ref[0])
    for d in range(1, ROUNDS + 1):
        put(ROUNDS - d, behind_ref[d] + from_rear[d - 1][...].astype(jnp.float32))
        put(ROUNDS + d, ahead_ref[d] + from_ahead[d - 1][...].astype(jnp.float32))


def join(behind, ahead, from_ahead, from_rear):
    _, rows, lanes = behind.shape
    vmem = pl.BlockSpec(memory_space=pltpu.VMEM)
    return pl.pallas_call(
        join_kernel,
        out_shape=jax.ShapeDtypeStruct((2 * ROUNDS + 1, rows // 2, 2, lanes), jnp.bfloat16),
        in_specs=[vmem] * (2 * ROUNDS + 2),
        out_specs=vmem,
        compiler_params=pltpu.CompilerParams(vmem_limit_bytes=4 * MIB),
        name="join",
    )(behind, ahead, *from_ahead, *from_rear)


LEVEL = 4
DISTANCES = ((3, 1, 2), (1, 3, 2), (3, 2, 1), (1, 2, 3))


def send(value, count, mirrored, *hops):
    levels = count // LEVEL
    pairs = [
        (LEVEL * level + source, LEVEL * ((level + up) % levels) + target)
        for source, target, up in hops
        for level in range(levels)
    ]
    if mirrored:
        pairs = [(count - 1 - source, count - 1 - target) for source, target in pairs]
    return lax.ppermute(value, "sta", pairs)


def shift(value, count, steps):
    pairs = [(source, (source + steps) % count) for source in range(count)]
    return lax.ppermute(value, "sta", pairs)


def fetch_partners(block, count, hour):
    mirrored = hour % 2 == 1
    if count % LEVEL:
        way = -1 if mirrored else 1
        return [shift(block, count, way * steps) for steps in range(1, ROUNDS + 1)]
    far = send(block, count, mirrored, (0, 2, 0), (1, 3, 0), (2, 1, 1), (3, 0, 1))
    near = send(block, count, mirrored, (0, 1, 0), (2, 3, 0), (1, 0, 1), (3, 2, 1))
    other = send(far, count, mirrored, (0, 1, 0), (1, 0, 0), (2, 3, 0), (3, 2, 0))
    return [near, far, other]


def distances_of(mirrored):
    count = lax.axis_size("sta")
    if count % LEVEL:
        return list(range(1, ROUNDS + 1))
    role = lax.rem(lax.axis_index("sta"), LEVEL)
    role = LEVEL - 1 - role if mirrored else role
    chosen = []
    for q in range(ROUNDS):
        away = jnp.int32(DISTANCES[LEVEL - 1][q])
        for r in range(LEVEL - 1):
            away = jnp.where(role == r, DISTANCES[r][q], away)
        chosen.append(away)
    return chosen


def spectra(records, counts, gap_mask):
    channels, _, samples = records.shape
    hours = counts.shape[1]
    bins = samples // 2
    count = lax.axis_size("sta")
    table = fourier_matrix(samples)
    first, rest, valid = whiten_first(records, counts, gap_mask, table)
    whitened = [first] + [whiten_hour(rest, valid, table, hour) for hour in range(1, hours)]
    partners = [fetch_partners(whitened[hour], count, hour) for hour in range(hours)]
    sums = [None, None]
    for hour in range(hours):
        mirrored = hour % 2
        sums[mirrored] = pair_hour(
            [whitened[hour], *partners[hour]],
            sums[mirrored],
            hours,
            hour + 2 >= hours,
            mirrored == 1,
        )
    (behind, *back), (ahead, *forth) = sums
    from_ahead, from_rear = [], []
    for d in range(1, ROUNDS + 1):
        from_ahead.append(shift(back[d - 1], count, -d))
        from_rear.append(shift(forth[d - 1], count, d))
    stacked = join(behind, ahead, from_ahead, from_rear)
    stacked = stacked.reshape(2 * ROUNDS + 1, channels, channels, 2, bins)
    return jnp.transpose(stacked, (0, 3, 1, 2, 4))


def solution(mesh):
    in_specs = (P(("days", "sta"), None, None), P(("days", "sta"), None), P(("days", "sta"), None))
    out_specs = P(None, None, ("days", "sta"), None, None)
    return jax.shard_map(
        spectra, mesh=mesh, in_specs=in_specs, out_specs=out_specs, check_vma=False
    )
```

```python
import math

import jax
import jax.numpy as jnp
import numpy as np
from jax import lax
from jax.experimental import pallas as pl
from jax.experimental.pallas import tpu as pltpu
from jax.sharding import PartitionSpec as P


ROUNDS = 3
LANES = 128
PITCH = 16
SKEW = 8
MIB = 1 << 20
PAIR_LIMIT = 10 * MIB
PAIR_COST = pl.CostEstimate(flops=3_000_000_000, transcendentals=0, bytes_accessed=12_000_000)
WHITEN_COST = pl.CostEstimate(flops=2_000_000_000, transcendentals=0, bytes_accessed=8_000_000)

epsilon = 1e-06

NT = (((1,), (1,)), ((), ()))


def fourier_matrix(samples):
    freq_bins = samples // 2
    times_axis = np.arange(samples, dtype=np.int32)
    bins_axis = np.arange(freq_bins, dtype=np.int32)
    phase_idx = times_axis[:, None] * bins_axis[None, :] % samples
    step = np.float32(2.0 * math.pi / samples)
    angle = step * phase_idx.astype(np.float32)
    half = np.float32(0.5)
    taper = half - half * np.cos(step * (times_axis.astype(np.float32) + half))
    table_re = taper[:, None] * np.cos(angle)
    table_im = -taper[:, None] * np.sin(angle)
    return jnp.asarray(np.concatenate([table_re.T, table_im.T], axis=0).astype(jnp.bfloat16))


def lane_iota(rows):
    return lax.broadcasted_iota(jnp.int32, (rows, LANES), 1)


def validity_rows(hour, seg_hour, counts_ref, gap_ref):
    stations = gap_ref.shape[0]
    per_tile = LANES // seg_hour
    tile = gap_ref[:, pl.ds(hour // per_tile * LANES, LANES)].astype(jnp.float32)
    turned = pltpu.roll(tile, seg_hour, 1)
    lane = lane_iota(stations)
    low = lane < seg_hour
    doubled = jnp.where(low, tile, turned) if hour % per_tile == 0 else jnp.where(low, turned, tile)
    position = jnp.where(low, lane, lane - seg_hour)
    return [
        jnp.where(
            position[station : station + 1] < counts_ref[station, hour],
            doubled[station : station + 1],
            0.0,
        )
        for station in range(stations)
    ]


def whiten_block(records_ref, valid, table_ref, out_ref):
    channels, seg_hour, samples = records_ref.shape
    bins = samples // 2
    row = lax.broadcasted_iota(jnp.int32, (bins, LANES), 0)
    low_side = lane_iota(bins) < seg_hour
    slot = jnp.logical_and(row == 0, jnp.logical_not(low_side))
    table = table_ref[...]
    per_station = channels // len(valid)
    first_half = lane_iota(1) < seg_hour
    for channel in range(0, channels, 2):
        both = jnp.concatenate([records_ref[channel], records_ref[channel + 1]], axis=0)
        spectrum = lax.dot_general(table, both, NT, preferred_element_type=jnp.float32)
        power = jnp.sum(spectrum * spectrum, axis=0, keepdims=True) * (1.0 / samples)
        pair_valid = jnp.where(
            first_half, valid[channel // per_station], valid[(channel + 1) // per_station]
        )
        scaled = spectrum * (lax.rsqrt(power + epsilon) * pair_valid)
        real, imag = scaled[:bins], scaled[bins:]
        one = jnp.where(low_side, real, pltpu.roll(imag, seg_hour, 1))
        two = jnp.where(low_side, pltpu.roll(real, seg_hour, 1), imag)
        for value, at in ((one, channel), (two, channel + 1)):
            value = jnp.where(slot, valid[at // per_station], value)
            out_ref[at] = value.astype(jnp.bfloat16)


def whiten_first_kernel(counts_hbm, records_hbm, gap_hbm, table_hbm, *refs):
    out_ref, rest_ref, valid_ref, table_ref, counts_ref, records_ref, gap_ref, sems = refs
    seg_hour = records_ref.shape[1]
    hours = valid_ref.shape[0]

    def hour_of(hour):
        return records_hbm.at[:, pl.ds(hour * seg_hour, seg_hour), :]

    moves = [
        (counts_hbm, counts_ref),
        (gap_hbm, gap_ref),
        (table_hbm, table_ref),
        (hour_of(0), records_ref),
    ]
    now = len(moves)
    moves += [(hour_of(hour), rest_ref.at[hour - 1]) for hour in range(1, hours)]
    copies = [
        pltpu.make_async_copy(source, target, sems.at[i])
        for i, (source, target) in enumerate(moves)
    ]
    for copy in copies:
        copy.start()
    for copy in copies[:now]:
        copy.wait()
    valid = [validity_rows(hour, seg_hour, counts_ref, gap_ref) for hour in range(hours)]
    for hour in range(1, hours):
        for station, row in enumerate(valid[hour]):
            valid_ref[hour, station : station + 1, :] = row
    whiten_block(records_ref, valid[0], table_ref, out_ref)
    for copy in copies[now:]:
        copy.wait()


def whiten_first(records, counts, gap_mask, table):
    channels, segments, samples = records.shape
    stations, hours = counts.shape
    seg_hour = segments // hours
    hbm = pl.BlockSpec(memory_space=pltpu.HBM)
    vmem = pl.BlockSpec(memory_space=pltpu.VMEM)
    block = (channels, seg_hour, samples)
    return pl.pallas_call(
        whiten_first_kernel,
        out_shape=[
            jax.ShapeDtypeStruct((channels, samples // 2, LANES), jnp.bfloat16),
            jax.ShapeDtypeStruct((hours - 1, *block), records.dtype),
            jax.ShapeDtypeStruct((hours, stations, LANES), jnp.float32),
            jax.ShapeDtypeStruct(table.shape, table.dtype),
        ],
        in_specs=[hbm] * 4,
        out_specs=[vmem] * 4,
        scratch_shapes=[
            pltpu.SMEM(counts.shape, counts.dtype),
            pltpu.VMEM(block, records.dtype),
            pltpu.VMEM(gap_mask.shape, gap_mask.dtype),
            pltpu.SemaphoreType.DMA((hours + 3,)),
        ],
        cost_estimate=WHITEN_COST,
        compiler_params=pltpu.CompilerParams(vmem_limit_bytes=4 * MIB),
        name="whiten_first",
    )(
        *(
            pltpu.with_memory_space_constraint(x, pltpu.HBM)
            for x in (counts, records, gap_mask, table)
        )
    )


def whiten_hour_kernel(hour, rest_ref, valid_ref, table_ref, out_ref):
    valid = [valid_ref[hour, station : station + 1, :] for station in range(valid_ref.shape[1])]
    whiten_block(rest_ref.at[hour - 1], valid, table_ref, out_ref)


def whiten_hour(rest, valid, table, hour):
    _, channels, _, samples = rest.shape
    vmem = pl.BlockSpec(memory_space=pltpu.VMEM)
    return pl.pallas_call(
        lambda *refs: whiten_hour_kernel(hour, *refs),
        out_shape=jax.ShapeDtypeStruct((channels, samples // 2, LANES), jnp.bfloat16),
        in_specs=[vmem] * 3,
        out_specs=vmem,
        cost_estimate=WHITEN_COST,
        compiler_params=pltpu.CompilerParams(vmem_limit_bytes=4 * MIB),
        name="whiten_hour",
    )(rest, valid, table)


def pair_hour_kernel(hours, first, last, mirrored, *refs):
    refs = list(refs)
    blocks = [refs.pop(0) for _ in range(ROUNDS + 1)]
    before_ref = None if first else refs.pop(0)
    channels, bins, _ = blocks[0].shape
    half = LANES // 2
    if last:
        kept_ref, *back_refs, wide_ref, acc_ref, back_f32 = refs
    else:
        acc_ref, wide_ref = refs
    pitch = bins + SKEW
    for q, block in enumerate(blocks):
        for channel in range(channels):
            start = (q * channels + channel) * pitch
            wide_ref[start : start + bins, :] = block[channel].astype(jnp.float32)
    for pad in range(PITCH - channels):
        start = (len(blocks) * channels + pad) * pitch
        wide_ref[start : start + bins, :] = jnp.zeros((bins, LANES), jnp.float32)

    def tile_at(q, k):
        return wide_ref[pl.ds(q * channels * pitch + k, PITCH, stride=pitch), :]

    low = lane_iota(PITCH) < half
    zeroth = [tile_at(q, 0) for q in range(len(blocks))]
    valid = [jnp.where(low, pltpu.roll(t, half, 1), t).astype(jnp.bfloat16) for t in zeroth]
    for q, t in enumerate(zeroth):
        wide_ref[pl.ds(q * channels * pitch, PITCH, stride=pitch), :] = jnp.where(low, t, 0.0)
    joint = 0.5 * lax.dot_general(
        valid[0], jnp.concatenate(valid + valid, axis=0), NT, preferred_element_type=jnp.float32
    )
    weight = 1.0 / (hours * jnp.maximum(joint, 1.0))
    weight = jnp.concatenate([weight, weight], axis=0)
    sign = jnp.where(low, 1.0, -1.0)
    low_product = lane_iota(2 * PITCH) < half
    half_bins = bins // 2

    def step(k, carry):
        left, right = [], []
        for part in range(2):
            tiles = [tile_at(q, k + part * half_bins) for q in range(len(blocks))]
            turned = pltpu.roll(tiles[0], half, 1) * sign
            tiles = [t.astype(jnp.bfloat16) for t in tiles]
            left += [tiles[0], turned.astype(jnp.bfloat16)]
            right += tiles
        product = lax.dot_general(
            jnp.concatenate(left, axis=0),
            jnp.concatenate(right, axis=0),
            NT,
            preferred_element_type=jnp.float32,
        )
        product = weight * jnp.where(low_product, product[: 2 * PITCH], product[2 * PITCH :])
        place = pl.ds(pl.multiple_of(k * 2 * PITCH, 2 * PITCH), 2 * PITCH)
        if not first:
            product = product + before_ref[place, :]
        acc_ref[place, :] = product
        return carry

    lax.fori_loop(0, half_bins, step, 0, unroll=half_bins)
    if not last:
        return
    low_half = lane_iota(half) < half
    distances = distances_of(mirrored)

    def finish(a, carry):
        both = jnp.concatenate(
            [
                acc_ref[pl.ds(part * PITCH + a, half_bins, stride=2 * PITCH), :]
                for part in range(2)
            ],
            axis=0,
        )
        by_bin = both.T
        upper, lower = by_bin[:half], by_bin[half:]
        real = jnp.where(low_half, upper, pltpu.roll(lower, half, 1))
        imag = jnp.where(low_half, pltpu.roll(upper, half, 1), lower)
        for part, value in enumerate((real, imag)):
            for q in range(len(blocks)):
                rows = value[q * PITCH : q * PITCH + channels]
                place = pl.ds(a * 2 * channels + part, channels, stride=2)
                if q:
                    kept_ref[distances[q - 1], place, :] = rows
                    back_f32[q - 1, pl.ds(2 * a + part, channels, stride=2 * channels), :] = (
                        -rows if part else rows
                    )
                else:
                    kept_ref[0, place, :] = rows
        return carry

    lax.fori_loop(0, channels, finish, 0, unroll=12)
    for q in range(ROUNDS):
        for d in range(ROUNDS):

            @pl.when(distances[q] == d + 1)
            def _():
                back_refs[d][...] = back_f32[q].astype(jnp.bfloat16)


def pair_hour(blocks, before, hours, last, mirrored):
    channels, bins, lanes = blocks[0].shape
    first = before is None
    acc = (bins // 2 * 2 * PITCH, lanes)
    rows = 2 * channels * channels
    wide = pltpu.VMEM(
        ((len(blocks) * channels + PITCH - channels) * (bins + SKEW), lanes), jnp.float32
    )
    vmem = pl.BlockSpec(memory_space=pltpu.VMEM)
    args, specs = [], []
    args += blocks
    specs += [vmem] * len(blocks)
    if not first:
        args.append(before)
        specs.append(vmem)
    if last:
        out_shape = [
            jax.ShapeDtypeStruct((ROUNDS + 1, rows, lanes), jnp.float32),
            *[jax.ShapeDtypeStruct((rows, lanes), jnp.bfloat16)] * ROUNDS,
        ]
        out_specs = [vmem] * (ROUNDS + 1)
        scratch = [
            wide,
            pltpu.VMEM(acc, jnp.float32),
            pltpu.VMEM((ROUNDS, rows, lanes), jnp.float32),
        ]
    else:
        out_shape = jax.ShapeDtypeStruct(acc, jnp.float32)
        out_specs = vmem
        scratch = [wide]
    return pl.pallas_call(
        lambda *refs: pair_hour_kernel(hours, first, last, mirrored, *refs),
        out_shape=out_shape,
        in_specs=specs,
        out_specs=out_specs,
        scratch_shapes=scratch,
        cost_estimate=PAIR_COST,
        compiler_params=pltpu.CompilerParams(vmem_limit_bytes=PAIR_LIMIT),
        name="pair_hour_last" if last else "pair_hour",
    )(*args)


def join_kernel(behind_ref, ahead_ref, *refs):
    from_ahead, from_rear, out_ref = refs[:ROUNDS], refs[ROUNDS : 2 * ROUNDS], refs[-1]
    pairs = out_ref.shape[1]

    def put(slot, value):
        out_ref[slot] = value.reshape(pairs, 2, LANES).astype(jnp.bfloat16)

    put(ROUNDS, behind_ref[0] + ahead_ref[0])
    for d in range(1, ROUNDS + 1):
        put(ROUNDS - d, behind_ref[d] + from_rear[d - 1][...].astype(jnp.float32))
        put(ROUNDS + d, ahead_ref[d] + from_ahead[d - 1][...].astype(jnp.float32))


def join(behind, ahead, from_ahead, from_rear):
    _, rows, lanes = behind.shape
    vmem = pl.BlockSpec(memory_space=pltpu.VMEM)
    return pl.pallas_call(
        join_kernel,
        out_shape=jax.ShapeDtypeStruct((2 * ROUNDS + 1, rows // 2, 2, lanes), jnp.bfloat16),
        in_specs=[vmem] * (2 * ROUNDS + 2),
        out_specs=vmem,
        compiler_params=pltpu.CompilerParams(vmem_limit_bytes=4 * MIB),
        name="join",
    )(behind, ahead, *from_ahead, *from_rear)


LEVEL = 4
DISTANCES = ((3, 1, 2), (1, 3, 2), (3, 2, 1), (1, 2, 3))


def send(value, count, mirrored, *hops):
    levels = count // LEVEL
    pairs = [
        (LEVEL * level + source, LEVEL * ((level + up) % levels) + target)
        for source, target, up in hops
        for level in range(levels)
    ]
    if mirrored:
        pairs = [(count - 1 - source, count - 1 - target) for source, target in pairs]
    return lax.ppermute(value, "sta", pairs)


def shift(value, count, steps):
    pairs = [(source, (source + steps) % count) for source in range(count)]
    return lax.ppermute(value, "sta", pairs)


def fetch_partners(block, count, hour):
    mirrored = hour % 2 == 1
    if count % LEVEL:
        way = -1 if mirrored else 1
        return [shift(block, count, way * steps) for steps in range(1, ROUNDS + 1)]
    far = send(block, count, mirrored, (0, 2, 0), (1, 3, 0), (2, 1, 1), (3, 0, 1))
    near = send(block, count, mirrored, (0, 1, 0), (2, 3, 0), (1, 0, 1), (3, 2, 1))
    other = send(far, count, mirrored, (0, 1, 0), (1, 0, 0), (2, 3, 0), (3, 2, 0))
    return [near, far, other]


def distances_of(mirrored):
    count = lax.axis_size("sta")
    if count % LEVEL:
        return list(range(1, ROUNDS + 1))
    role = lax.rem(lax.axis_index("sta"), LEVEL)
    role = LEVEL - 1 - role if mirrored else role
    chosen = []
    for q in range(ROUNDS):
        away = jnp.int32(DISTANCES[LEVEL - 1][q])
        for r in range(LEVEL - 1):
            away = jnp.where(role == r, DISTANCES[r][q], away)
        chosen.append(away)
    return chosen


def spectra(records, counts, gap_mask):
    channels, _, samples = records.shape
    hours = counts.shape[1]
    bins = samples // 2
    count = lax.axis_size("sta")
    table = fourier_matrix(samples)
    first, rest, valid, table = whiten_first(records, counts, gap_mask, table)
    whitened = [first] + [whiten_hour(rest, valid, table, hour) for hour in range(1, hours)]
    partners = [fetch_partners(whitened[hour], count, hour) for hour in range(hours)]
    sums = [None, None]
    for hour in range(hours):
        mirrored = hour % 2
        sums[mirrored] = pair_hour(
            [whitened[hour], *partners[hour]],
            sums[mirrored],
            hours,
            hour + 2 >= hours,
            mirrored == 1,
        )
    (behind, *back), (ahead, *forth) = sums
    from_ahead, from_rear = [], []
    for d in range(1, ROUNDS + 1):
        from_ahead.append(shift(back[d - 1], count, -d))
        from_rear.append(shift(forth[d - 1], count, d))
    stacked = join(behind, ahead, from_ahead, from_rear)
    stacked = stacked.reshape(2 * ROUNDS + 1, channels, channels, 2, bins)
    return jnp.transpose(stacked, (0, 3, 1, 2, 4))


def solution(mesh):
    in_specs = (P(("days", "sta"), None, None), P(("days", "sta"), None), P(("days", "sta"), None))
    out_specs = P(None, None, ("days", "sta"), None, None)
    return jax.shard_map(
        spectra, mesh=mesh, in_specs=in_specs, out_specs=out_specs, check_vma=False
    )
```

```python
import math

import jax
import jax.numpy as jnp
import numpy as np
from jax import lax
from jax.experimental import pallas as pl
from jax.experimental.pallas import tpu as pltpu
from jax.sharding import PartitionSpec as P


ROUNDS = 3
LANES = 128
PITCH = 16
SKEW = 8
MIB = 1 << 20
PAIR_LIMIT = 10 * MIB
PAIR_COST = pl.CostEstimate(flops=3_000_000_000, transcendentals=0, bytes_accessed=12_000_000)
WHITEN_COST = pl.CostEstimate(flops=2_000_000_000, transcendentals=0, bytes_accessed=8_000_000)

epsilon = 1e-06

NT = (((1,), (1,)), ((), ()))


def fourier_matrix(samples):
    freq_bins = samples // 2
    times_axis = np.arange(samples, dtype=np.int32)
    bins_axis = np.arange(freq_bins, dtype=np.int32)
    phase_idx = times_axis[:, None] * bins_axis[None, :] % samples
    step = np.float32(2.0 * math.pi / samples)
    angle = step * phase_idx.astype(np.float32)
    half = np.float32(0.5)
    taper = half - half * np.cos(step * (times_axis.astype(np.float32) + half))
    table_re = taper[:, None] * np.cos(angle)
    table_im = -taper[:, None] * np.sin(angle)
    return jnp.asarray(np.concatenate([table_re.T, table_im.T], axis=0).astype(jnp.bfloat16))


def lane_iota(rows):
    return lax.broadcasted_iota(jnp.int32, (rows, LANES), 1)


def validity_rows(hour, seg_hour, counts_ref, gap_ref):
    stations = gap_ref.shape[0]
    per_tile = LANES // seg_hour
    tile = gap_ref[:, pl.ds(hour // per_tile * LANES, LANES)].astype(jnp.float32)
    turned = pltpu.roll(tile, seg_hour, 1)
    lane = lane_iota(stations)
    low = lane < seg_hour
    doubled = jnp.where(low, tile, turned) if hour % per_tile == 0 else jnp.where(low, turned, tile)
    position = jnp.where(low, lane, lane - seg_hour)
    return [
        jnp.where(
            position[station : station + 1] < counts_ref[station, hour],
            doubled[station : station + 1],
            0.0,
        )
        for station in range(stations)
    ]


def whiten_block(records_ref, valid, table_ref, out_ref):
    channels, seg_hour, samples = records_ref.shape
    bins = samples // 2
    row = lax.broadcasted_iota(jnp.int32, (bins, LANES), 0)
    low_side = lane_iota(bins) < seg_hour
    slot = jnp.logical_and(row == 0, jnp.logical_not(low_side))
    table = table_ref[...]
    per_station = channels // len(valid)
    first_half = lane_iota(1) < seg_hour
    for channel in range(0, channels, 2):
        both = jnp.concatenate([records_ref[channel], records_ref[channel + 1]], axis=0)
        spectrum = lax.dot_general(table, both, NT, preferred_element_type=jnp.float32)
        power = jnp.sum(spectrum * spectrum, axis=0, keepdims=True) * (1.0 / samples)
        pair_valid = jnp.where(
            first_half, valid[channel // per_station], valid[(channel + 1) // per_station]
        )
        scaled = spectrum * (lax.rsqrt(power + epsilon) * pair_valid)
        real, imag = scaled[:bins], scaled[bins:]
        one = jnp.where(low_side, real, pltpu.roll(imag, seg_hour, 1))
        two = jnp.where(low_side, pltpu.roll(real, seg_hour, 1), imag)
        for value, at in ((one, channel), (two, channel + 1)):
            value = jnp.where(slot, valid[at // per_station], value)
            out_ref[at] = value.astype(jnp.bfloat16)


def whiten_first_kernel(counts_hbm, records_hbm, gap_hbm, table_hbm, *refs):
    out_ref, rest_ref, valid_ref, table_ref, counts_ref, records_ref, gap_ref, sems = refs
    seg_hour = records_ref.shape[1]
    hours = valid_ref.shape[0]

    def hour_of(hour):
        return records_hbm.at[:, pl.ds(hour * seg_hour, seg_hour), :]

    moves = [
        (counts_hbm, counts_ref),
        (gap_hbm, gap_ref),
        (table_hbm, table_ref),
        (hour_of(0), records_ref),
    ]
    now = len(moves)
    moves += [(hour_of(hour), rest_ref.at[hour - 1]) for hour in range(1, hours)]
    copies = [
        pltpu.make_async_copy(source, target, sems.at[i])
        for i, (source, target) in enumerate(moves)
    ]
    for copy in copies:
        copy.start()
    for copy in copies[:now]:
        copy.wait()
    valid = [validity_rows(hour, seg_hour, counts_ref, gap_ref) for hour in range(hours)]
    for hour in range(1, hours):
        for station, row in enumerate(valid[hour]):
            valid_ref[hour, station : station + 1, :] = row
    whiten_block(records_ref, valid[0], table_ref, out_ref)
    for copy in copies[now:]:
        copy.wait()


def whiten_first(records, counts, gap_mask, table):
    channels, segments, samples = records.shape
    stations, hours = counts.shape
    seg_hour = segments // hours
    hbm = pl.BlockSpec(memory_space=pltpu.HBM)
    vmem = pl.BlockSpec(memory_space=pltpu.VMEM)
    block = (channels, seg_hour, samples)
    return pl.pallas_call(
        whiten_first_kernel,
        out_shape=[
            jax.ShapeDtypeStruct((channels, samples // 2, LANES), jnp.bfloat16),
            jax.ShapeDtypeStruct((hours - 1, *block), records.dtype),
            jax.ShapeDtypeStruct((hours, stations, LANES), jnp.float32),
            jax.ShapeDtypeStruct(table.shape, table.dtype),
        ],
        in_specs=[hbm] * 4,
        out_specs=[vmem] * 4,
        scratch_shapes=[
            pltpu.SMEM(counts.shape, counts.dtype),
            pltpu.VMEM(block, records.dtype),
            pltpu.VMEM(gap_mask.shape, gap_mask.dtype),
            pltpu.SemaphoreType.DMA((hours + 3,)),
        ],
        cost_estimate=WHITEN_COST,
        compiler_params=pltpu.CompilerParams(vmem_limit_bytes=4 * MIB),
        name="whiten_first",
    )(
        *(
            pltpu.with_memory_space_constraint(x, pltpu.HBM)
            for x in (counts, records, gap_mask, table)
        )
    )


def whiten_hour_kernel(hour, rest_ref, valid_ref, table_ref, out_ref):
    valid = [valid_ref[hour, station : station + 1, :] for station in range(valid_ref.shape[1])]
    whiten_block(rest_ref.at[hour - 1], valid, table_ref, out_ref)


def whiten_hour(rest, valid, table, hour):
    _, channels, _, samples = rest.shape
    vmem = pl.BlockSpec(memory_space=pltpu.VMEM)
    return pl.pallas_call(
        lambda *refs: whiten_hour_kernel(hour, *refs),
        out_shape=jax.ShapeDtypeStruct((channels, samples // 2, LANES), jnp.bfloat16),
        in_specs=[vmem] * 3,
        out_specs=vmem,
        cost_estimate=WHITEN_COST,
        compiler_params=pltpu.CompilerParams(vmem_limit_bytes=4 * MIB),
        name="whiten_hour",
    )(rest, valid, table)


def pair_hour_kernel(hours, first, last, mirrored, *refs):
    refs = list(refs)
    blocks = [refs.pop(0) for _ in range(ROUNDS + 1)]
    before_ref = None if first else refs.pop(0)
    channels, bins, _ = blocks[0].shape
    half = LANES // 2
    if last:
        kept_ref, *back_refs, wide_ref, acc_ref, back_f32 = refs
    else:
        acc_ref, wide_ref = refs
    pitch = bins + SKEW
    for q, block in enumerate(blocks):
        for channel in range(channels):
            start = (q * channels + channel) * pitch
            wide_ref[start : start + bins, :] = block[channel].astype(jnp.float32)
    for pad in range(PITCH - channels):
        start = (len(blocks) * channels + pad) * pitch
        wide_ref[start : start + bins, :] = jnp.zeros((bins, LANES), jnp.float32)

    def tile_at(q, k):
        return wide_ref[pl.ds(q * channels * pitch + k, PITCH, stride=pitch), :]

    low = lane_iota(PITCH) < half
    zeroth = [tile_at(q, 0) for q in range(len(blocks))]
    valid = [jnp.where(low, pltpu.roll(t, half, 1), t).astype(jnp.bfloat16) for t in zeroth]
    for q, t in enumerate(zeroth):
        wide_ref[pl.ds(q * channels * pitch, PITCH, stride=pitch), :] = jnp.where(low, t, 0.0)
    joint = 0.5 * lax.dot_general(
        valid[0], jnp.concatenate(valid + valid, axis=0), NT, preferred_element_type=jnp.float32
    )
    weight = 1.0 / (hours * jnp.maximum(joint, 1.0))
    weight = jnp.concatenate([weight, weight], axis=0)
    sign = jnp.where(low, 1.0, -1.0)
    low_product = lane_iota(2 * PITCH) < half
    half_bins = bins // 2

    def step(k, carry):
        left, right = [], []
        for part in range(2):
            tiles = [tile_at(q, k + part * half_bins) for q in range(len(blocks))]
            turned = pltpu.roll(tiles[0], half, 1) * sign
            tiles = [t.astype(jnp.bfloat16) for t in tiles]
            left += [tiles[0], turned.astype(jnp.bfloat16)]
            right += tiles
        product = lax.dot_general(
            jnp.concatenate(left, axis=0),
            jnp.concatenate(right, axis=0),
            NT,
            preferred_element_type=jnp.float32,
        )
        product = weight * jnp.where(low_product, product[: 2 * PITCH], product[2 * PITCH :])
        place = pl.ds(pl.multiple_of(k * 2 * PITCH, 2 * PITCH), 2 * PITCH)
        if not first:
            product = product + before_ref[place, :]
        acc_ref[place, :] = product
        return carry

    lax.fori_loop(0, half_bins, step, 0, unroll=half_bins)
    if not last:
        return
    low_half = lane_iota(half) < half
    distances = distances_of(mirrored)

    def finish(a, carry):
        both = jnp.concatenate(
            [
                acc_ref[pl.ds(part * PITCH + a, half_bins, stride=2 * PITCH), :]
                for part in range(2)
            ],
            axis=0,
        )
        by_bin = both.T
        upper, lower = by_bin[:half], by_bin[half:]
        real = jnp.where(low_half, upper, pltpu.roll(lower, half, 1))
        imag = jnp.where(low_half, pltpu.roll(upper, half, 1), lower)
        for part, value in enumerate((real, imag)):
            for q in range(len(blocks)):
                rows = value[q * PITCH : q * PITCH + channels]
                place = pl.ds(a * 2 * channels + part, channels, stride=2)
                if q:
                    kept_ref[distances[q - 1], place, :] = rows
                    back_f32[q - 1, pl.ds(2 * a + part, channels, stride=2 * channels), :] = (
                        -rows if part else rows
                    )
                else:
                    kept_ref[0, place, :] = rows
        return carry

    lax.fori_loop(0, channels, finish, 0, unroll=12)
    for q in range(ROUNDS):
        for d in range(ROUNDS):

            @pl.when(distances[q] == d + 1)
            def _():
                back_refs[d][...] = back_f32[q].astype(jnp.bfloat16)


def pair_hour(blocks, before, hours, last, mirrored):
    channels, bins, lanes = blocks[0].shape
    first = before is None
    acc = (bins // 2 * 2 * PITCH, lanes)
    rows = 2 * channels * channels
    wide = pltpu.VMEM(
        ((len(blocks) * channels + PITCH - channels) * (bins + SKEW), lanes), jnp.float32
    )
    vmem = pl.BlockSpec(memory_space=pltpu.VMEM)
    args, specs = [], []
    args += blocks
    specs += [vmem] * len(blocks)
    if not first:
        args.append(before)
        specs.append(vmem)
    if last:
        out_shape = [
            jax.ShapeDtypeStruct((ROUNDS + 1, rows, lanes), jnp.float32),
            *[jax.ShapeDtypeStruct((rows, lanes), jnp.bfloat16)] * ROUNDS,
        ]
        out_specs = [vmem] * (ROUNDS + 1)
        scratch = [
            wide,
            pltpu.VMEM(acc, jnp.float32),
            pltpu.VMEM((ROUNDS, rows, lanes), jnp.float32),
        ]
    else:
        out_shape = jax.ShapeDtypeStruct(acc, jnp.float32)
        out_specs = vmem
        scratch = [wide]
    return pl.pallas_call(
        lambda *refs: pair_hour_kernel(hours, first, last, mirrored, *refs),
        out_shape=out_shape,
        in_specs=specs,
        out_specs=out_specs,
        scratch_shapes=scratch,
        cost_estimate=PAIR_COST,
        compiler_params=pltpu.CompilerParams(vmem_limit_bytes=PAIR_LIMIT),
        name="pair_hour_last" if last else "pair_hour",
    )(*args)


def put(out_ref, slot, value):
    out_ref[slot] = value.reshape(out_ref.shape[1], 2, LANES).astype(jnp.bfloat16)


def join_below_kernel(behind_ref, ahead_ref, *refs):
    from_rear, out_ref = refs[:ROUNDS], refs[-1]
    put(out_ref, ROUNDS, behind_ref[0] + ahead_ref[0])
    for d in range(1, ROUNDS + 1):
        put(out_ref, ROUNDS - d, behind_ref[d] + from_rear[d - 1][...].astype(jnp.float32))


def join_above_kernel(ahead_ref, *refs):
    from_ahead, out_ref = refs[:ROUNDS], refs[-1]
    for d in range(1, ROUNDS + 1):
        put(out_ref, d - 1, ahead_ref[d] + from_ahead[d - 1][...].astype(jnp.float32))


def join(behind, ahead, from_ahead, from_rear):
    _, rows, lanes = behind.shape
    vmem = pl.BlockSpec(memory_space=pltpu.VMEM)
    out = jax.ShapeDtypeStruct((2 * ROUNDS + 1, rows // 2, 2, lanes), jnp.bfloat16)
    half = (ROUNDS + 1, rows // 2, 2, lanes)
    params = pltpu.CompilerParams(vmem_limit_bytes=4 * MIB)
    below = pl.pallas_call(
        join_below_kernel,
        grid=(1,),
        out_shape=out,
        in_specs=[vmem] * (ROUNDS + 2),
        out_specs=pl.BlockSpec(half, lambda i: (0, 0, 0, 0)),
        compiler_params=params,
        name="join_below",
    )(behind, ahead, *from_rear)
    return pl.pallas_call(
        join_above_kernel,
        grid=(1,),
        out_shape=out,
        in_specs=[vmem] * (ROUNDS + 1) + [pl.BlockSpec(memory_space=pl.ANY)],
        out_specs=pl.BlockSpec(half, lambda i: (1, 0, 0, 0)),
        input_output_aliases={ROUNDS + 1: 0},
        compiler_params=params,
        name="join_above",
    )(ahead, *from_ahead, below)


LEVEL = 4
DISTANCES = ((3, 1, 2), (1, 3, 2), (3, 2, 1), (1, 2, 3))


def send(value, count, mirrored, *hops):
    levels = count // LEVEL
    pairs = [
        (LEVEL * level + source, LEVEL * ((level + up) % levels) + target)
        for source, target, up in hops
        for level in range(levels)
    ]
    if mirrored:
        pairs = [(count - 1 - source, count - 1 - target) for source, target in pairs]
    return lax.ppermute(value, "sta", pairs)


def shift(value, count, steps):
    pairs = [(source, (source + steps) % count) for source in range(count)]
    return lax.ppermute(value, "sta", pairs)


def pick_kernel(role, far_ref, relayed_ref, out_ref):
    mine = lax.rem(lax.axis_index("sta"), LEVEL) == role

    @pl.when(mine)
    def _():
        out_ref[...] = relayed_ref[...]

    @pl.when(jnp.logical_not(mine))
    def _():
        out_ref[...] = far_ref[...]


def pick(far, relayed, role):
    vmem = pl.BlockSpec(memory_space=pltpu.VMEM)
    return pl.pallas_call(
        lambda *refs: pick_kernel(role, *refs),
        out_shape=jax.ShapeDtypeStruct(far.shape, far.dtype),
        in_specs=[vmem, vmem],
        out_specs=vmem,
        compiler_params=pltpu.CompilerParams(vmem_limit_bytes=4 * MIB),
        name="pick",
    )(far, relayed)


def fetch_partners(block, count, hour):
    mirrored = hour % 2 == 1
    if count % LEVEL:
        way = -1 if mirrored else 1
        return [shift(block, count, way * steps) for steps in range(1, ROUNDS + 1)]
    near = send(block, count, mirrored, (0, 1, 0), (2, 3, 0), (1, 0, 1), (3, 2, 1))
    far = send(block, count, mirrored, (0, 2, 0), (1, 3, 0), (2, 1, 1))
    relayed = send(near, count, mirrored, (2, 0, 0))
    far = pick(far, relayed, LEVEL - 1 if mirrored else 0)
    other = send(far, count, mirrored, (0, 1, 0), (1, 0, 0), (2, 3, 0), (3, 2, 0))
    return [near, far, other]


def distances_of(mirrored):
    count = lax.axis_size("sta")
    if count % LEVEL:
        return list(range(1, ROUNDS + 1))
    role = lax.rem(lax.axis_index("sta"), LEVEL)
    role = LEVEL - 1 - role if mirrored else role
    chosen = []
    for q in range(ROUNDS):
        away = jnp.int32(DISTANCES[LEVEL - 1][q])
        for r in range(LEVEL - 1):
            away = jnp.where(role == r, DISTANCES[r][q], away)
        chosen.append(away)
    return chosen


def spectra(records, counts, gap_mask):
    channels, _, samples = records.shape
    hours = counts.shape[1]
    bins = samples // 2
    count = lax.axis_size("sta")
    table = fourier_matrix(samples)
    first, rest, valid, table = whiten_first(records, counts, gap_mask, table)
    whitened = [first] + [whiten_hour(rest, valid, table, hour) for hour in range(1, hours)]
    partners = [fetch_partners(whitened[hour], count, hour) for hour in range(hours)]
    sums = [None, None]
    for hour in range(hours):
        mirrored = hour % 2
        sums[mirrored] = pair_hour(
            [whitened[hour], *partners[hour]],
            sums[mirrored],
            hours,
            hour + 2 >= hours,
            mirrored == 1,
        )
    (behind, *back), (ahead, *forth) = sums
    from_ahead, from_rear = [], []
    for d in range(1, ROUNDS + 1):
        from_ahead.append(shift(back[d - 1], count, -d))
        from_rear.append(shift(forth[d - 1], count, d))
    stacked = join(behind, ahead, from_ahead, from_rear)
    stacked = stacked.reshape(2 * ROUNDS + 1, channels, channels, 2, bins)
    return jnp.transpose(stacked, (0, 3, 1, 2, 4))


def solution(mesh):
    in_specs = (P(("days", "sta"), None, None), P(("days", "sta"), None), P(("days", "sta"), None))
    out_specs = P(None, None, ("days", "sta"), None, None)
    return jax.shard_map(
        spectra, mesh=mesh, in_specs=in_specs, out_specs=out_specs, check_vma=False
    )
```

```python
import math

import jax
import jax.numpy as jnp
import numpy as np
from jax import lax
from jax.experimental import pallas as pl
from jax.experimental.pallas import tpu as pltpu
from jax.sharding import PartitionSpec as P


ROUNDS = 3
LANES = 128
PITCH = 16
SKEW = 8
MIB = 1 << 20
PAIR_LIMIT = 10 * MIB
PAIR_COST = pl.CostEstimate(flops=3_000_000_000, transcendentals=0, bytes_accessed=12_000_000)
WHITEN_COST = pl.CostEstimate(flops=2_000_000_000, transcendentals=0, bytes_accessed=8_000_000)

epsilon = 1e-06

NT = (((1,), (1,)), ((), ()))


def fourier_matrix(samples):
    freq_bins = samples // 2
    times_axis = np.arange(samples, dtype=np.int32)
    bins_axis = np.arange(freq_bins, dtype=np.int32)
    phase_idx = times_axis[:, None] * bins_axis[None, :] % samples
    step = np.float32(2.0 * math.pi / samples)
    angle = step * phase_idx.astype(np.float32)
    half = np.float32(0.5)
    taper = half - half * np.cos(step * (times_axis.astype(np.float32) + half))
    table_re = taper[:, None] * np.cos(angle)
    table_im = -taper[:, None] * np.sin(angle)
    return jnp.asarray(np.concatenate([table_re.T, table_im.T], axis=0).astype(jnp.bfloat16))


def lane_iota(rows):
    return lax.broadcasted_iota(jnp.int32, (rows, LANES), 1)


def validity_rows(hour, seg_hour, counts_ref, gap_ref):
    stations = gap_ref.shape[0]
    per_tile = LANES // seg_hour
    tile = gap_ref[:, pl.ds(hour // per_tile * LANES, LANES)].astype(jnp.float32)
    turned = pltpu.roll(tile, seg_hour, 1)
    lane = lane_iota(stations)
    low = lane < seg_hour
    doubled = jnp.where(low, tile, turned) if hour % per_tile == 0 else jnp.where(low, turned, tile)
    position = jnp.where(low, lane, lane - seg_hour)
    return [
        jnp.where(
            position[station : station + 1] < counts_ref[station, hour],
            doubled[station : station + 1],
            0.0,
        )
        for station in range(stations)
    ]


def whiten_block(records_ref, valid, table_ref, out_ref):
    channels, seg_hour, samples = records_ref.shape
    bins = samples // 2
    row = lax.broadcasted_iota(jnp.int32, (bins, LANES), 0)
    low_side = lane_iota(bins) < seg_hour
    slot = jnp.logical_and(row == 0, jnp.logical_not(low_side))
    table = table_ref[...]
    per_station = channels // len(valid)
    first_half = lane_iota(1) < seg_hour
    for channel in range(0, channels, 2):
        both = jnp.concatenate([records_ref[channel], records_ref[channel + 1]], axis=0)
        spectrum = lax.dot_general(table, both, NT, preferred_element_type=jnp.float32)
        power = jnp.sum(spectrum * spectrum, axis=0, keepdims=True) * (1.0 / samples)
        pair_valid = jnp.where(
            first_half, valid[channel // per_station], valid[(channel + 1) // per_station]
        )
        scaled = spectrum * (lax.rsqrt(power + epsilon) * pair_valid)
        real, imag = scaled[:bins], scaled[bins:]
        one = jnp.where(low_side, real, pltpu.roll(imag, seg_hour, 1))
        two = jnp.where(low_side, pltpu.roll(real, seg_hour, 1), imag)
        for value, at in ((one, channel), (two, channel + 1)):
            value = jnp.where(slot, valid[at // per_station], value)
            out_ref[at] = value.astype(jnp.bfloat16)


def whiten_first_kernel(counts_hbm, records_hbm, gap_hbm, table_hbm, *refs):
    out_ref, rest_ref, valid_ref, table_ref, counts_ref, records_ref, gap_ref, sems = refs
    seg_hour = records_ref.shape[1]
    hours = valid_ref.shape[0]

    def hour_of(hour):
        return records_hbm.at[:, pl.ds(hour * seg_hour, seg_hour), :]

    moves = [
        (counts_hbm, counts_ref),
        (gap_hbm, gap_ref),
        (table_hbm, table_ref),
        (hour_of(0), records_ref),
    ]
    now = len(moves)
    moves += [(hour_of(hour), rest_ref.at[hour - 1]) for hour in range(1, hours)]
    copies = [
        pltpu.make_async_copy(source, target, sems.at[i])
        for i, (source, target) in enumerate(moves)
    ]
    for copy in copies[:now]:
        copy.start()
    for copy in copies[:now]:
        copy.wait()
    for copy in copies[now:]:
        copy.start()
    valid = [validity_rows(hour, seg_hour, counts_ref, gap_ref) for hour in range(hours)]
    for hour in range(1, hours):
        for station, row in enumerate(valid[hour]):
            valid_ref[hour, station : station + 1, :] = row
    whiten_block(records_ref, valid[0], table_ref, out_ref)
    for copy in copies[now:]:
        copy.wait()


def whiten_first(records, counts, gap_mask, table):
    channels, segments, samples = records.shape
    stations, hours = counts.shape
    seg_hour = segments // hours
    hbm = pl.BlockSpec(memory_space=pltpu.HBM)
    vmem = pl.BlockSpec(memory_space=pltpu.VMEM)
    block = (channels, seg_hour, samples)
    return pl.pallas_call(
        whiten_first_kernel,
        out_shape=[
            jax.ShapeDtypeStruct((channels, samples // 2, LANES), jnp.bfloat16),
            jax.ShapeDtypeStruct((hours - 1, *block), records.dtype),
            jax.ShapeDtypeStruct((hours, stations, LANES), jnp.float32),
            jax.ShapeDtypeStruct(table.shape, table.dtype),
        ],
        in_specs=[hbm] * 4,
        out_specs=[vmem] * 4,
        scratch_shapes=[
            pltpu.SMEM(counts.shape, counts.dtype),
            pltpu.VMEM(block, records.dtype),
            pltpu.VMEM(gap_mask.shape, gap_mask.dtype),
            pltpu.SemaphoreType.DMA((hours + 3,)),
        ],
        cost_estimate=WHITEN_COST,
        compiler_params=pltpu.CompilerParams(vmem_limit_bytes=4 * MIB),
        name="whiten_first",
    )(
        *(
            pltpu.with_memory_space_constraint(x, pltpu.HBM)
            for x in (counts, records, gap_mask, table)
        )
    )


def whiten_hour_kernel(hour, rest_ref, valid_ref, table_ref, out_ref):
    valid = [valid_ref[hour, station : station + 1, :] for station in range(valid_ref.shape[1])]
    whiten_block(rest_ref.at[hour - 1], valid, table_ref, out_ref)


def whiten_hour(rest, valid, table, hour):
    _, channels, _, samples = rest.shape
    vmem = pl.BlockSpec(memory_space=pltpu.VMEM)
    return pl.pallas_call(
        lambda *refs: whiten_hour_kernel(hour, *refs),
        out_shape=jax.ShapeDtypeStruct((channels, samples // 2, LANES), jnp.bfloat16),
        in_specs=[vmem] * 3,
        out_specs=vmem,
        cost_estimate=WHITEN_COST,
        compiler_params=pltpu.CompilerParams(vmem_limit_bytes=4 * MIB),
        name="whiten_hour",
    )(rest, valid, table)


def pair_hour_kernel(hours, first, last, mirrored, *refs):
    refs = list(refs)
    blocks = [refs.pop(0) for _ in range(ROUNDS + 1)]
    before_ref = None if first else refs.pop(0)
    channels, bins, _ = blocks[0].shape
    half = LANES // 2
    if last:
        kept_ref, *back_refs, wide_ref, acc_ref, back_f32 = refs
    else:
        acc_ref, wide_ref = refs
    pitch = bins + SKEW
    for q, block in enumerate(blocks):
        for channel in range(channels):
            start = (q * channels + channel) * pitch
            wide_ref[start : start + bins, :] = block[channel].astype(jnp.float32)
    for pad in range(PITCH - channels):
        start = (len(blocks) * channels + pad) * pitch
        wide_ref[start : start + bins, :] = jnp.zeros((bins, LANES), jnp.float32)

    def tile_at(q, k):
        return wide_ref[pl.ds(q * channels * pitch + k, PITCH, stride=pitch), :]

    low = lane_iota(PITCH) < half
    zeroth = [tile_at(q, 0) for q in range(len(blocks))]
    valid = [jnp.where(low, pltpu.roll(t, half, 1), t).astype(jnp.bfloat16) for t in zeroth]
    for q, t in enumerate(zeroth):
        wide_ref[pl.ds(q * channels * pitch, PITCH, stride=pitch), :] = jnp.where(low, t, 0.0)
    joint = 0.5 * lax.dot_general(
        valid[0], jnp.concatenate(valid + valid, axis=0), NT, preferred_element_type=jnp.float32
    )
    weight = 1.0 / (hours * jnp.maximum(joint, 1.0))
    weight = jnp.concatenate([weight, weight], axis=0)
    sign = jnp.where(low, 1.0, -1.0)
    low_product = lane_iota(2 * PITCH) < half
    half_bins = bins // 2

    def step(k, carry):
        left, right = [], []
        for part in range(2):
            tiles = [tile_at(q, k + part * half_bins) for q in range(len(blocks))]
            turned = pltpu.roll(tiles[0], half, 1) * sign
            tiles = [t.astype(jnp.bfloat16) for t in tiles]
            left += [tiles[0], turned.astype(jnp.bfloat16)]
            right += tiles
        product = lax.dot_general(
            jnp.concatenate(left, axis=0),
            jnp.concatenate(right, axis=0),
            NT,
            preferred_element_type=jnp.float32,
        )
        product = weight * jnp.where(low_product, product[: 2 * PITCH], product[2 * PITCH :])
        place = pl.ds(pl.multiple_of(k * 2 * PITCH, 2 * PITCH), 2 * PITCH)
        if not first:
            product = product + before_ref[place, :]
        acc_ref[place, :] = product
        return carry

    lax.fori_loop(0, half_bins, step, 0, unroll=half_bins)
    if not last:
        return
    low_half = lane_iota(half) < half
    distances = distances_of(mirrored)

    def finish(a, carry):
        both = jnp.concatenate(
            [
                acc_ref[pl.ds(part * PITCH + a, half_bins, stride=2 * PITCH), :]
                for part in range(2)
            ],
            axis=0,
        )
        by_bin = both.T
        upper, lower = by_bin[:half], by_bin[half:]
        real = jnp.where(low_half, upper, pltpu.roll(lower, half, 1))
        imag = jnp.where(low_half, pltpu.roll(upper, half, 1), lower)
        for part, value in enumerate((real, imag)):
            for q in range(len(blocks)):
                rows = value[q * PITCH : q * PITCH + channels]
                place = pl.ds(a * 2 * channels + part, channels, stride=2)
                if q:
                    kept_ref[distances[q - 1], place, :] = rows
                    back_f32[q - 1, pl.ds(2 * a + part, channels, stride=2 * channels), :] = (
                        -rows if part else rows
                    )
                else:
                    kept_ref[0, place, :] = rows
        return carry

    lax.fori_loop(0, channels, finish, 0, unroll=12)
    for q in range(ROUNDS):
        for d in range(ROUNDS):

            @pl.when(distances[q] == d + 1)
            def _():
                back_refs[d][...] = back_f32[q].astype(jnp.bfloat16)


def pair_hour(blocks, before, hours, last, mirrored):
    channels, bins, lanes = blocks[0].shape
    first = before is None
    acc = (bins // 2 * 2 * PITCH, lanes)
    rows = 2 * channels * channels
    wide = pltpu.VMEM(
        ((len(blocks) * channels + PITCH - channels) * (bins + SKEW), lanes), jnp.float32
    )
    vmem = pl.BlockSpec(memory_space=pltpu.VMEM)
    args, specs = [], []
    args += blocks
    specs += [vmem] * len(blocks)
    if not first:
        args.append(before)
        specs.append(vmem)
    if last:
        out_shape = [
            jax.ShapeDtypeStruct((ROUNDS + 1, rows, lanes), jnp.float32),
            *[jax.ShapeDtypeStruct((rows, lanes), jnp.bfloat16)] * ROUNDS,
        ]
        out_specs = [vmem] * (ROUNDS + 1)
        scratch = [
            wide,
            pltpu.VMEM(acc, jnp.float32),
            pltpu.VMEM((ROUNDS, rows, lanes), jnp.float32),
        ]
    else:
        out_shape = jax.ShapeDtypeStruct(acc, jnp.float32)
        out_specs = vmem
        scratch = [wide]
    return pl.pallas_call(
        lambda *refs: pair_hour_kernel(hours, first, last, mirrored, *refs),
        out_shape=out_shape,
        in_specs=specs,
        out_specs=out_specs,
        scratch_shapes=scratch,
        cost_estimate=PAIR_COST,
        compiler_params=pltpu.CompilerParams(vmem_limit_bytes=PAIR_LIMIT),
        name="pair_hour_last" if last else "pair_hour",
    )(*args)


def put(out_ref, slot, value):
    out_ref[slot] = value.reshape(out_ref.shape[1], 2, LANES).astype(jnp.bfloat16)


def join_below_kernel(behind_ref, ahead_ref, *refs):
    from_rear, out_ref = refs[:ROUNDS], refs[-1]
    put(out_ref, ROUNDS, behind_ref[0] + ahead_ref[0])
    for d in range(1, ROUNDS + 1):
        put(out_ref, ROUNDS - d, behind_ref[d] + from_rear[d - 1][...].astype(jnp.float32))


def join_above_kernel(ahead_ref, *refs):
    from_ahead, out_ref = refs[:ROUNDS], refs[-1]
    for d in range(1, ROUNDS + 1):
        put(out_ref, d - 1, ahead_ref[d] + from_ahead[d - 1][...].astype(jnp.float32))


def join(behind, ahead, from_ahead, from_rear):
    _, rows, lanes = behind.shape
    vmem = pl.BlockSpec(memory_space=pltpu.VMEM)
    out = jax.ShapeDtypeStruct((2 * ROUNDS + 1, rows // 2, 2, lanes), jnp.bfloat16)
    half = (ROUNDS + 1, rows // 2, 2, lanes)
    params = pltpu.CompilerParams(vmem_limit_bytes=4 * MIB)
    below = pl.pallas_call(
        join_below_kernel,
        grid=(1,),
        out_shape=out,
        in_specs=[vmem] * (ROUNDS + 2),
        out_specs=pl.BlockSpec(half, lambda i: (0, 0, 0, 0)),
        compiler_params=params,
        name="join_below",
    )(behind, ahead, *from_rear)
    return pl.pallas_call(
        join_above_kernel,
        grid=(1,),
        out_shape=out,
        in_specs=[vmem] * (ROUNDS + 1) + [pl.BlockSpec(memory_space=pl.ANY)],
        out_specs=pl.BlockSpec(half, lambda i: (1, 0, 0, 0)),
        input_output_aliases={ROUNDS + 1: 0},
        compiler_params=params,
        name="join_above",
    )(ahead, *from_ahead, below)


LEVEL = 4
DISTANCES = ((3, 1, 2), (1, 3, 2), (3, 2, 1), (1, 2, 3))


def send(value, count, mirrored, *hops):
    levels = count // LEVEL
    pairs = [
        (LEVEL * level + source, LEVEL * ((level + up) % levels) + target)
        for source, target, up in hops
        for level in range(levels)
    ]
    if mirrored:
        pairs = [(count - 1 - source, count - 1 - target) for source, target in pairs]
    return lax.ppermute(value, "sta", pairs)


def shift(value, count, steps):
    pairs = [(source, (source + steps) % count) for source in range(count)]
    return lax.ppermute(value, "sta", pairs)


def fetch_partners(block, count, hour):
    mirrored = hour % 2 == 1
    if count % LEVEL:
        way = -1 if mirrored else 1
        return [shift(block, count, way * steps) for steps in range(1, ROUNDS + 1)]
    far = send(block, count, mirrored, (0, 2, 0), (1, 3, 0), (2, 1, 1), (3, 0, 1))
    near = send(block, count, mirrored, (0, 1, 0), (2, 3, 0), (1, 0, 1), (3, 2, 1))
    other = send(far, count, mirrored, (0, 1, 0), (1, 0, 0), (2, 3, 0), (3, 2, 0))
    return [near, far, other]


def distances_of(mirrored):
    count = lax.axis_size("sta")
    if count % LEVEL:
        return list(range(1, ROUNDS + 1))
    role = lax.rem(lax.axis_index("sta"), LEVEL)
    role = LEVEL - 1 - role if mirrored else role
    chosen = []
    for q in range(ROUNDS):
        away = jnp.int32(DISTANCES[LEVEL - 1][q])
        for r in range(LEVEL - 1):
            away = jnp.where(role == r, DISTANCES[r][q], away)
        chosen.append(away)
    return chosen


def spectra(records, counts, gap_mask):
    channels, _, samples = records.shape
    hours = counts.shape[1]
    bins = samples // 2
    count = lax.axis_size("sta")
    table = fourier_matrix(samples)
    first, rest, valid, table = whiten_first(records, counts, gap_mask, table)
    whitened = [first] + [whiten_hour(rest, valid, table, hour) for hour in range(1, hours)]
    partners = [fetch_partners(whitened[hour], count, hour) for hour in range(hours)]
    sums = [None, None]
    for hour in range(hours):
        mirrored = hour % 2
        sums[mirrored] = pair_hour(
            [whitened[hour], *partners[hour]],
            sums[mirrored],
            hours,
            hour + 2 >= hours,
            mirrored == 1,
        )
    (behind, *back), (ahead, *forth) = sums
    from_ahead, from_rear = [], []
    for d in range(1, ROUNDS + 1):
        from_ahead.append(shift(back[d - 1], count, -d))
        from_rear.append(shift(forth[d - 1], count, d))
    stacked = join(behind, ahead, from_ahead, from_rear)
    stacked = stacked.reshape(2 * ROUNDS + 1, channels, channels, 2, bins)
    return jnp.transpose(stacked, (0, 3, 1, 2, 4))


def solution(mesh):
    in_specs = (P(("days", "sta"), None, None), P(("days", "sta"), None), P(("days", "sta"), None))
    out_specs = P(None, None, ("days", "sta"), None, None)
    return jax.shard_map(
        spectra, mesh=mesh, in_specs=in_specs, out_specs=out_specs, check_vma=False
    )
```

```python
import math

import jax
import jax.numpy as jnp
import numpy as np
from jax import lax
from jax.experimental import pallas as pl
from jax.experimental.pallas import tpu as pltpu
from jax.sharding import PartitionSpec as P


ROUNDS = 3
LANES = 128
PITCH = 16
SKEW = 8
MIB = 1 << 20
PAIR_LIMIT = 10 * MIB
PAIR_COST = pl.CostEstimate(flops=3_000_000_000, transcendentals=0, bytes_accessed=12_000_000)
WHITEN_COST = pl.CostEstimate(flops=2_000_000_000, transcendentals=0, bytes_accessed=8_000_000)

epsilon = 1e-06

NT = (((1,), (1,)), ((), ()))


def fourier_matrix(samples):
    freq_bins = samples // 2
    times_axis = np.arange(samples, dtype=np.int32)
    bins_axis = np.arange(freq_bins, dtype=np.int32)
    phase_idx = times_axis[:, None] * bins_axis[None, :] % samples
    step = np.float32(2.0 * math.pi / samples)
    angle = step * phase_idx.astype(np.float32)
    half = np.float32(0.5)
    taper = half - half * np.cos(step * (times_axis.astype(np.float32) + half))
    table_re = taper[:, None] * np.cos(angle)
    table_im = -taper[:, None] * np.sin(angle)
    return jnp.asarray(np.concatenate([table_re.T, table_im.T], axis=0).astype(jnp.bfloat16))


def lane_iota(rows):
    return lax.broadcasted_iota(jnp.int32, (rows, LANES), 1)


def validity_rows(hour, seg_hour, counts_ref, gap_ref):
    stations = gap_ref.shape[0]
    per_tile = LANES // seg_hour
    tile = gap_ref[:, pl.ds(hour // per_tile * LANES, LANES)].astype(jnp.float32)
    turned = pltpu.roll(tile, seg_hour, 1)
    lane = lane_iota(stations)
    low = lane < seg_hour
    doubled = jnp.where(low, tile, turned) if hour % per_tile == 0 else jnp.where(low, turned, tile)
    position = jnp.where(low, lane, lane - seg_hour)
    return [
        jnp.where(
            position[station : station + 1] < counts_ref[station, hour],
            doubled[station : station + 1],
            0.0,
        )
        for station in range(stations)
    ]


def whiten_block(records_ref, valid, table_ref, out_ref):
    channels, seg_hour, samples = records_ref.shape
    bins = samples // 2
    row = lax.broadcasted_iota(jnp.int32, (bins, LANES), 0)
    low_side = lane_iota(bins) < seg_hour
    slot = jnp.logical_and(row == 0, jnp.logical_not(low_side))
    table = table_ref[...]
    per_station = channels // len(valid)
    first_half = lane_iota(1) < seg_hour
    for channel in range(0, channels, 2):
        both = jnp.concatenate([records_ref[channel], records_ref[channel + 1]], axis=0)
        spectrum = lax.dot_general(table, both, NT, preferred_element_type=jnp.float32)
        power = jnp.sum(spectrum * spectrum, axis=0, keepdims=True) * (1.0 / samples)
        pair_valid = jnp.where(
            first_half, valid[channel // per_station], valid[(channel + 1) // per_station]
        )
        scaled = spectrum * (lax.rsqrt(power + epsilon) * pair_valid)
        real, imag = scaled[:bins], scaled[bins:]
        one = jnp.where(low_side, real, pltpu.roll(imag, seg_hour, 1))
        two = jnp.where(low_side, pltpu.roll(real, seg_hour, 1), imag)
        for value, at in ((one, channel), (two, channel + 1)):
            value = jnp.where(slot, valid[at // per_station], value)
            out_ref[at] = value.astype(jnp.bfloat16)


def hour_of(records_hbm, hour, seg_hour):
    return records_hbm.at[:, pl.ds(hour * seg_hour, seg_hour), :]


def whiten_first_kernel(counts_hbm, records_hbm, gap_hbm, table_hbm, *refs):
    out_ref, next_ref, valid_ref, table_ref, counts_ref, records_ref, gap_ref, sems = refs
    seg_hour = records_ref.shape[1]
    hours = valid_ref.shape[0]
    moves = [
        (hour_of(records_hbm, 0, seg_hour), records_ref),
        (counts_hbm, counts_ref),
        (gap_hbm, gap_ref),
        (table_hbm, table_ref),
        (hour_of(records_hbm, 1, seg_hour), next_ref),
    ]
    *copies, ahead = [
        pltpu.make_async_copy(source, target, sems.at[i])
        for i, (source, target) in enumerate(moves)
    ]
    for copy in copies:
        copy.start()
    for copy in copies:
        copy.wait()
    ahead.start()
    valid = [validity_rows(hour, seg_hour, counts_ref, gap_ref) for hour in range(hours)]
    for hour in range(1, hours):
        for station, row in enumerate(valid[hour]):
            valid_ref[hour, station : station + 1, :] = row
    whiten_block(records_ref, valid[0], table_ref, out_ref)
    ahead.wait()


def whiten_first(records, counts, gap_mask, table):
    channels, segments, samples = records.shape
    stations, hours = counts.shape
    seg_hour = segments // hours
    hbm = pl.BlockSpec(memory_space=pltpu.HBM)
    vmem = pl.BlockSpec(memory_space=pltpu.VMEM)
    block = (channels, seg_hour, samples)
    return pl.pallas_call(
        whiten_first_kernel,
        out_shape=[
            jax.ShapeDtypeStruct((channels, samples // 2, LANES), jnp.bfloat16),
            jax.ShapeDtypeStruct(block, records.dtype),
            jax.ShapeDtypeStruct((hours, stations, LANES), jnp.float32),
            jax.ShapeDtypeStruct(table.shape, table.dtype),
        ],
        in_specs=[hbm] * 4,
        out_specs=[vmem] * 4,
        scratch_shapes=[
            pltpu.SMEM(counts.shape, counts.dtype),
            pltpu.VMEM(block, records.dtype),
            pltpu.VMEM(gap_mask.shape, gap_mask.dtype),
            pltpu.SemaphoreType.DMA((5,)),
        ],
        cost_estimate=WHITEN_COST,
        compiler_params=pltpu.CompilerParams(vmem_limit_bytes=4 * MIB),
        name="whiten_first",
    )(
        *(
            pltpu.with_memory_space_constraint(x, pltpu.HBM)
            for x in (counts, records, gap_mask, table)
        )
    )


def whiten_hour_kernel(hour, last, records_hbm, current_ref, valid_ref, table_ref, out_ref, *refs):
    if not last:
        next_ref, sem = refs
        seg_hour = current_ref.shape[1]
        ahead = pltpu.make_async_copy(hour_of(records_hbm, hour + 1, seg_hour), next_ref, sem)
        ahead.start()
    valid = [valid_ref[hour, station : station + 1, :] for station in range(valid_ref.shape[1])]
    whiten_block(current_ref, valid, table_ref, out_ref)
    if not last:
        ahead.wait()


def whiten_hour(records, current, valid, table, hour):
    channels, _, samples = current.shape
    last = hour + 1 == valid.shape[0]
    vmem = pl.BlockSpec(memory_space=pltpu.VMEM)
    out_shape = [jax.ShapeDtypeStruct((channels, samples // 2, LANES), jnp.bfloat16)]
    if not last:
        out_shape.append(jax.ShapeDtypeStruct(current.shape, current.dtype))
    return pl.pallas_call(
        lambda *refs: whiten_hour_kernel(hour, last, *refs),
        out_shape=out_shape,
        in_specs=[pl.BlockSpec(memory_space=pltpu.HBM)] + [vmem] * 3,
        out_specs=[vmem] * len(out_shape),
        scratch_shapes=[] if last else [pltpu.SemaphoreType.DMA],
        cost_estimate=WHITEN_COST,
        compiler_params=pltpu.CompilerParams(vmem_limit_bytes=4 * MIB),
        name="whiten_hour",
    )(pltpu.with_memory_space_constraint(records, pltpu.HBM), current, valid, table)


def pair_hour_kernel(hours, first, last, mirrored, *refs):
    refs = list(refs)
    blocks = [refs.pop(0) for _ in range(ROUNDS + 1)]
    before_ref = None if first else refs.pop(0)
    channels, bins, _ = blocks[0].shape
    half = LANES // 2
    if last:
        kept_ref, *back_refs, wide_ref, acc_ref, back_f32 = refs
    else:
        acc_ref, wide_ref = refs
    pitch = bins + SKEW
    for q, block in enumerate(blocks):
        for channel in range(channels):
            start = (q * channels + channel) * pitch
            wide_ref[start : start + bins, :] = block[channel].astype(jnp.float32)
    for pad in range(PITCH - channels):
        start = (len(blocks) * channels + pad) * pitch
        wide_ref[start : start + bins, :] = jnp.zeros((bins, LANES), jnp.float32)

    def tile_at(q, k):
        return wide_ref[pl.ds(q * channels * pitch + k, PITCH, stride=pitch), :]

    low = lane_iota(PITCH) < half
    zeroth = [tile_at(q, 0) for q in range(len(blocks))]
    valid = [jnp.where(low, pltpu.roll(t, half, 1), t).astype(jnp.bfloat16) for t in zeroth]
    for q, t in enumerate(zeroth):
        wide_ref[pl.ds(q * channels * pitch, PITCH, stride=pitch), :] = jnp.where(low, t, 0.0)
    joint = 0.5 * lax.dot_general(
        valid[0], jnp.concatenate(valid + valid, axis=0), NT, preferred_element_type=jnp.float32
    )
    weight = 1.0 / (hours * jnp.maximum(joint, 1.0))
    weight = jnp.concatenate([weight, weight], axis=0)
    sign = jnp.where(low, 1.0, -1.0)
    low_product = lane_iota(2 * PITCH) < half
    half_bins = bins // 2

    def step(k, carry):
        left, right = [], []
        for part in range(2):
            tiles = [tile_at(q, k + part * half_bins) for q in range(len(blocks))]
            turned = pltpu.roll(tiles[0], half, 1) * sign
            tiles = [t.astype(jnp.bfloat16) for t in tiles]
            left += [tiles[0], turned.astype(jnp.bfloat16)]
            right += tiles
        product = lax.dot_general(
            jnp.concatenate(left, axis=0),
            jnp.concatenate(right, axis=0),
            NT,
            preferred_element_type=jnp.float32,
        )
        product = weight * jnp.where(low_product, product[: 2 * PITCH], product[2 * PITCH :])
        place = pl.ds(pl.multiple_of(k * 2 * PITCH, 2 * PITCH), 2 * PITCH)
        if not first:
            product = product + before_ref[place, :]
        acc_ref[place, :] = product
        return carry

    lax.fori_loop(0, half_bins, step, 0, unroll=half_bins)
    if not last:
        return
    low_half = lane_iota(half) < half
    distances = distances_of(mirrored)

    def finish(a, carry):
        both = jnp.concatenate(
            [
                acc_ref[pl.ds(part * PITCH + a, half_bins, stride=2 * PITCH), :]
                for part in range(2)
            ],
            axis=0,
        )
        by_bin = both.T
        upper, lower = by_bin[:half], by_bin[half:]
        real = jnp.where(low_half, upper, pltpu.roll(lower, half, 1))
        imag = jnp.where(low_half, pltpu.roll(upper, half, 1), lower)
        for part, value in enumerate((real, imag)):
            for q in range(len(blocks)):
                rows = value[q * PITCH : q * PITCH + channels]
                place = pl.ds(a * 2 * channels + part, channels, stride=2)
                if q:
                    kept_ref[distances[q - 1], place, :] = rows
                    back_f32[q - 1, pl.ds(2 * a + part, channels, stride=2 * channels), :] = (
                        -rows if part else rows
                    )
                else:
                    kept_ref[0, place, :] = rows
        return carry

    lax.fori_loop(0, channels, finish, 0, unroll=12)
    for q in range(ROUNDS):
        for d in range(ROUNDS):

            @pl.when(distances[q] == d + 1)
            def _():
                back_refs[d][...] = back_f32[q].astype(jnp.bfloat16)


def pair_hour(blocks, before, hours, last, mirrored):
    channels, bins, lanes = blocks[0].shape
    first = before is None
    acc = (bins // 2 * 2 * PITCH, lanes)
    rows = 2 * channels * channels
    wide = pltpu.VMEM(
        ((len(blocks) * channels + PITCH - channels) * (bins + SKEW), lanes), jnp.float32
    )
    vmem = pl.BlockSpec(memory_space=pltpu.VMEM)
    args, specs = [], []
    args += blocks
    specs += [vmem] * len(blocks)
    if not first:
        args.append(before)
        specs.append(vmem)
    if last:
        out_shape = [
            jax.ShapeDtypeStruct((ROUNDS + 1, rows, lanes), jnp.float32),
            *[jax.ShapeDtypeStruct((rows, lanes), jnp.bfloat16)] * ROUNDS,
        ]
        out_specs = [vmem] * (ROUNDS + 1)
        scratch = [
            wide,
            pltpu.VMEM(acc, jnp.float32),
            pltpu.VMEM((ROUNDS, rows, lanes), jnp.float32),
        ]
    else:
        out_shape = jax.ShapeDtypeStruct(acc, jnp.float32)
        out_specs = vmem
        scratch = [wide]
    return pl.pallas_call(
        lambda *refs: pair_hour_kernel(hours, first, last, mirrored, *refs),
        out_shape=out_shape,
        in_specs=specs,
        out_specs=out_specs,
        scratch_shapes=scratch,
        cost_estimate=PAIR_COST,
        compiler_params=pltpu.CompilerParams(vmem_limit_bytes=PAIR_LIMIT),
        name="pair_hour_last" if last else "pair_hour",
    )(*args)


def put(out_ref, slot, value):
    out_ref[slot] = value.reshape(out_ref.shape[1], 2, LANES).astype(jnp.bfloat16)


def join_below_kernel(behind_ref, ahead_ref, *refs):
    from_rear, out_ref = refs[:ROUNDS], refs[-1]
    put(out_ref, ROUNDS, behind_ref[0] + ahead_ref[0])
    for d in range(1, ROUNDS + 1):
        put(out_ref, ROUNDS - d, behind_ref[d] + from_rear[d - 1][...].astype(jnp.float32))


def join_above_kernel(ahead_ref, *refs):
    from_ahead, out_ref = refs[:ROUNDS], refs[-1]
    for d in range(1, ROUNDS + 1):
        put(out_ref, d - 1, ahead_ref[d] + from_ahead[d - 1][...].astype(jnp.float32))


def join(behind, ahead, from_ahead, from_rear):
    _, rows, lanes = behind.shape
    vmem = pl.BlockSpec(memory_space=pltpu.VMEM)
    out = jax.ShapeDtypeStruct((2 * ROUNDS + 1, rows // 2, 2, lanes), jnp.bfloat16)
    half = (ROUNDS + 1, rows // 2, 2, lanes)
    params = pltpu.CompilerParams(vmem_limit_bytes=4 * MIB)
    below = pl.pallas_call(
        join_below_kernel,
        grid=(1,),
        out_shape=out,
        in_specs=[vmem] * (ROUNDS + 2),
        out_specs=pl.BlockSpec(half, lambda i: (0, 0, 0, 0)),
        compiler_params=params,
        name="join_below",
    )(behind, ahead, *from_rear)
    return pl.pallas_call(
        join_above_kernel,
        grid=(1,),
        out_shape=out,
        in_specs=[vmem] * (ROUNDS + 1) + [pl.BlockSpec(memory_space=pl.ANY)],
        out_specs=pl.BlockSpec(half, lambda i: (1, 0, 0, 0)),
        input_output_aliases={ROUNDS + 1: 0},
        compiler_params=params,
        name="join_above",
    )(ahead, *from_ahead, below)


LEVEL = 4
DISTANCES = ((3, 1, 2), (1, 3, 2), (3, 2, 1), (1, 2, 3))


def send(value, count, mirrored, *hops):
    levels = count // LEVEL
    pairs = [
        (LEVEL * level + source, LEVEL * ((level + up) % levels) + target)
        for source, target, up in hops
        for level in range(levels)
    ]
    if mirrored:
        pairs = [(count - 1 - source, count - 1 - target) for source, target in pairs]
    return lax.ppermute(value, "sta", pairs)


def shift(value, count, steps):
    pairs = [(source, (source + steps) % count) for source in range(count)]
    return lax.ppermute(value, "sta", pairs)


def fetch_partners(block, count, hour):
    mirrored = hour % 2 == 1
    if count % LEVEL:
        way = -1 if mirrored else 1
        return [shift(block, count, way * steps) for steps in range(1, ROUNDS + 1)]
    far = send(block, count, mirrored, (0, 2, 0), (1, 3, 0), (2, 1, 1), (3, 0, 1))
    near = send(block, count, mirrored, (0, 1, 0), (2, 3, 0), (1, 0, 1), (3, 2, 1))
    other = send(far, count, mirrored, (0, 1, 0), (1, 0, 0), (2, 3, 0), (3, 2, 0))
    return [near, far, other]


def distances_of(mirrored):
    count = lax.axis_size("sta")
    if count % LEVEL:
        return list(range(1, ROUNDS + 1))
    role = lax.rem(lax.axis_index("sta"), LEVEL)
    role = LEVEL - 1 - role if mirrored else role
    chosen = []
    for q in range(ROUNDS):
        away = jnp.int32(DISTANCES[LEVEL - 1][q])
        for r in range(LEVEL - 1):
            away = jnp.where(role == r, DISTANCES[r][q], away)
        chosen.append(away)
    return chosen


def spectra(records, counts, gap_mask):
    channels, _, samples = records.shape
    hours = counts.shape[1]
    bins = samples // 2
    count = lax.axis_size("sta")
    table = fourier_matrix(samples)
    first, current, valid, table = whiten_first(records, counts, gap_mask, table)
    whitened = [first]
    for hour in range(1, hours):
        block, *ahead = whiten_hour(records, current, valid, table, hour)
        whitened.append(block)
        current = ahead[0] if ahead else None
    partners = [fetch_partners(whitened[hour], count, hour) for hour in range(hours)]
    sums = [None, None]
    for hour in range(hours):
        mirrored = hour % 2
        sums[mirrored] = pair_hour(
            [whitened[hour], *partners[hour]],
            sums[mirrored],
            hours,
            hour + 2 >= hours,
            mirrored == 1,
        )
    (behind, *back), (ahead, *forth) = sums
    from_ahead, from_rear = [], []
    for d in range(1, ROUNDS + 1):
        from_ahead.append(shift(back[d - 1], count, -d))
        from_rear.append(shift(forth[d - 1], count, d))
    stacked = join(behind, ahead, from_ahead, from_rear)
    stacked = stacked.reshape(2 * ROUNDS + 1, channels, channels, 2, bins)
    return jnp.transpose(stacked, (0, 3, 1, 2, 4))


def solution(mesh):
    in_specs = (P(("days", "sta"), None, None), P(("days", "sta"), None), P(("days", "sta"), None))
    out_specs = P(None, None, ("days", "sta"), None, None)
    return jax.shard_map(
        spectra, mesh=mesh, in_specs=in_specs, out_specs=out_specs, check_vma=False
    )
```

```python
import math

import jax
import jax.numpy as jnp
import numpy as np
from jax import lax
from jax.experimental import pallas as pl
from jax.experimental.pallas import tpu as pltpu
from jax.sharding import PartitionSpec as P


ROUNDS = 3
COMPONENTS = 3
LANES = 128
PITCH = 16
SKEW = 8
MIB = 1 << 20
PAIR_LIMIT = 10 * MIB
FETCHES = COMPONENTS
PAIR_COST = pl.CostEstimate(flops=3_000_000_000, transcendentals=0, bytes_accessed=12_000_000)
WHITEN_COST = pl.CostEstimate(flops=2_000_000_000, transcendentals=0, bytes_accessed=8_000_000)

epsilon = 1e-06

NT = (((1,), (1,)), ((), ()))


def fourier_matrix(samples):
    freq_bins = samples // 2
    times_axis = np.arange(samples, dtype=np.int32)
    bins_axis = np.arange(freq_bins, dtype=np.int32)
    phase_idx = times_axis[:, None] * bins_axis[None, :] % samples
    step = np.float32(2.0 * math.pi / samples)
    angle = step * phase_idx.astype(np.float32)
    half = np.float32(0.5)
    taper = half - half * np.cos(step * (times_axis.astype(np.float32) + half))
    table_re = taper[:, None] * np.cos(angle)
    table_im = -taper[:, None] * np.sin(angle)
    return jnp.asarray(np.concatenate([table_re.T, table_im.T], axis=0).astype(jnp.bfloat16))


def lane_iota(rows):
    return lax.broadcasted_iota(jnp.int32, (rows, LANES), 1)


def validity_rows(hour, seg_hour, counts_ref, gap_ref):
    stations = gap_ref.shape[0]
    per_tile = LANES // seg_hour
    tile = gap_ref[:, pl.ds(hour // per_tile * LANES, LANES)].astype(jnp.float32)
    turned = pltpu.roll(tile, seg_hour, 1)
    lane = lane_iota(stations)
    low = lane < seg_hour
    doubled = jnp.where(low, tile, turned) if hour % per_tile == 0 else jnp.where(low, turned, tile)
    position = jnp.where(low, lane, lane - seg_hour)
    return [
        jnp.where(
            position[station : station + 1] < counts_ref[station, hour],
            doubled[station : station + 1],
            0.0,
        )
        for station in range(stations)
    ]


def whiten_block(records_ref, valid, table_ref, out_ref):
    channels, seg_hour, samples = records_ref.shape
    bins = samples // 2
    row = lax.broadcasted_iota(jnp.int32, (bins, LANES), 0)
    low_side = lane_iota(bins) < seg_hour
    slot = jnp.logical_and(row == 0, jnp.logical_not(low_side))
    table = table_ref[...]
    per_station = channels // len(valid)
    first_half = lane_iota(1) < seg_hour
    for channel in range(0, channels, 2):
        both = jnp.concatenate([records_ref[channel], records_ref[channel + 1]], axis=0)
        spectrum = lax.dot_general(table, both, NT, preferred_element_type=jnp.float32)
        power = jnp.sum(spectrum * spectrum, axis=0, keepdims=True) * (1.0 / samples)
        pair_valid = jnp.where(
            first_half, valid[channel // per_station], valid[(channel + 1) // per_station]
        )
        scaled = spectrum * (lax.rsqrt(power + epsilon) * pair_valid)
        real, imag = scaled[:bins], scaled[bins:]
        one = jnp.where(low_side, real, pltpu.roll(imag, seg_hour, 1))
        two = jnp.where(low_side, pltpu.roll(real, seg_hour, 1), imag)
        for value, at in ((one, channel), (two, channel + 1)):
            value = jnp.where(slot, valid[at // per_station], value)
            out_ref[at] = value.astype(jnp.bfloat16)


def whiten_first_kernel(counts_hbm, records_hbm, gap_hbm, table_hbm, *refs):
    out_ref, rest_ref, valid_ref, table_ref, counts_ref, records_ref, gap_ref, sems = refs
    seg_hour = records_ref.shape[1]
    hours = valid_ref.shape[0]

    channels = records_ref.shape[0]

    def parts(hour, target, count):
        size = channels // count
        for part in range(count):
            span = pl.ds(part * size, size)
            yield (
                records_hbm.at[span, pl.ds(hour * seg_hour, seg_hour), :],
                target.at[span],
            )

    moves = list(parts(0, records_ref, channels))
    moves += [(counts_hbm, counts_ref), (gap_hbm, gap_ref), (table_hbm, table_ref)]
    now = len(moves)
    for hour in range(1, hours):
        moves += parts(hour, rest_ref.at[hour - 1], FETCHES)
    copies = [
        pltpu.make_async_copy(source, target, sems.at[i])
        for i, (source, target) in enumerate(moves)
    ]
    for copy in copies:
        copy.start()
    for copy in copies[:now]:
        copy.wait()
    valid = [validity_rows(hour, seg_hour, counts_ref, gap_ref) for hour in range(hours)]
    for hour in range(1, hours):
        for station, row in enumerate(valid[hour]):
            valid_ref[hour, station : station + 1, :] = row
    whiten_block(records_ref, valid[0], table_ref, out_ref)
    for copy in copies[now:]:
        copy.wait()


def whiten_first(records, counts, gap_mask, table):
    channels, segments, samples = records.shape
    stations, hours = counts.shape
    seg_hour = segments // hours
    hbm = pl.BlockSpec(memory_space=pltpu.HBM)
    vmem = pl.BlockSpec(memory_space=pltpu.VMEM)
    block = (channels, seg_hour, samples)
    return pl.pallas_call(
        whiten_first_kernel,
        out_shape=[
            jax.ShapeDtypeStruct((channels, samples // 2, LANES), jnp.bfloat16),
            jax.ShapeDtypeStruct((hours - 1, *block), records.dtype),
            jax.ShapeDtypeStruct((hours, stations, LANES), jnp.float32),
            jax.ShapeDtypeStruct(table.shape, table.dtype),
        ],
        in_specs=[hbm] * 4,
        out_specs=[vmem] * 4,
        scratch_shapes=[
            pltpu.SMEM(counts.shape, counts.dtype),
            pltpu.VMEM(block, records.dtype),
            pltpu.VMEM(gap_mask.shape, gap_mask.dtype),
            pltpu.SemaphoreType.DMA((channels + 3 + (hours - 1) * FETCHES,)),
        ],
        cost_estimate=WHITEN_COST,
        compiler_params=pltpu.CompilerParams(vmem_limit_bytes=4 * MIB),
        name="whiten_first",
    )(
        *(
            pltpu.with_memory_space_constraint(x, pltpu.HBM)
            for x in (counts, records, gap_mask, table)
        )
    )


def whiten_hour_kernel(hour, rest_ref, valid_ref, table_ref, out_ref):
    valid = [valid_ref[hour, station : station + 1, :] for station in range(valid_ref.shape[1])]
    whiten_block(rest_ref.at[hour - 1], valid, table_ref, out_ref)


def whiten_hour(rest, valid, table, hour):
    _, channels, _, samples = rest.shape
    vmem = pl.BlockSpec(memory_space=pltpu.VMEM)
    return pl.pallas_call(
        lambda *refs: whiten_hour_kernel(hour, *refs),
        out_shape=jax.ShapeDtypeStruct((channels, samples // 2, LANES), jnp.bfloat16),
        in_specs=[vmem] * 3,
        out_specs=vmem,
        cost_estimate=WHITEN_COST,
        compiler_params=pltpu.CompilerParams(vmem_limit_bytes=4 * MIB),
        name="whiten_hour",
    )(rest, valid, table)


def pair_hour_kernel(hours, first, last, mirrored, *refs):
    refs = list(refs)
    blocks = [refs.pop(0) for _ in range(ROUNDS + 1)]
    before_ref = None if first else refs.pop(0)
    channels, bins, _ = blocks[0].shape
    half = LANES // 2
    if last:
        kept_ref, *back_refs, wide_ref, acc_ref, back_f32 = refs
    else:
        acc_ref, wide_ref = refs
    pitch = bins + SKEW
    for q, block in enumerate(blocks):
        for channel in range(channels):
            start = (q * channels + channel) * pitch
            wide_ref[start : start + bins, :] = block[channel].astype(jnp.float32)
    for pad in range(PITCH - channels):
        start = (len(blocks) * channels + pad) * pitch
        wide_ref[start : start + bins, :] = jnp.zeros((bins, LANES), jnp.float32)

    def tile_at(q, k):
        return wide_ref[pl.ds(q * channels * pitch + k, PITCH, stride=pitch), :]

    low = lane_iota(PITCH) < half
    zeroth = [tile_at(q, 0) for q in range(len(blocks))]
    valid = [jnp.where(low, pltpu.roll(t, half, 1), t).astype(jnp.bfloat16) for t in zeroth]
    for q, t in enumerate(zeroth):
        wide_ref[pl.ds(q * channels * pitch, PITCH, stride=pitch), :] = jnp.where(low, t, 0.0)
    joint = 0.5 * lax.dot_general(
        valid[0], jnp.concatenate(valid + valid, axis=0), NT, preferred_element_type=jnp.float32
    )
    weight = 1.0 / (hours * jnp.maximum(joint, 1.0))
    weight = jnp.concatenate([weight, weight], axis=0)
    sign = jnp.where(low, 1.0, -1.0)
    low_product = lane_iota(2 * PITCH) < half
    half_bins = bins // 2

    def step(k, carry):
        left, right = [], []
        for part in range(2):
            tiles = [tile_at(q, k + part * half_bins) for q in range(len(blocks))]
            turned = pltpu.roll(tiles[0], half, 1) * sign
            tiles = [t.astype(jnp.bfloat16) for t in tiles]
            left += [tiles[0], turned.astype(jnp.bfloat16)]
            right += tiles
        product = lax.dot_general(
            jnp.concatenate(left, axis=0),
            jnp.concatenate(right, axis=0),
            NT,
            preferred_element_type=jnp.float32,
        )
        product = weight * jnp.where(low_product, product[: 2 * PITCH], product[2 * PITCH :])
        place = pl.ds(pl.multiple_of(k * 2 * PITCH, 2 * PITCH), 2 * PITCH)
        if not first:
            product = product + before_ref[place, :]
        acc_ref[place, :] = product
        return carry

    lax.fori_loop(0, half_bins, step, 0, unroll=half_bins)
    if not last:
        return
    low_half = lane_iota(half) < half
    distances = distances_of(mirrored)

    def finish(a, carry):
        both = jnp.concatenate(
            [
                acc_ref[pl.ds(part * PITCH + a, half_bins, stride=2 * PITCH), :]
                for part in range(2)
            ],
            axis=0,
        )
        by_bin = both.T
        upper, lower = by_bin[:half], by_bin[half:]
        real = jnp.where(low_half, upper, pltpu.roll(lower, half, 1))
        imag = jnp.where(low_half, pltpu.roll(upper, half, 1), lower)
        for part, value in enumerate((real, imag)):
            for q in range(len(blocks)):
                rows = value[q * PITCH : q * PITCH + channels]
                place = pl.ds(a * 2 * channels + part, channels, stride=2)
                if q:
                    kept_ref[distances[q - 1], place, :] = rows
                    back_f32[q - 1, pl.ds(2 * a + part, channels, stride=2 * channels), :] = (
                        -rows if part else rows
                    )
                else:
                    kept_ref[0, place, :] = rows
        return carry

    lax.fori_loop(0, channels, finish, 0, unroll=12)
    for q in range(ROUNDS):
        for d in range(ROUNDS):

            @pl.when(distances[q] == d + 1)
            def _():
                back_refs[d][...] = back_f32[q].astype(jnp.bfloat16)


def pair_hour(blocks, before, hours, last, mirrored):
    channels, bins, lanes = blocks[0].shape
    first = before is None
    acc = (bins // 2 * 2 * PITCH, lanes)
    rows = 2 * channels * channels
    wide = pltpu.VMEM(
        ((len(blocks) * channels + PITCH - channels) * (bins + SKEW), lanes), jnp.float32
    )
    vmem = pl.BlockSpec(memory_space=pltpu.VMEM)
    args, specs = [], []
    args += blocks
    specs += [vmem] * len(blocks)
    if not first:
        args.append(before)
        specs.append(vmem)
    if last:
        out_shape = [
            jax.ShapeDtypeStruct((ROUNDS + 1, rows, lanes), jnp.float32),
            *[jax.ShapeDtypeStruct((rows, lanes), jnp.bfloat16)] * ROUNDS,
        ]
        out_specs = [vmem] * (ROUNDS + 1)
        scratch = [
            wide,
            pltpu.VMEM(acc, jnp.float32),
            pltpu.VMEM((ROUNDS, rows, lanes), jnp.float32),
        ]
    else:
        out_shape = jax.ShapeDtypeStruct(acc, jnp.float32)
        out_specs = vmem
        scratch = [wide]
    return pl.pallas_call(
        lambda *refs: pair_hour_kernel(hours, first, last, mirrored, *refs),
        out_shape=out_shape,
        in_specs=specs,
        out_specs=out_specs,
        scratch_shapes=scratch,
        cost_estimate=PAIR_COST,
        compiler_params=pltpu.CompilerParams(vmem_limit_bytes=PAIR_LIMIT),
        name="pair_hour_last" if last else "pair_hour",
    )(*args)


def put(out_ref, slot, value):
    out_ref[slot] = value.reshape(out_ref.shape[1], 2, LANES).astype(jnp.bfloat16)


def join_below_kernel(behind_ref, ahead_ref, *refs):
    from_rear, out_ref = refs[:ROUNDS], refs[-1]
    put(out_ref, ROUNDS, behind_ref[0] + ahead_ref[0])
    for d in range(1, ROUNDS + 1):
        put(out_ref, ROUNDS - d, behind_ref[d] + from_rear[d - 1][...].astype(jnp.float32))


def join_above_kernel(ahead_ref, *refs):
    from_ahead, out_ref = refs[:ROUNDS], refs[-1]
    for d in range(1, ROUNDS + 1):
        put(out_ref, d - 1, ahead_ref[d] + from_ahead[d - 1][...].astype(jnp.float32))


def join(behind, ahead, from_ahead, from_rear):
    _, rows, lanes = behind.shape
    vmem = pl.BlockSpec(memory_space=pltpu.VMEM)
    out = jax.ShapeDtypeStruct((2 * ROUNDS + 1, rows // 2, 2, lanes), jnp.bfloat16)
    half = (ROUNDS + 1, rows // 2, 2, lanes)
    params = pltpu.CompilerParams(vmem_limit_bytes=4 * MIB)
    below = pl.pallas_call(
        join_below_kernel,
        grid=(1,),
        out_shape=out,
        in_specs=[vmem] * (ROUNDS + 2),
        out_specs=pl.BlockSpec(half, lambda i: (0, 0, 0, 0)),
        compiler_params=params,
        name="join_below",
    )(behind, ahead, *from_rear)
    return pl.pallas_call(
        join_above_kernel,
        grid=(1,),
        out_shape=out,
        in_specs=[vmem] * (ROUNDS + 1) + [pl.BlockSpec(memory_space=pl.ANY)],
        out_specs=pl.BlockSpec(half, lambda i: (1, 0, 0, 0)),
        input_output_aliases={ROUNDS + 1: 0},
        compiler_params=params,
        name="join_above",
    )(ahead, *from_ahead, below)


LEVEL = 4
DISTANCES = ((3, 1, 2), (1, 3, 2), (3, 2, 1), (1, 2, 3))


def send(value, count, mirrored, *hops):
    levels = count // LEVEL
    pairs = [
        (LEVEL * level + source, LEVEL * ((level + up) % levels) + target)
        for source, target, up in hops
        for level in range(levels)
    ]
    if mirrored:
        pairs = [(count - 1 - source, count - 1 - target) for source, target in pairs]
    return lax.ppermute(value, "sta", pairs)


def shift(value, count, steps):
    pairs = [(source, (source + steps) % count) for source in range(count)]
    return lax.ppermute(value, "sta", pairs)


def fetch_partners(block, count, hour):
    mirrored = hour % 2 == 1
    if count % LEVEL:
        way = -1 if mirrored else 1
        return [shift(block, count, way * steps) for steps in range(1, ROUNDS + 1)]
    far = send(block, count, mirrored, (0, 2, 0), (1, 3, 0), (2, 1, 1), (3, 0, 1))
    near = send(block, count, mirrored, (0, 1, 0), (2, 3, 0), (1, 0, 1), (3, 2, 1))
    other = send(far, count, mirrored, (0, 1, 0), (1, 0, 0), (2, 3, 0), (3, 2, 0))
    return [near, far, other]


def distances_of(mirrored):
    count = lax.axis_size("sta")
    if count % LEVEL:
        return list(range(1, ROUNDS + 1))
    role = lax.rem(lax.axis_index("sta"), LEVEL)
    role = LEVEL - 1 - role if mirrored else role
    chosen = []
    for q in range(ROUNDS):
        away = jnp.int32(DISTANCES[LEVEL - 1][q])
        for r in range(LEVEL - 1):
            away = jnp.where(role == r, DISTANCES[r][q], away)
        chosen.append(away)
    return chosen


def spectra(records, counts, gap_mask):
    channels, _, samples = records.shape
    hours = counts.shape[1]
    bins = samples // 2
    count = lax.axis_size("sta")
    table = fourier_matrix(samples)
    first, rest, valid, table = whiten_first(records, counts, gap_mask, table)
    whitened = [first] + [whiten_hour(rest, valid, table, hour) for hour in range(1, hours)]
    partners = [fetch_partners(whitened[hour], count, hour) for hour in range(hours)]
    sums = [None, None]
    for hour in range(hours):
        mirrored = hour % 2
        sums[mirrored] = pair_hour(
            [whitened[hour], *partners[hour]],
            sums[mirrored],
            hours,
            hour + 2 >= hours,
            mirrored == 1,
        )
    (behind, *back), (ahead, *forth) = sums
    from_ahead, from_rear = [], []
    for d in range(1, ROUNDS + 1):
        from_ahead.append(shift(back[d - 1], count, -d))
        from_rear.append(shift(forth[d - 1], count, d))
    stacked = join(behind, ahead, from_ahead, from_rear)
    stacked = stacked.reshape(2 * ROUNDS + 1, channels, channels, 2, bins)
    return jnp.transpose(stacked, (0, 3, 1, 2, 4))


def solution(mesh):
    in_specs = (P(("days", "sta"), None, None), P(("days", "sta"), None), P(("days", "sta"), None))
    out_specs = P(None, None, ("days", "sta"), None, None)
    return jax.shard_map(
        spectra, mesh=mesh, in_specs=in_specs, out_specs=out_specs, check_vma=False
    )
```

```python
import math

import jax
import jax.numpy as jnp
import numpy as np
from jax import lax
from jax.experimental import pallas as pl
from jax.experimental.pallas import tpu as pltpu
from jax.sharding import PartitionSpec as P


ROUNDS = 3
LANES = 128
PITCH = 16
SKEW = 8
MIB = 1 << 20
PAIR_LIMIT = 10 * MIB
PAIR_COST = pl.CostEstimate(flops=3_000_000_000, transcendentals=0, bytes_accessed=12_000_000)
WHITEN_COST = pl.CostEstimate(flops=2_000_000_000, transcendentals=0, bytes_accessed=8_000_000)

epsilon = 1e-06

NT = (((1,), (1,)), ((), ()))


def fourier_matrix(samples):
    freq_bins = samples // 2
    times_axis = np.arange(samples, dtype=np.int32)
    bins_axis = np.arange(freq_bins, dtype=np.int32)
    phase_idx = times_axis[:, None] * bins_axis[None, :] % samples
    step = np.float32(2.0 * math.pi / samples)
    angle = step * phase_idx.astype(np.float32)
    half = np.float32(0.5)
    taper = half - half * np.cos(step * (times_axis.astype(np.float32) + half))
    table_re = taper[:, None] * np.cos(angle)
    table_im = -taper[:, None] * np.sin(angle)
    return jnp.asarray(np.concatenate([table_re.T, table_im.T], axis=0).astype(jnp.bfloat16))


def lane_iota(rows):
    return lax.broadcasted_iota(jnp.int32, (rows, LANES), 1)


def validity_rows(hour, seg_hour, counts_ref, gap_ref):
    stations = gap_ref.shape[0]
    per_tile = LANES // seg_hour
    tile = gap_ref[:, pl.ds(hour // per_tile * LANES, LANES)].astype(jnp.float32)
    turned = pltpu.roll(tile, seg_hour, 1)
    lane = lane_iota(stations)
    low = lane < seg_hour
    doubled = jnp.where(low, tile, turned) if hour % per_tile == 0 else jnp.where(low, turned, tile)
    position = jnp.where(low, lane, lane - seg_hour)
    return [
        jnp.where(
            position[station : station + 1] < counts_ref[station, hour],
            doubled[station : station + 1],
            0.0,
        )
        for station in range(stations)
    ]


def whiten_block(records_ref, valid, table_ref, out_ref):
    channels, seg_hour, samples = records_ref.shape
    bins = samples // 2
    row = lax.broadcasted_iota(jnp.int32, (bins, LANES), 0)
    low_side = lane_iota(bins) < seg_hour
    slot = jnp.logical_and(row == 0, jnp.logical_not(low_side))
    table = table_ref[...]
    per_station = channels // len(valid)
    first_half = lane_iota(1) < seg_hour
    for channel in range(0, channels, 2):
        both = jnp.concatenate([records_ref[channel], records_ref[channel + 1]], axis=0)
        spectrum = lax.dot_general(table, both, NT, preferred_element_type=jnp.float32)
        power = jnp.sum(spectrum * spectrum, axis=0, keepdims=True) * (1.0 / samples)
        pair_valid = jnp.where(
            first_half, valid[channel // per_station], valid[(channel + 1) // per_station]
        )
        scaled = spectrum * (lax.rsqrt(power + epsilon) * pair_valid)
        real, imag = scaled[:bins], scaled[bins:]
        one = jnp.where(low_side, real, pltpu.roll(imag, seg_hour, 1))
        two = jnp.where(low_side, pltpu.roll(real, seg_hour, 1), imag)
        for value, at in ((one, channel), (two, channel + 1)):
            value = jnp.where(slot, valid[at // per_station], value)
            out_ref[at] = value.astype(jnp.bfloat16)


def whiten_first_kernel(counts_hbm, records_hbm, gap_hbm, table_hbm, *refs):
    out_ref, valid_ref, table_ref, counts_ref, records_ref, gap_ref, sems = refs
    seg_hour = records_ref.shape[1]
    hours = valid_ref.shape[0]

    channels = records_ref.shape[0]

    def parts(hour, target, count):
        size = channels // count
        for part in range(count):
            span = pl.ds(part * size, size)
            yield (
                records_hbm.at[span, pl.ds(hour * seg_hour, seg_hour), :],
                target.at[span],
            )

    moves = list(parts(0, records_ref, channels))
    moves += [(counts_hbm, counts_ref), (gap_hbm, gap_ref), (table_hbm, table_ref)]
    copies = [
        pltpu.make_async_copy(source, target, sems.at[i])
        for i, (source, target) in enumerate(moves)
    ]
    for copy in copies:
        copy.start()
    for copy in copies:
        copy.wait()
    valid = [validity_rows(hour, seg_hour, counts_ref, gap_ref) for hour in range(hours)]
    for hour in range(1, hours):
        for station, row in enumerate(valid[hour]):
            valid_ref[hour, station : station + 1, :] = row
    whiten_block(records_ref, valid[0], table_ref, out_ref)


def whiten_first(records, counts, gap_mask, table):
    channels, segments, samples = records.shape
    stations, hours = counts.shape
    seg_hour = segments // hours
    hbm = pl.BlockSpec(memory_space=pltpu.HBM)
    vmem = pl.BlockSpec(memory_space=pltpu.VMEM)
    block = (channels, seg_hour, samples)
    return pl.pallas_call(
        whiten_first_kernel,
        out_shape=[
            jax.ShapeDtypeStruct((channels, samples // 2, LANES), jnp.bfloat16),
            jax.ShapeDtypeStruct((hours, stations, LANES), jnp.float32),
            jax.ShapeDtypeStruct(table.shape, table.dtype),
        ],
        in_specs=[hbm] * 4,
        out_specs=[vmem] * 3,
        scratch_shapes=[
            pltpu.SMEM(counts.shape, counts.dtype),
            pltpu.VMEM(block, records.dtype),
            pltpu.VMEM(gap_mask.shape, gap_mask.dtype),
            pltpu.SemaphoreType.DMA((channels + 3,)),
        ],
        cost_estimate=WHITEN_COST,
        compiler_params=pltpu.CompilerParams(vmem_limit_bytes=4 * MIB),
        name="whiten_first",
    )(
        *(
            pltpu.with_memory_space_constraint(x, pltpu.HBM)
            for x in (counts, records, gap_mask, table)
        )
    )


def whiten_hour_kernel(hour, records_ref, valid_ref, table_ref, out_ref):
    valid = [valid_ref[hour, station : station + 1, :] for station in range(valid_ref.shape[1])]
    seg_hour = out_ref.shape[2] // 2
    whiten_block(records_ref.at[:, pl.ds(hour * seg_hour, seg_hour), :], valid, table_ref, out_ref)


def whiten_hour(records, valid, table, hour):
    channels, _, samples = records.shape
    vmem = pl.BlockSpec(memory_space=pltpu.VMEM)
    return pl.pallas_call(
        lambda *refs: whiten_hour_kernel(hour, *refs),
        out_shape=jax.ShapeDtypeStruct((channels, samples // 2, LANES), jnp.bfloat16),
        in_specs=[vmem] * 3,
        out_specs=vmem,
        cost_estimate=WHITEN_COST,
        compiler_params=pltpu.CompilerParams(vmem_limit_bytes=4 * MIB),
        name="whiten_hour",
    )(records, valid, table)


def pair_hour_kernel(hours, first, last, mirrored, *refs):
    refs = list(refs)
    blocks = [refs.pop(0) for _ in range(ROUNDS + 1)]
    before_ref = None if first else refs.pop(0)
    channels, bins, _ = blocks[0].shape
    half = LANES // 2
    if last:
        kept_ref, *back_refs, wide_ref, acc_ref, back_f32 = refs
    else:
        acc_ref, wide_ref = refs
    pitch = bins + SKEW
    for q, block in enumerate(blocks):
        for channel in range(channels):
            start = (q * channels + channel) * pitch
            wide_ref[start : start + bins, :] = block[channel].astype(jnp.float32)
    for pad in range(PITCH - channels):
        start = (len(blocks) * channels + pad) * pitch
        wide_ref[start : start + bins, :] = jnp.zeros((bins, LANES), jnp.float32)

    def tile_at(q, k):
        return wide_ref[pl.ds(q * channels * pitch + k, PITCH, stride=pitch), :]

    low = lane_iota(PITCH) < half
    zeroth = [tile_at(q, 0) for q in range(len(blocks))]
    valid = [jnp.where(low, pltpu.roll(t, half, 1), t).astype(jnp.bfloat16) for t in zeroth]
    for q, t in enumerate(zeroth):
        wide_ref[pl.ds(q * channels * pitch, PITCH, stride=pitch), :] = jnp.where(low, t, 0.0)
    joint = 0.5 * lax.dot_general(
        valid[0], jnp.concatenate(valid + valid, axis=0), NT, preferred_element_type=jnp.float32
    )
    weight = 1.0 / (hours * jnp.maximum(joint, 1.0))
    weight = jnp.concatenate([weight, weight], axis=0)
    sign = jnp.where(low, 1.0, -1.0)
    low_product = lane_iota(2 * PITCH) < half
    half_bins = bins // 2

    def step(k, carry):
        left, right = [], []
        for part in range(2):
            tiles = [tile_at(q, k + part * half_bins) for q in range(len(blocks))]
            turned = pltpu.roll(tiles[0], half, 1) * sign
            tiles = [t.astype(jnp.bfloat16) for t in tiles]
            left += [tiles[0], turned.astype(jnp.bfloat16)]
            right += tiles
        product = lax.dot_general(
            jnp.concatenate(left, axis=0),
            jnp.concatenate(right, axis=0),
            NT,
            preferred_element_type=jnp.float32,
        )
        product = weight * jnp.where(low_product, product[: 2 * PITCH], product[2 * PITCH :])
        place = pl.ds(pl.multiple_of(k * 2 * PITCH, 2 * PITCH), 2 * PITCH)
        if not first:
            product = product + before_ref[place, :]
        acc_ref[place, :] = product
        return carry

    lax.fori_loop(0, half_bins, step, 0, unroll=half_bins)
    if not last:
        return
    low_half = lane_iota(half) < half
    distances = distances_of(mirrored)

    def finish(a, carry):
        both = jnp.concatenate(
            [
                acc_ref[pl.ds(part * PITCH + a, half_bins, stride=2 * PITCH), :]
                for part in range(2)
            ],
            axis=0,
        )
        by_bin = both.T
        upper, lower = by_bin[:half], by_bin[half:]
        real = jnp.where(low_half, upper, pltpu.roll(lower, half, 1))
        imag = jnp.where(low_half, pltpu.roll(upper, half, 1), lower)
        for part, value in enumerate((real, imag)):
            for q in range(len(blocks)):
                rows = value[q * PITCH : q * PITCH + channels]
                place = pl.ds(a * 2 * channels + part, channels, stride=2)
                if q:
                    kept_ref[distances[q - 1], place, :] = rows
                    back_f32[q - 1, pl.ds(2 * a + part, channels, stride=2 * channels), :] = (
                        -rows if part else rows
                    )
                else:
                    kept_ref[0, place, :] = rows
        return carry

    lax.fori_loop(0, channels, finish, 0, unroll=12)
    for q in range(ROUNDS):
        for d in range(ROUNDS):

            @pl.when(distances[q] == d + 1)
            def _():
                back_refs[d][...] = back_f32[q].astype(jnp.bfloat16)


def pair_hour(blocks, before, hours, last, mirrored):
    channels, bins, lanes = blocks[0].shape
    first = before is None
    acc = (bins // 2 * 2 * PITCH, lanes)
    rows = 2 * channels * channels
    wide = pltpu.VMEM(
        ((len(blocks) * channels + PITCH - channels) * (bins + SKEW), lanes), jnp.float32
    )
    vmem = pl.BlockSpec(memory_space=pltpu.VMEM)
    args, specs = [], []
    args += blocks
    specs += [vmem] * len(blocks)
    if not first:
        args.append(before)
        specs.append(vmem)
    if last:
        out_shape = [
            jax.ShapeDtypeStruct((ROUNDS + 1, rows, lanes), jnp.float32),
            *[jax.ShapeDtypeStruct((rows, lanes), jnp.bfloat16)] * ROUNDS,
        ]
        out_specs = [vmem] * (ROUNDS + 1)
        scratch = [
            wide,
            pltpu.VMEM(acc, jnp.float32),
            pltpu.VMEM((ROUNDS, rows, lanes), jnp.float32),
        ]
    else:
        out_shape = jax.ShapeDtypeStruct(acc, jnp.float32)
        out_specs = vmem
        scratch = [wide]
    return pl.pallas_call(
        lambda *refs: pair_hour_kernel(hours, first, last, mirrored, *refs),
        out_shape=out_shape,
        in_specs=specs,
        out_specs=out_specs,
        scratch_shapes=scratch,
        cost_estimate=PAIR_COST,
        compiler_params=pltpu.CompilerParams(vmem_limit_bytes=PAIR_LIMIT),
        name="pair_hour_last" if last else "pair_hour",
    )(*args)


def put(out_ref, slot, value):
    out_ref[slot] = value.reshape(out_ref.shape[1], 2, LANES).astype(jnp.bfloat16)


def join_below_kernel(behind_ref, ahead_ref, *refs):
    from_rear, out_ref = refs[:ROUNDS], refs[-1]
    put(out_ref, ROUNDS, behind_ref[0] + ahead_ref[0])
    for d in range(1, ROUNDS + 1):
        put(out_ref, ROUNDS - d, behind_ref[d] + from_rear[d - 1][...].astype(jnp.float32))


def join_above_kernel(ahead_ref, *refs):
    from_ahead, out_ref = refs[:ROUNDS], refs[-1]
    for d in range(1, ROUNDS + 1):
        put(out_ref, d - 1, ahead_ref[d] + from_ahead[d - 1][...].astype(jnp.float32))


def join(behind, ahead, from_ahead, from_rear):
    _, rows, lanes = behind.shape
    vmem = pl.BlockSpec(memory_space=pltpu.VMEM)
    out = jax.ShapeDtypeStruct((2 * ROUNDS + 1, rows // 2, 2, lanes), jnp.bfloat16)
    half = (ROUNDS + 1, rows // 2, 2, lanes)
    params = pltpu.CompilerParams(vmem_limit_bytes=4 * MIB)
    below = pl.pallas_call(
        join_below_kernel,
        grid=(1,),
        out_shape=out,
        in_specs=[vmem] * (ROUNDS + 2),
        out_specs=pl.BlockSpec(half, lambda i: (0, 0, 0, 0)),
        compiler_params=params,
        name="join_below",
    )(behind, ahead, *from_rear)
    return pl.pallas_call(
        join_above_kernel,
        grid=(1,),
        out_shape=out,
        in_specs=[vmem] * (ROUNDS + 1) + [pl.BlockSpec(memory_space=pl.ANY)],
        out_specs=pl.BlockSpec(half, lambda i: (1, 0, 0, 0)),
        input_output_aliases={ROUNDS + 1: 0},
        compiler_params=params,
        name="join_above",
    )(ahead, *from_ahead, below)


LEVEL = 4
DISTANCES = ((3, 1, 2), (1, 3, 2), (3, 2, 1), (1, 2, 3))


def send(value, count, mirrored, *hops):
    levels = count // LEVEL
    pairs = [
        (LEVEL * level + source, LEVEL * ((level + up) % levels) + target)
        for source, target, up in hops
        for level in range(levels)
    ]
    if mirrored:
        pairs = [(count - 1 - source, count - 1 - target) for source, target in pairs]
    return lax.ppermute(value, "sta", pairs)


def shift(value, count, steps):
    pairs = [(source, (source + steps) % count) for source in range(count)]
    return lax.ppermute(value, "sta", pairs)


def fetch_partners(block, count, hour):
    mirrored = hour % 2 == 1
    if count % LEVEL:
        way = -1 if mirrored else 1
        return [shift(block, count, way * steps) for steps in range(1, ROUNDS + 1)]
    far = send(block, count, mirrored, (0, 2, 0), (1, 3, 0), (2, 1, 1), (3, 0, 1))
    near = send(block, count, mirrored, (0, 1, 0), (2, 3, 0), (1, 0, 1), (3, 2, 1))
    other = send(far, count, mirrored, (0, 1, 0), (1, 0, 0), (2, 3, 0), (3, 2, 0))
    return [near, far, other]


def distances_of(mirrored):
    count = lax.axis_size("sta")
    if count % LEVEL:
        return list(range(1, ROUNDS + 1))
    role = lax.rem(lax.axis_index("sta"), LEVEL)
    role = LEVEL - 1 - role if mirrored else role
    chosen = []
    for q in range(ROUNDS):
        away = jnp.int32(DISTANCES[LEVEL - 1][q])
        for r in range(LEVEL - 1):
            away = jnp.where(role == r, DISTANCES[r][q], away)
        chosen.append(away)
    return chosen


def spectra(records, counts, gap_mask):
    channels, _, samples = records.shape
    hours = counts.shape[1]
    bins = samples // 2
    count = lax.axis_size("sta")
    table = fourier_matrix(samples)
    first, valid, table = whiten_first(records, counts, gap_mask, table)
    whitened = [first] + [whiten_hour(records, valid, table, hour) for hour in range(1, hours)]
    partners = [fetch_partners(whitened[hour], count, hour) for hour in range(hours)]
    sums = [None, None]
    for hour in range(hours):
        mirrored = hour % 2
        sums[mirrored] = pair_hour(
            [whitened[hour], *partners[hour]],
            sums[mirrored],
            hours,
            hour + 2 >= hours,
            mirrored == 1,
        )
    (behind, *back), (ahead, *forth) = sums
    from_ahead, from_rear = [], []
    for d in range(1, ROUNDS + 1):
        from_ahead.append(shift(back[d - 1], count, -d))
        from_rear.append(shift(forth[d - 1], count, d))
    stacked = join(behind, ahead, from_ahead, from_rear)
    stacked = stacked.reshape(2 * ROUNDS + 1, channels, channels, 2, bins)
    return jnp.transpose(stacked, (0, 3, 1, 2, 4))


def solution(mesh):
    in_specs = (P(("days", "sta"), None, None), P(("days", "sta"), None), P(("days", "sta"), None))
    out_specs = P(None, None, ("days", "sta"), None, None)
    return jax.shard_map(
        spectra, mesh=mesh, in_specs=in_specs, out_specs=out_specs, check_vma=False
    )
```
